128 devices in a mesh: seq: 16 (over z, y_lo, core), tensor: 8 (over y_hi, x).
Axes of the slice: x: 4, y: 4 (y_hi: 2, y_lo: 2; y = y_hi * 2 + y_lo), z: 4, core: 2. Of those that a mesh axis runs over, the one named last changes fastest.
Arguments:
- queries: bfloat16 [12288, 4096], P('seq', 'tensor'), may hold values from -12 to 12
- keys: bfloat16 [12288, 1024], P('seq', 'tensor'), may hold values from -12 to 12
- values: bfloat16 [12288, 1024], P('seq', 'tensor'), may hold values from -6 to 6
- out_weight: bfloat16 [4096, 4096], P('tensor'), may hold values from -0.09375 to 0.09375
- out_grad: bfloat16 [12288, 4096], P('seq', 'tensor'), may hold values from -6 to 6
- doc_ids: int32 [12288], P('seq'), may hold values from 0 to 7, never falling along the last dimension, each value on 1 to 3072 neighbouring positions
Outputs:
- grad_queries: bfloat16 [12288, 4096], P('seq', 'tensor')
- grad_keys: bfloat16 [12288, 1024], P('seq', 'tensor')
- grad_values: bfloat16 [12288, 1024], P('seq', 'tensor')
- grad_out_weight: bfloat16 [4096, 4096], P('tensor', 'seq')
The draws below stay inside these ranges and needn't reach their ends.
Inputs may be any that keep to these rules, and one draw needn't show every extreme that they name: `doc_ids`: document numbers never fall along the sequence; a document holds 1 to 3072 tokens and one holds exactly that many.
All inputs are finite; a program needn't handle non-finite values.
Results may differ from the reference program's by a relative error of at most 0.015.
Values may be sent and summed in bfloat16 or wider, within the bound.
No kernel may reach another device: no remote copies, remote signals or barrier semaphores. Data moves between devices by JAX's collectives and lax.ppermute only.
A program may use at most 128 MiB of HBM per device.

```python
import math
import jax
import jax.numpy as jnp
import numpy as np
from jax import lax

D = 4096
QUERY_HEADS = 32
KEY_VALUE_HEADS = 8
HEAD_SIZE = 128
TOKENS_PER_SHARD = 768
SEQUENCE_TOKENS = 12288
WINDOW = 1536
DOCS = 8
N_SEQ = 16


def draw_queries(key, part):
    newest_part = jax.random.fold_in(key, 13)
    return jnp.clip(jax.random.normal(newest_part, (SEQUENCE_TOKENS, QUERY_HEADS * HEAD_SIZE), jnp.float32), -6.0, 6.0).astype(jnp.bfloat16)


def draw_keys(key, part):
    newest_part = jax.random.fold_in(key, 12)
    return jnp.clip(2.0 * jax.random.normal(newest_part, (SEQUENCE_TOKENS, KEY_VALUE_HEADS * HEAD_SIZE), jnp.float32), -12.0, 12.0).astype(jnp.bfloat16)


def raised(result, stream_key, source, target, blocks, factor):
    owner, partner = [(jnp.arange(result.shape[dim]) // (result.shape[dim] // blocks)).reshape([-1 if axis == dim else 1 for axis in range(result.ndim)]) for dim in (source, target)]
    chosen = jax.random.permutation(stream_key, blocks)[partner]
    strong = (owner == chosen) | (owner == (partner + blocks // 2) % blocks)
    return jnp.where(strong, factor * result, result)


def shard_levels(own_key, shape, split, smallest, high):
    loudness = 1.0
    for axis_at, blocks in split:
        heights = jax.random.uniform(jax.random.fold_in(jax.random.fold_in(own_key, 6), axis_at), (blocks,), jnp.float32, smallest / len(split), high / len(split))
        loudness = loudness * jnp.repeat(jnp.exp(heights), shape[axis_at] // blocks).reshape((-1,) + (1,) * (len(shape) - 1 - axis_at))
    return loudness


def split_up(number_of, total, limit, slope):
    weights = [(1 << 20) // math.isqrt(standing ** slope) + 1 for standing in range(2, number_of + 1)]
    surplus, given = total - limit - (number_of - 1), [1] * (number_of - 1)
    while surplus > 0:
        candidates = [i for i in range(number_of - 1) if given[i] < limit]
        mass, budget = sum([weights[i] for i in candidates]), surplus
        for i in candidates:
            addition = min(limit - given[i], max(1, budget * weights[i] // mass), surplus)
            given[i] = given[i] + addition
            surplus = surplus - addition
    return np.array([limit] + given)


def ragged_sizes(own_key, amount, total, reach, skew):
    if amount == 2:
        one = jax.random.randint(own_key, (), max(1, total - reach), min(reach, total - 1) + 1)
        return jnp.stack([one, total - one])
    lengths = jnp.asarray(split_up(amount, total, reach, skew), jnp.int32)
    pairs = (amount - 1) // 2
    source_of, taker = lengths[1:1 + 2 * pairs:2], lengths[2:2 + 2 * pairs:2]
    margin = jnp.minimum(source_of - 1, reach - taker)
    passed = jax.random.randint(jax.random.fold_in(own_key, 1), (pairs,), 0, 1 << 20) % (margin + 1)
    lengths = lengths.at[1:1 + 2 * pairs:2].set(source_of - passed).at[2:2 + 2 * pairs:2].set(taker + passed)
    return lengths[jax.random.permutation(jax.random.fold_in(own_key, 2), amount)]


def bell_draw(own_key, shape, deviation, bound, split=(), kind=jnp.bfloat16):
    array = jax.random.normal(own_key, shape, jnp.float32) * deviation
    if len(split) > 0:
        array = shard_levels(own_key, shape, split, -0.22, 0.18) * array
    return jnp.clip(array, min=-bound, max=bound).astype(kind)


def bell_draw_with(key, dims, scale, bound, pieces, heavy, held_as=jnp.bfloat16):
    array = scale * jax.random.normal(key, dims, jnp.float32)
    if pieces:
        array = array * shard_levels(key, dims, pieces, -0.22, 0.18)
    return jnp.clip(raised(array, jax.random.fold_in(key, 3), *heavy), -bound, bound).astype(held_as)


def setup_inputs(seed: int = 0) -> dict:
    streams_of = jax.random.split(jax.random.key(seed), 7)
    return {
        "queries": draw_queries(jax.random.fold_in(streams_of[6], 71), 0),
        "keys": draw_keys(jax.random.fold_in(streams_of[6], 71), 0),
        "values": bell_draw(streams_of[2], (SEQUENCE_TOKENS, KEY_VALUE_HEADS * HEAD_SIZE), 1.0, 6.0, ((0, 16), (1, 8))),
        "out_weight": bell_draw(streams_of[3], (QUERY_HEADS * HEAD_SIZE, D), (QUERY_HEADS * HEAD_SIZE) ** -0.5, 0.09375, ((0, 8),)),
        "out_grad": bell_draw_with(streams_of[4], (SEQUENCE_TOKENS, D), 1.0, 6.0, ((0, 16), (1, 8)), (0, 1, 16, 2.0)),
        "doc_ids": jnp.searchsorted(jnp.cumsum(ragged_sizes(streams_of[5], DOCS, SEQUENCE_TOKENS, 4 * TOKENS_PER_SHARD, 1)), jnp.arange(SEQUENCE_TOKENS), side="right").astype(jnp.int32),
    }


NEG_BIG = -1e+30

def reference(queries, keys, values, out_weight, out_grad, doc_ids):
    group_factor = QUERY_HEADS // KEY_VALUE_HEADS
    scale = 1.0 / math.sqrt(HEAD_SIZE)
    attention_gradient = jnp.dot(out_grad, out_weight.T, preferred_element_type=jnp.float32).astype(jnp.bfloat16)
    padded_keys = jnp.concatenate([jnp.zeros((2 * TOKENS_PER_SHARD, KEY_VALUE_HEADS * HEAD_SIZE), keys.dtype), keys], axis=0)
    padded_values = jnp.concatenate([jnp.zeros((2 * TOKENS_PER_SHARD, KEY_VALUE_HEADS * HEAD_SIZE), values.dtype), values], axis=0)
    pad_docs = jnp.concatenate([jnp.zeros((2 * TOKENS_PER_SHARD,), jnp.int32), doc_ids.astype(jnp.int32)])

    def block(index):
        start_index = (index * TOKENS_PER_SHARD).astype(jnp.int32)
        query_block = lax.dynamic_slice_in_dim(queries, start_index, TOKENS_PER_SHARD, 0).astype(jnp.float32).reshape(TOKENS_PER_SHARD, KEY_VALUE_HEADS, group_factor, HEAD_SIZE)
        key_block = lax.dynamic_slice_in_dim(padded_keys, start_index, 3 * TOKENS_PER_SHARD, 0).astype(jnp.float32).reshape(3 * TOKENS_PER_SHARD, KEY_VALUE_HEADS, HEAD_SIZE)
        value_block = lax.dynamic_slice_in_dim(padded_values, start_index, 3 * TOKENS_PER_SHARD, 0).astype(jnp.float32).reshape(3 * TOKENS_PER_SHARD, KEY_VALUE_HEADS, HEAD_SIZE)
        doc_q = lax.dynamic_slice_in_dim(doc_ids.astype(jnp.int32), start_index, TOKENS_PER_SHARD, 0)
        doc_k = lax.dynamic_slice_in_dim(pad_docs, start_index, 3 * TOKENS_PER_SHARD, 0)
        block_gradient = lax.dynamic_slice_in_dim(attention_gradient, start_index, TOKENS_PER_SHARD, 0).astype(jnp.float32).reshape(TOKENS_PER_SHARD, KEY_VALUE_HEADS, group_factor, HEAD_SIZE)
        q_pos = start_index + jnp.arange(TOKENS_PER_SHARD, dtype=jnp.int32)
        k_pos = start_index - 2 * TOKENS_PER_SHARD + jnp.arange(3 * TOKENS_PER_SHARD, dtype=jnp.int32)
        gap = q_pos[:, None] - k_pos[None, :]
        visible = (gap >= 0) & (gap < WINDOW) & (k_pos[None, :] >= 0) & (doc_q[:, None] == doc_k[None, :])
        raw = jnp.einsum('qgeh,kgh->geqk', query_block, key_block) * scale
        masked = jnp.where(visible, raw, NEG_BIG)
        top = lax.optimization_barrier(jnp.max(masked, axis=-1, keepdims=True))
        expo = jnp.where(visible, jnp.exp(masked - top), 0.0)
        probs = expo / lax.optimization_barrier(jnp.sum(expo, axis=-1, keepdims=True))
        probs_low = lax.optimization_barrier(probs.astype(jnp.bfloat16)).astype(jnp.float32)
        attention_output = jnp.einsum('geqk,kgh->qgeh', probs_low, value_block).astype(jnp.bfloat16)
        attn_wide = lax.optimization_barrier(attention_output).astype(jnp.float32)
        delta = jnp.transpose(lax.optimization_barrier(jnp.sum(block_gradient * attn_wide, axis=-1)), (1, 2, 0))[..., None]
        d_prob = jnp.einsum('qgeh,kgh->geqk', block_gradient, value_block)
        d_score = lax.optimization_barrier((probs * (d_prob - delta)).astype(jnp.bfloat16)).astype(jnp.float32)
        query_gradient = (jnp.einsum('geqk,kgh->qgeh', d_score, key_block) * scale).astype(jnp.bfloat16)
        key_gradient = jnp.einsum('geqk,qgeh->kgh', d_score, query_block) * scale
        value_gradient = jnp.einsum('geqk,qgeh->kgh', probs_low, block_gradient)
        return (attention_output.reshape(TOKENS_PER_SHARD, QUERY_HEADS * HEAD_SIZE), query_gradient.reshape(TOKENS_PER_SHARD, QUERY_HEADS * HEAD_SIZE), key_gradient.reshape(3, TOKENS_PER_SHARD, KEY_VALUE_HEADS * HEAD_SIZE), value_gradient.reshape(3, TOKENS_PER_SHARD, KEY_VALUE_HEADS * HEAD_SIZE))
    attention_output, query_gradient, k_parts, v_parts = lax.map(block, jnp.arange(N_SEQ, dtype=jnp.int32))

    def combine(part_count):
        first_zeros = jnp.zeros((1, TOKENS_PER_SHARD, KEY_VALUE_HEADS * HEAD_SIZE), jnp.float32)
        second_zeros = jnp.zeros((2, TOKENS_PER_SHARD, KEY_VALUE_HEADS * HEAD_SIZE), jnp.float32)
        nearby_part = jnp.concatenate([part_count[1:, 1], first_zeros], axis=0)
        distant_part = jnp.concatenate([part_count[2:, 0], second_zeros], axis=0)
        return (part_count[:, 2] + nearby_part + distant_part).reshape(SEQUENCE_TOKENS, KEY_VALUE_HEADS * HEAD_SIZE).astype(jnp.bfloat16)
    attention_output = attention_output.reshape(SEQUENCE_TOKENS, QUERY_HEADS * HEAD_SIZE)
    grad_w = lax.dot_general(attention_output, out_grad, (((0,), (0,)), ((), ())), preferred_element_type=jnp.float32)
    return (query_gradient.reshape(SEQUENCE_TOKENS, QUERY_HEADS * HEAD_SIZE), combine(k_parts), combine(v_parts), grad_w.astype(jnp.bfloat16))
```

```python
import math

import jax
import jax.numpy as jnp
from jax import lax
from jax.experimental import pallas as pl
from jax.experimental.pallas import tpu as pltpu
from jax.sharding import PartitionSpec as P

HEAD_SIZE = 128
NEG_BIG = -1e30
ROWS = 256


def shifted(value, axis, steps):
    count = lax.axis_size(axis)
    initial, last = (max(0, -steps), min(count, count - steps))
    return lax.ppermute(value, axis, [(source, source + steps) for source in range(initial, last)])


def contract_rows(left, right):
    return lax.dot_general(
        left, right, (((0,), (0,)), ((), ())), preferred_element_type=jnp.float32
    )


def contract_last(left, right):
    return lax.dot_general(
        left, right, (((1,), (1,)), ((), ())), preferred_element_type=jnp.float32
    )


def gather_keys(parts, key_all, value_all, tok):
    for index, part in enumerate(parts):
        rows = pl.ds(index * tok, tok)
        key_all[rows, :] = part[pl.ds(0, tok), :]
        value_all[rows, :] = part[pl.ds(tok, tok), :]


def first_step():
    return (pl.program_id(0) == 0) & (pl.program_id(1) == 0)


def forward_kernel(tok, span, low_ref, q_ref, far_ref, near_ref, own_ref, probs_ref, attn_ref, key_all, value_all):
    @pl.when(first_step())
    def _():
        gather_keys((far_ref, near_ref, own_ref), key_all, value_all, tok)

    block = pl.program_id(0)
    begin = pl.multiple_of(block * ROWS, ROWS)
    keys = key_all[pl.ds(begin, span), :]
    values = value_all[pl.ds(begin, span), :]
    raw = contract_last(q_ref[...], keys)
    key_at = lax.broadcasted_iota(jnp.int32, (ROWS, span), 1)
    row_at = lax.broadcasted_iota(jnp.int32, (ROWS, 1), 0)
    visible = (key_at >= low_ref[...] - begin) & (key_at <= row_at + 2 * tok)
    masked = jnp.where(visible, raw, NEG_BIG)
    top = jnp.max(masked, axis=1, keepdims=True)
    expo = jnp.exp2((masked - top) * (math.log2(math.e) / math.sqrt(HEAD_SIZE)))
    total = jnp.sum(expo, axis=1, keepdims=True)
    probs_low = (expo * (1.0 / total)).astype(jnp.bfloat16)
    probs_ref[0] = probs_low
    attn_ref[...] = jnp.dot(probs_low, values, preferred_element_type=jnp.float32).astype(jnp.bfloat16)


def backward_kernel(
    tok, span, q_ref, grad_ref, attn_ref, probs_ref, far_ref, near_ref, own_ref,
    gq_ref, far_out, near_out, own_out, key_all, value_all, key_sum, value_sum,
):
    scale = 1.0 / math.sqrt(HEAD_SIZE)

    @pl.when(first_step())
    def _():
        gather_keys((far_ref, near_ref, own_ref), key_all, value_all, tok)
        key_sum[...] = jnp.zeros_like(key_sum)
        value_sum[...] = jnp.zeros_like(value_sum)

    begin = pl.multiple_of(pl.program_id(0) * ROWS, ROWS)
    window = pl.ds(begin, span)
    grad = grad_ref[...]
    delta = jnp.sum(grad.astype(jnp.float32) * attn_ref[...].astype(jnp.float32), axis=1, keepdims=True)
    d_prob = contract_last(grad, value_all[window, :])
    probs = probs_ref[0]
    d_score = (probs.astype(jnp.float32) * (d_prob - delta)).astype(jnp.bfloat16)
    gq = jnp.dot(d_score, key_all[window, :], preferred_element_type=jnp.float32)
    gq_ref[...] = (gq * scale).astype(jnp.bfloat16)
    key_sum[window, :] += contract_rows(d_score, q_ref[...])
    value_sum[window, :] += contract_rows(probs, grad)

    @pl.when((pl.program_id(0) == pl.num_programs(0) - 1) & (pl.program_id(1) == pl.num_programs(1) - 1))
    def _():
        for index, out in enumerate((far_out, near_out, own_out)):
            rows = pl.ds(index * tok, tok)
            out[pl.ds(0, tok), :] = (key_sum[rows, :] * scale).astype(out.dtype)
            out[pl.ds(tok, tok), :] = value_sum[rows, :].astype(out.dtype)


def whole():
    return pl.BlockSpec(memory_space=pltpu.VMEM)


def local(queries, keys, values, out_weight, out_grad, doc_ids):
    tok = queries.shape[0]
    heads = queries.shape[1] // HEAD_SIZE
    blocks = tok // ROWS
    span = 2 * tok + ROWS
    shard = lax.axis_index("seq")
    docs = jnp.pad(doc_ids.astype(jnp.bfloat16).reshape(tok // HEAD_SIZE, HEAD_SIZE), ((0, 16 - tok // HEAD_SIZE), (0, 0)))
    own = jnp.concatenate([keys, values, docs], axis=0)
    far, near = shifted(own, "seq", 2), shifted(own, "seq", 1)
    doc_of = lambda part: part[2 * tok : 2 * tok + tok // HEAD_SIZE].reshape(tok).astype(jnp.int32)
    doc_keys = jnp.concatenate([
        jnp.where(shard >= 2, doc_of(far), -1), jnp.where(shard >= 1, doc_of(near), -1), doc_ids
    ])
    earlier = jnp.sum((doc_keys[None, :] < doc_ids[:, None]).astype(jnp.int32), axis=1)
    low = jnp.maximum(earlier, jnp.arange(tok, dtype=jnp.int32) + 1)[:, None]

    head_block = pl.BlockSpec((ROWS, HEAD_SIZE), lambda b, h: (b, h))
    probs_block = pl.BlockSpec((1, ROWS, span), lambda b, h: (h, b, 0))
    held = [pltpu.VMEM((3 * tok, HEAD_SIZE), jnp.bfloat16)] * 2
    work = heads * tok * span * HEAD_SIZE * 2
    probs, attn = pl.pallas_call(
        lambda *refs: forward_kernel(tok, span, *refs),
        grid=(blocks, heads),
        in_specs=[pl.BlockSpec((ROWS, 1), lambda b, h: (b, 0)), head_block, whole(), whole(), whole()],
        out_specs=[probs_block, head_block],
        out_shape=[
            jax.ShapeDtypeStruct((heads, tok, span), jnp.bfloat16),
            jax.ShapeDtypeStruct((tok, heads * HEAD_SIZE), jnp.bfloat16),
        ],
        scratch_shapes=held,
        compiler_params=pltpu.CompilerParams(vmem_limit_bytes=40 << 20),
        cost_estimate=pl.CostEstimate(flops=2 * work, bytes_accessed=14 << 20, transcendentals=heads * tok * span),
        name="forward",
    )(low, queries, far, near, own)

    grad_full = lax.all_gather(out_grad, "tensor", axis=1, tiled=True)
    weight_part = contract_rows(grad_full, attn)
    summed = lax.psum_scatter(weight_part.astype(jnp.bfloat16), "seq", scatter_dimension=0, tiled=True)
    weight_grad = summed.T
    attention_gradient = contract_last(grad_full, out_weight).astype(jnp.bfloat16)

    pair = lambda dtype: jax.ShapeDtypeStruct((2 * tok, HEAD_SIZE), dtype)
    grad_queries, far_sum, near_sum, own_sum = pl.pallas_call(
        lambda *refs: backward_kernel(tok, span, *refs),
        grid=(blocks, heads),
        in_specs=[head_block, head_block, head_block, probs_block, whole(), whole(), whole()],
        out_specs=[head_block, whole(), whole(), whole()],
        out_shape=[
            jax.ShapeDtypeStruct((tok, heads * HEAD_SIZE), jnp.bfloat16),
            pair(jnp.bfloat16), pair(jnp.bfloat16), pair(jnp.float32),
        ],
        scratch_shapes=held + [pltpu.VMEM((3 * tok, HEAD_SIZE), jnp.float32)] * 2,
        compiler_params=pltpu.CompilerParams(vmem_limit_bytes=40 << 20),
        cost_estimate=pl.CostEstimate(flops=4 * work, bytes_accessed=14 << 20, transcendentals=0),
        name="backward",
    )(queries, attention_gradient, attn, probs, far, near, own)
    total = own_sum + shifted(far_sum, "seq", -2).astype(jnp.float32) + shifted(near_sum, "seq", -1).astype(jnp.float32)
    total = total.astype(jnp.bfloat16)
    return (grad_queries, total[:tok], total[tok:], weight_grad)


def solution(mesh):
    placed = (
        P("seq", "tensor"),
        P("seq", "tensor"),
        P("seq", "tensor"),
        P("tensor", None),
        P("seq", "tensor"),
        P("seq"),
    )
    return jax.shard_map(
        local,
        mesh=mesh,
        in_specs=placed,
        out_specs=(P("seq", "tensor"), P("seq", "tensor"), P("seq", "tensor"), P("tensor", "seq")),
        check_vma=False,
    )
```

```python
import math

import jax
import jax.numpy as jnp
from jax import lax
from jax.experimental import pallas as pl
from jax.experimental.pallas import tpu as pltpu
from jax.sharding import PartitionSpec as P

HEAD_SIZE = 128
NEG_BIG = -1e30
ROWS = 256
VMEM_BYTES = 24 << 20


def shifted(value, axis, steps):
    count = lax.axis_size(axis)
    initial, last = (max(0, -steps), min(count, count - steps))
    return lax.ppermute(value, axis, [(source, source + steps) for source in range(initial, last)])


def step_x(value, step):
    pairs = [(t, t // 4 * 4 + (t + step) % 4) for t in range(8)]
    return lax.ppermute(value, "tensor", pairs)


def step_y(value):
    return lax.ppermute(value, "tensor", [(t, t ^ 4) for t in range(8)])


def step_core(value):
    return lax.ppermute(value, "seq", [(s, s ^ 1) for s in range(16)])


def contract_rows(left, right):
    return lax.dot_general(
        left, right, (((0,), (0,)), ((), ())), preferred_element_type=jnp.float32
    )


def contract_last(left, right):
    return lax.dot_general(
        left, right, (((1,), (1,)), ((), ())), preferred_element_type=jnp.float32
    )


def gather_keys(parts, key_all, value_all, tok):
    for index, part in enumerate(parts):
        rows = pl.ds(index * tok, tok)
        key_all[rows, :] = part[pl.ds(0, tok), :]
        value_all[rows, :] = part[pl.ds(tok, tok), :]


def forward_kernel(
    tok, span, heads, low_ref, q_ref, far_ref, near_ref, own_ref,
    expo_ref, attn_ref, turned_ref, inverse_ref, key_all, value_all, bias,
):
    @pl.when(pl.program_id(0) == 0)
    def _():
        gather_keys((far_ref, near_ref, own_ref), key_all, value_all, tok)

    begin = pl.multiple_of(pl.program_id(0) * ROWS, ROWS)
    window = pl.ds(begin, span)
    key_at = lax.broadcasted_iota(jnp.int32, (ROWS, span), 1)
    row_at = lax.broadcasted_iota(jnp.int32, (ROWS, 1), 0)
    visible = (key_at >= low_ref[...] - begin) & (key_at <= row_at + 2 * tok)
    bias[...] = jnp.where(visible, 0.0, NEG_BIG)
    for head in range(heads):
        columns = slice(head * HEAD_SIZE, (head + 1) * HEAD_SIZE)
        raw = contract_last(q_ref[:, columns], key_all[window, :]) + bias[...]
        top = jnp.max(raw, axis=1, keepdims=True)
        expo = jnp.exp2((raw - top) * (math.log2(math.e) / math.sqrt(HEAD_SIZE)))
        inverse = 1.0 / jnp.sum(expo, axis=1, keepdims=True)
        expo_low = expo.astype(jnp.bfloat16)
        expo_ref[head] = expo_low
        inverse_ref[:, columns] = jnp.broadcast_to(inverse, (ROWS, HEAD_SIZE))
        attn = jnp.dot(expo_low, value_all[window, :], preferred_element_type=jnp.float32) * inverse
        attn = attn.astype(jnp.bfloat16)
        attn_ref[:, columns] = attn
        turned_ref[columns, :] = attn.T


def backward_rows(heads, width, first, q_ref, grad_ref, attn_ref, inverse_ref, probs_of, keys, values, gq_of, key_sum, value_sum):
    at = slice(first, first + width)
    for head in range(heads):
        columns = slice(head * HEAD_SIZE, (head + 1) * HEAD_SIZE)
        grad = (grad_ref[:, columns].astype(jnp.float32) * inverse_ref[:, columns]).astype(jnp.bfloat16)
        delta = jnp.sum(grad.astype(jnp.float32) * attn_ref[:, columns].astype(jnp.float32), axis=1, keepdims=True)
        d_prob = contract_last(grad, values[at, :])
        probs = probs_of(head)
        d_score = (probs.astype(jnp.float32) * (d_prob - delta)).astype(jnp.bfloat16)
        gq_of(columns, jnp.dot(d_score, keys[at, :], preferred_element_type=jnp.float32))
        key_sum[:, at] += jnp.dot(q_ref[:, columns].T, d_score, preferred_element_type=jnp.float32)
        value_sum[:, at] += jnp.dot(grad.T, probs, preferred_element_type=jnp.float32)


def backward_past_kernel(
    tok, heads, q_ref, grad_ref, attn_ref, inverse_ref, expo_ref, far_ref, near_ref,
    gq_ref, far_out, near_out, key_all, value_all, key_sum, value_sum,
):
    scale = 1.0 / math.sqrt(HEAD_SIZE)

    @pl.when(pl.program_id(0) == 0)
    def _():
        gather_keys((far_ref, near_ref), key_all, value_all, tok)
        key_sum[...] = jnp.zeros_like(key_sum)
        value_sum[...] = jnp.zeros_like(value_sum)

    def put(columns, value):
        gq_ref[:, columns] = value

    for block in range(tok // ROWS):
        @pl.when(pl.program_id(0) == block)
        def _(block=block):
            first = block * ROWS
            width = 2 * tok - first
            backward_rows(
                heads, width, first, q_ref, grad_ref, attn_ref, inverse_ref,
                lambda head: expo_ref[head, :, :width], key_all, value_all, put, key_sum, value_sum,
            )

    @pl.when(pl.program_id(0) == pl.num_programs(0) - 1)
    def _():
        for index, out in enumerate((far_out, near_out)):
            rows = pl.ds(index * tok, tok)
            out[pl.ds(0, tok), :] = (key_sum[:, rows].T * scale).astype(out.dtype)
            out[pl.ds(tok, tok), :] = value_sum[:, rows].T.astype(out.dtype)


def backward_own_kernel(
    tok, heads, q_ref, grad_ref, attn_ref, inverse_ref, expo_a, expo_b, expo_c, own_ref, past_ref,
    gq_ref, own_out, key_all, value_all, key_sum, value_sum,
):
    scale = 1.0 / math.sqrt(HEAD_SIZE)
    blocks = tok // ROWS
    expos = (expo_a, expo_b, expo_c)

    @pl.when(pl.program_id(0) == 0)
    def _():
        gather_keys((own_ref,), key_all, value_all, tok)
        key_sum[...] = jnp.zeros_like(key_sum)
        value_sum[...] = jnp.zeros_like(value_sum)

    def put(columns, value):
        gq_ref[:, columns] = ((past_ref[:, columns] + value) * scale).astype(gq_ref.dtype)

    for block in range(blocks):
        @pl.when(pl.program_id(0) == block)
        def _(block=block):
            width = (block + 1) * ROWS
            probs_of = lambda head: jnp.concatenate([expo[head] for expo in expos[blocks - 1 - block :]], axis=1)
            backward_rows(
                heads, width, 0, q_ref, grad_ref, attn_ref, inverse_ref,
                probs_of, key_all, value_all, put, key_sum, value_sum,
            )

    @pl.when(pl.program_id(0) == pl.num_programs(0) - 1)
    def _():
        own_out[pl.ds(0, tok), :] = key_sum[...].T * scale
        own_out[pl.ds(tok, tok), :] = value_sum[...].T


def project_kernel(sources, shapes, where_ref, weight_ref, turned_ref, *refs):
    count = len(shapes)
    pieces, refs = refs[:count], refs[count:]
    sems, turned, weights, *buffers = refs[-3 - count :]
    before, (total_ref, mine_ref, other_ref) = refs[: -6 - count], refs[-6 - count : -3 - count]
    width = weights.shape[1]
    cut = width // 2
    copies = []

    def fetch(source, target):
        copies.append(pltpu.make_async_copy(source, target, sems.at[len(copies)]))
        copies[-1].start()
        return copies[-1]

    pending = {}
    turned_copy = None
    for index, blocks in enumerate(sources):
        columns = pl.ds(pl.multiple_of(where_ref[1 + index] * width, width), width)
        pending["weight", index] = fetch(weight_ref.at[:, columns], weights.at[index])
        for operand, _, _, _ in blocks:
            if ("piece", operand) not in pending:
                pending["piece", operand] = fetch(pieces[operand], buffers[operand])
        if turned_copy is None:
            turned_copy = fetch(turned_ref, turned)
    pending["turned"] = turned_copy
    done = set()

    def ready(key):
        if key not in done:
            done.add(key)
            pending[key].wait()

    mine = pl.multiple_of(where_ref[0] * cut, cut)
    other = pl.multiple_of((1 - where_ref[0]) * cut, cut)
    total = before[0] if before else total_ref
    for index, blocks in enumerate(sources):
        ready(("weight", index))
        for operand, _, _, _ in blocks:
            ready(("piece", operand))
        weight = weights[index]
        for operand, there, row, rows in blocks:
            term = contract_last(buffers[operand][pl.ds(there, rows), :], weight)
            at = pl.ds(row, rows)
            if before or index:
                term = total[at, :] + term
            total_ref[at, :] = term.astype(total_ref.dtype)
        total = total_ref
        ready("turned")
        for out, begin in ((mine_ref, mine), (other_ref, other)):
            part = None
            for operand, there, row, rows in blocks:
                term = jnp.dot(
                    turned[:, pl.ds(row, rows)],
                    buffers[operand][pl.ds(there, rows), pl.ds(begin, cut)],
                    preferred_element_type=jnp.float32,
                )
                part = term if part is None else part + term
            out[index] = part.astype(out.dtype)


def in_hbm(value):
    return pltpu.with_memory_space_constraint(value, pltpu.HBM)


def hbm():
    return pl.BlockSpec(memory_space=pltpu.HBM)


def project(sources, last, flops, where, weight, turned, pieces, before):
    width, tok = turned.shape
    count = len(sources)
    parts = jax.ShapeDtypeStruct((count, width, width // 2), jnp.bfloat16)
    pieces = [in_hbm(piece) for piece in pieces]
    shapes = [piece.shape for piece in pieces]
    return pl.pallas_call(
        lambda *refs: project_kernel(sources, shapes, *refs),
        in_specs=[pl.BlockSpec(memory_space=pltpu.SMEM)] + [hbm()] * (2 + len(pieces)) + [whole()] * len(before),
        out_specs=[whole()] * 3,
        scratch_shapes=[
            pltpu.SemaphoreType.DMA((count + len(pieces) + 1,)), pltpu.VMEM((width, tok), jnp.bfloat16),
            pltpu.VMEM((count, width, width), jnp.bfloat16),
        ] + [pltpu.VMEM(shape, jnp.bfloat16) for shape in shapes],
        out_shape=[jax.ShapeDtypeStruct((tok, width), jnp.bfloat16 if last else jnp.float32), parts, parts],
        compiler_params=pltpu.CompilerParams(vmem_limit_bytes=VMEM_BYTES),
        cost_estimate=pl.CostEstimate(flops=flops, bytes_accessed=1 << 20, transcendentals=0),
        name="project",
    )(where, weight, turned, *pieces, *before)


def place_kernel(counts, where_ref, *refs):
    sems, mine, come = refs[-3:]
    out_ref, refs = refs[-4], refs[:-4]
    copies, index = [], 0
    for i, count in enumerate(counts):
        rows = pl.ds(index, count)
        for source, target, sem in ((refs[2 * i], mine, 2 * i), (refs[2 * i + 1], come, 2 * i + 1)):
            copies.append(pltpu.make_async_copy(source, target.at[rows], sems.at[sem]))
            copies[-1].start()
        index += count
    index = 0
    for i, count in enumerate(counts):
        copies[2 * i].wait()
        copies[2 * i + 1].wait()
        for _ in range(count):
            both = mine[index].astype(jnp.float32) + come[index].astype(jnp.float32)
            out_ref[where_ref[index]] = both.astype(out_ref.dtype)
            index += 1


def whole():
    return pl.BlockSpec(memory_space=pltpu.VMEM)


def local(queries, keys, values, out_weight, out_grad, doc_ids):
    tok = queries.shape[0]
    heads = queries.shape[1] // HEAD_SIZE
    blocks = tok // ROWS
    span = 2 * tok + ROWS
    shard = lax.axis_index("seq")
    docs = jnp.pad(doc_ids.astype(jnp.bfloat16).reshape(tok // HEAD_SIZE, HEAD_SIZE), ((0, 16 - tok // HEAD_SIZE), (0, 0)))
    own = jnp.concatenate([keys, values, docs], axis=0)
    far, near = shifted(own, "seq", 2), shifted(own, "seq", 1)
    doc_of = lambda part: part[2 * tok : 2 * tok + tok // HEAD_SIZE].reshape(tok).astype(jnp.int32)
    doc_keys = jnp.concatenate([
        jnp.where(shard >= 2, doc_of(far), -1), jnp.where(shard >= 1, doc_of(near), -1), doc_ids
    ])
    earlier = jnp.sum((doc_keys[None, :] < doc_ids[:, None]).astype(jnp.int32), axis=1)
    low = jnp.maximum(earlier, jnp.arange(tok, dtype=jnp.int32) + 1)[:, None]

    all_heads = heads * HEAD_SIZE
    row_block = pl.BlockSpec((ROWS, all_heads), lambda b: (b, 0))
    held = [pltpu.VMEM((3 * tok, HEAD_SIZE), jnp.bfloat16)] * 2
    work = heads * tok * span * HEAD_SIZE * 2
    rows_of = lambda dtype: jax.ShapeDtypeStruct((tok, all_heads), dtype)
    expo, attn, turned, inverse = pl.pallas_call(
        lambda *refs: forward_kernel(tok, span, heads, *refs),
        grid=(blocks,),
        in_specs=[pl.BlockSpec((ROWS, 1), lambda b: (b, 0)), row_block, whole(), whole(), whole()],
        out_specs=[
            pl.BlockSpec((heads, ROWS, span), lambda b: (0, b, 0)), row_block,
            pl.BlockSpec((all_heads, ROWS), lambda b: (0, b)), row_block,
        ],
        out_shape=[
            pltpu.HBM((heads, tok, span), jnp.bfloat16), rows_of(jnp.bfloat16),
            pltpu.HBM((all_heads, tok), jnp.bfloat16), rows_of(jnp.float32),
        ],
        scratch_shapes=held + [pltpu.VMEM((ROWS, span), jnp.float32)],
        compiler_params=pltpu.CompilerParams(vmem_limit_bytes=VMEM_BYTES),
        cost_estimate=pl.CostEstimate(flops=2 * work, bytes_accessed=14 << 20, transcendentals=heads * tok * span),
        name="forward",
    )(low, queries, far, near, own)
    expo = in_hbm(expo)

    tensor = lax.axis_index("tensor")
    row, column = tensor // 4, tensor % 4
    at = lambda flip, step: (row ^ flip) * 4 + (column + step) % 4
    core = shard % 2
    places = [at(0, 0), at(0, 3), at(0, 1), at(0, 2), at(1, 0), at(1, 3), at(1, 1), at(1, 2)]
    where = lambda some: jnp.stack([core, *some]).astype(jnp.int32)
    near_up, near_down, opposite = step_x(out_grad, 1), step_x(out_grad, -1), step_x(out_grad, 2)
    across = step_y(lax.optimization_barrier((out_grad, far, near))[0])
    across, turned = lax.optimization_barrier((across, turned))
    across_up, across_down = step_x(across, 1), step_x(across, -1)
    weight, turned = in_hbm(out_weight), in_hbm(turned)
    real = lambda count: 4 * count * tok * all_heads * all_heads
    total, mine_a, other_a = project(
        [((p, 0, 0, tok),) for p in range(4)], False, real(4),
        where(places[:4]), weight, turned, (out_grad, near_up, near_down, opposite), (),
    )
    last = step_y(opposite)
    total, mine_b, other_b = project(
        [((p, 0, 0, tok),) for p in range(3)], False, 4 * real(3),
        where(places[4:7]), weight, turned, (across, across_up, across_down), (total,),
    )
    attention_gradient, mine_c, other_c = project(
        [((0, 0, 0, tok),)], True, 1 << 20,
        where(places[7:]), weight, turned, (last,), (total,),
    )
    parts = [mine_a, step_core(other_a), mine_b, step_core(other_b), mine_c, step_core(other_c)]
    counts = [part.shape[0] for part in parts[::2]]
    both = pltpu.VMEM((8,) + mine_a.shape[1:], jnp.bfloat16)
    placed = pl.pallas_call(
        lambda *refs: place_kernel(counts, *refs),
        in_specs=[pl.BlockSpec(memory_space=pltpu.SMEM)] + [hbm()] * 6,
        out_specs=whole(),
        out_shape=jax.ShapeDtypeStruct((8,) + mine_a.shape[1:], jnp.bfloat16),
        scratch_shapes=[pltpu.SemaphoreType.DMA((6,)), both, both],
        compiler_params=pltpu.CompilerParams(vmem_limit_bytes=VMEM_BYTES),
        cost_estimate=pl.CostEstimate(flops=1 << 20, bytes_accessed=1 << 20, transcendentals=0),
        name="place",
    )(jnp.stack(places).astype(jnp.int32), *[in_hbm(part) for part in parts])
    placed, attention_gradient = lax.optimization_barrier((placed, attention_gradient))
    groups = [[2 * chip + c for chip in range(8)] for c in range(2)]
    arrived = lax.all_to_all(placed, "seq", 0, 0, axis_index_groups=groups)
    weight_grad = jnp.sum(arrived.astype(jnp.float32), axis=0).astype(jnp.bfloat16)

    pair = lambda dtype: jax.ShapeDtypeStruct((2 * tok, HEAD_SIZE), dtype)
    sums = lambda width: [pltpu.VMEM((width, HEAD_SIZE), jnp.bfloat16)] * 2 + [pltpu.VMEM((HEAD_SIZE, width), jnp.float32)] * 2
    past_queries, far_sum, near_sum = pl.pallas_call(
        lambda *refs: backward_past_kernel(tok, heads, *refs),
        grid=(blocks,),
        in_specs=[row_block] * 4 + [pl.BlockSpec((heads, ROWS, 2 * tok), lambda b: (0, b, 0)), whole(), whole()],
        out_specs=[row_block, whole(), whole()],
        out_shape=[rows_of(jnp.float32), pair(jnp.bfloat16), pair(jnp.bfloat16)],
        scratch_shapes=sums(2 * tok),
        compiler_params=pltpu.CompilerParams(vmem_limit_bytes=VMEM_BYTES),
        cost_estimate=pl.CostEstimate(flops=1 << 20, bytes_accessed=1 << 20, transcendentals=0),
        name="backward_past",
    )(queries, attention_gradient, attn, inverse, expo, far, near)
    far_come, near_come = shifted(far_sum, "seq", -2), shifted(near_sum, "seq", -1)
    last_blocks = [pl.BlockSpec((heads, ROWS, ROWS), lambda b, i=i: (0, b, span // ROWS - blocks + i)) for i in range(blocks)]
    grad_queries, own_sum = pl.pallas_call(
        lambda *refs: backward_own_kernel(tok, heads, *refs),
        grid=(blocks,),
        in_specs=[row_block] * 4 + last_blocks + [whole(), row_block],
        out_specs=[row_block, whole()],
        out_shape=[rows_of(jnp.bfloat16), pair(jnp.float32)],
        scratch_shapes=sums(tok),
        compiler_params=pltpu.CompilerParams(vmem_limit_bytes=VMEM_BYTES),
        cost_estimate=pl.CostEstimate(flops=1 << 20, bytes_accessed=1 << 20, transcendentals=0),
        name="backward_own",
    )(queries, attention_gradient, attn, inverse, *([expo] * blocks), own, past_queries)
    total = own_sum + near_come.astype(jnp.float32) + far_come.astype(jnp.float32)
    total = total.astype(jnp.bfloat16)
    return (grad_queries, total[:tok], total[tok:], weight_grad)


def solution(mesh):
    placed = (
        P("seq", "tensor"),
        P("seq", "tensor"),
        P("seq", "tensor"),
        P("tensor", None),
        P("seq", "tensor"),
        P("seq"),
    )
    return jax.shard_map(
        local,
        mesh=mesh,
        in_specs=placed,
        out_specs=(P("seq", "tensor"), P("seq", "tensor"), P("seq", "tensor"), P("tensor", "seq")),
        check_vma=False,
    )
```

```python
import math

import jax
import jax.numpy as jnp
from jax import lax
from jax.experimental import pallas as pl
from jax.experimental.pallas import tpu as pltpu
from jax.sharding import PartitionSpec as P

HEAD_SIZE = 128
NEG_BIG = -1e30
ROWS = 256
VMEM_BYTES = 20 << 20


def shifted(value, axis, steps):
    count = lax.axis_size(axis)
    initial, last = (max(0, -steps), min(count, count - steps))
    return lax.ppermute(value, axis, [(source, source + steps) for source in range(initial, last)])


def step_x(value, step):
    pairs = [(t, t // 4 * 4 + (t + step) % 4) for t in range(8)]
    return lax.ppermute(value, "tensor", pairs)


def step_y(value):
    return lax.ppermute(value, "tensor", [(t, t ^ 4) for t in range(8)])


def step_core(value):
    return lax.ppermute(value, "seq", [(s, s ^ 1) for s in range(16)])


def contract_rows(left, right):
    return lax.dot_general(
        left, right, (((0,), (0,)), ((), ())), preferred_element_type=jnp.float32
    )


def contract_last(left, right):
    return lax.dot_general(
        left, right, (((1,), (1,)), ((), ())), preferred_element_type=jnp.float32
    )


def gather_keys(parts, key_all, value_all, tok):
    for index, part in enumerate(parts):
        rows = pl.ds(index * tok, tok)
        key_all[rows, :] = part[pl.ds(0, tok), :]
        value_all[rows, :] = part[pl.ds(tok, tok), :]


def forward_kernel(
    tok, span, heads, low_ref, q_ref, far_ref, near_ref, own_ref,
    expo_ref, attn_ref, turned_ref, inverse_ref, key_all, value_all, bias,
):
    @pl.when(pl.program_id(0) == 0)
    def _():
        gather_keys((far_ref, near_ref, own_ref), key_all, value_all, tok)

    begin = pl.multiple_of(pl.program_id(0) * ROWS, ROWS)
    window = pl.ds(begin, span)
    key_at = lax.broadcasted_iota(jnp.int32, (ROWS, span), 1)
    row_at = lax.broadcasted_iota(jnp.int32, (ROWS, 1), 0)
    visible = (key_at >= low_ref[...] - begin) & (key_at <= row_at + 2 * tok)
    bias[...] = jnp.where(visible, 0.0, NEG_BIG)
    for head in range(heads):
        columns = slice(head * HEAD_SIZE, (head + 1) * HEAD_SIZE)
        raw = contract_last(q_ref[:, columns], key_all[window, :]) + bias[...]
        top = jnp.max(raw, axis=1, keepdims=True)
        expo = jnp.exp2((raw - top) * (math.log2(math.e) / math.sqrt(HEAD_SIZE)))
        inverse = 1.0 / jnp.sum(expo, axis=1, keepdims=True)
        expo_low = expo.astype(jnp.bfloat16)
        expo_ref[head] = expo_low
        inverse_ref[:, columns] = jnp.broadcast_to(inverse, (ROWS, HEAD_SIZE))
        attn = jnp.dot(expo_low, value_all[window, :], preferred_element_type=jnp.float32) * inverse
        attn = attn.astype(jnp.bfloat16)
        attn_ref[:, columns] = attn
        turned_ref[columns, :] = attn.T


def backward_rows(heads, width, first, q_ref, grad_ref, attn_ref, inverse_ref, probs_of, keys, values, gq_of, key_sum, value_sum):
    at = slice(first, first + width)
    for head in range(heads):
        columns = slice(head * HEAD_SIZE, (head + 1) * HEAD_SIZE)
        grad = (grad_ref[:, columns].astype(jnp.float32) * inverse_ref[:, columns]).astype(jnp.bfloat16)
        delta = jnp.sum(grad.astype(jnp.float32) * attn_ref[:, columns].astype(jnp.float32), axis=1, keepdims=True)
        d_prob = contract_last(grad, values[at, :])
        probs = probs_of(head)
        d_score = (probs.astype(jnp.float32) * (d_prob - delta)).astype(jnp.bfloat16)
        gq_of(columns, jnp.dot(d_score, keys[at, :], preferred_element_type=jnp.float32))
        key_sum[:, at] += jnp.dot(q_ref[:, columns].T, d_score, preferred_element_type=jnp.float32)
        value_sum[:, at] += jnp.dot(grad.T, probs, preferred_element_type=jnp.float32)


def backward_past_kernel(
    tok, heads, q_ref, grad_ref, attn_ref, inverse_ref, expo_ref, far_ref, near_ref,
    gq_ref, far_out, near_out, key_all, value_all, key_sum, value_sum,
):
    scale = 1.0 / math.sqrt(HEAD_SIZE)

    @pl.when(pl.program_id(0) == 0)
    def _():
        gather_keys((far_ref, near_ref), key_all, value_all, tok)
        key_sum[...] = jnp.zeros_like(key_sum)
        value_sum[...] = jnp.zeros_like(value_sum)

    def put(columns, value):
        gq_ref[:, columns] = value

    for block in range(tok // ROWS):
        @pl.when(pl.program_id(0) == block)
        def _(block=block):
            first = block * ROWS
            width = 2 * tok - first
            backward_rows(
                heads, width, first, q_ref, grad_ref, attn_ref, inverse_ref,
                lambda head: expo_ref[head, :, :width], key_all, value_all, put, key_sum, value_sum,
            )

    @pl.when(pl.program_id(0) == pl.num_programs(0) - 1)
    def _():
        for index, out in enumerate((far_out, near_out)):
            rows = pl.ds(index * tok, tok)
            out[pl.ds(0, tok), :] = (key_sum[:, rows].T * scale).astype(out.dtype)
            out[pl.ds(tok, tok), :] = value_sum[:, rows].T.astype(out.dtype)


def backward_own_kernel(
    tok, heads, q_ref, grad_ref, attn_ref, inverse_ref, expo_a, expo_b, expo_c, own_ref, past_ref,
    gq_ref, own_out, key_all, value_all, key_sum, value_sum,
):
    scale = 1.0 / math.sqrt(HEAD_SIZE)
    blocks = tok // ROWS
    expos = (expo_a, expo_b, expo_c)

    @pl.when(pl.program_id(0) == 0)
    def _():
        gather_keys((own_ref,), key_all, value_all, tok)
        key_sum[...] = jnp.zeros_like(key_sum)
        value_sum[...] = jnp.zeros_like(value_sum)

    def put(columns, value):
        gq_ref[:, columns] = ((past_ref[:, columns] + value) * scale).astype(gq_ref.dtype)

    for block in range(blocks):
        @pl.when(pl.program_id(0) == block)
        def _(block=block):
            width = (block + 1) * ROWS
            probs_of = lambda head: jnp.concatenate([expo[head] for expo in expos[blocks - 1 - block :]], axis=1)
            backward_rows(
                heads, width, 0, q_ref, grad_ref, attn_ref, inverse_ref,
                probs_of, key_all, value_all, put, key_sum, value_sum,
            )

    @pl.when(pl.program_id(0) == pl.num_programs(0) - 1)
    def _():
        own_out[pl.ds(0, tok), :] = key_sum[...].T * scale
        own_out[pl.ds(tok, tok), :] = value_sum[...].T


def project_kernel(sources, shapes, groups, where_ref, weight_ref, turned_ref, *refs):
    count = len(shapes)
    pieces, refs = refs[:count], refs[count:]
    earlier, refs = refs[: 2 * len(groups)], refs[2 * len(groups) :]
    if groups:
        come, placed, placed_sems = refs[-3:]
        refs = refs[:-3]
    sems, turned, weights, *buffers = refs[-3 - count :]
    refs = refs[: -3 - count]
    if groups:
        placed_ref, refs = refs[-1], refs[:-1]
    before, (total_ref, mine_ref, other_ref) = refs[:-3], refs[-3:]
    width = weights.shape[1]
    cut = width // 2
    copies = []

    def fetch(source, target):
        copies.append(pltpu.make_async_copy(source, target, sems.at[len(copies)]))
        copies[-1].start()
        return copies[-1]

    pending = {}
    turned_copy = None
    for index, blocks in enumerate(sources):
        columns = pl.ds(pl.multiple_of(where_ref[1 + index] * width, width), width)
        pending["weight", index] = fetch(weight_ref.at[:, columns], weights.at[index])
        for operand, _, _, _ in blocks:
            if ("piece", operand) not in pending:
                pending["piece", operand] = fetch(pieces[operand], buffers[operand])
        if turned_copy is None:
            turned_copy = fetch(turned_ref, turned)
    pending["turned"] = turned_copy
    at, loads = 0, []
    for i, size in enumerate(groups):
        for j, target in enumerate((placed, come)):
            loads.append(pltpu.make_async_copy(earlier[2 * i + j], target.at[pl.ds(at, size)], placed_sems.at[2 * i + j]))
            loads[-1].start()
        at += size
    done = set()

    def ready(key):
        if key not in done:
            done.add(key)
            pending[key].wait()

    mine = pl.multiple_of(where_ref[0] * cut, cut)
    other = pl.multiple_of((1 - where_ref[0]) * cut, cut)
    total = before[0] if before else total_ref
    for index, blocks in enumerate(sources):
        ready(("weight", index))
        for operand, _, _, _ in blocks:
            ready(("piece", operand))
        weight = weights[index]
        for operand, there, row, rows in blocks:
            term = contract_last(buffers[operand][pl.ds(there, rows), :], weight)
            at = pl.ds(row, rows)
            if before or index:
                term = total[at, :] + term
            total_ref[at, :] = term.astype(total_ref.dtype)
        total = total_ref
        ready("turned")
        for out, begin in ((mine_ref, mine), (other_ref, other)):
            part = None
            for operand, there, row, rows in blocks:
                term = jnp.dot(
                    turned[:, pl.ds(row, rows)],
                    buffers[operand][pl.ds(there, rows), pl.ds(begin, cut)],
                    preferred_element_type=jnp.float32,
                )
                part = term if part is None else part + term
            out[index] = part.astype(out.dtype)
    for load in loads:
        load.wait()
    stores = []
    for index in range(sum(groups)):
        both = placed[index].astype(jnp.float32) + come[index].astype(jnp.float32)
        placed[index] = both.astype(placed.dtype)
        place = where_ref[1 + len(sources) + index]
        stores.append(pltpu.make_async_copy(placed.at[index], placed_ref.at[place], placed_sems.at[2 * len(groups) + index]))
        stores[-1].start()
    for store in stores:
        store.wait()


def in_hbm(value):
    return pltpu.with_memory_space_constraint(value, pltpu.HBM)


def hbm():
    return pl.BlockSpec(memory_space=pltpu.HBM)


def project(sources, last, flops, where, weight, turned, pieces, before, earlier=()):
    width, tok = turned.shape
    count = len(sources)
    parts = jax.ShapeDtypeStruct((count, width, width // 2), jnp.bfloat16)
    pieces = [in_hbm(piece) for piece in pieces]
    earlier = [in_hbm(part) for part in earlier]
    shapes = [piece.shape for piece in pieces]
    groups = [part.shape[0] for part in earlier[::2]]
    slots = (sum(groups), width, width // 2)
    out_specs = [whole()] * 3
    out_shape = [jax.ShapeDtypeStruct((tok, width), jnp.bfloat16 if last else jnp.float32), parts, parts]
    scratch = [
        pltpu.SemaphoreType.DMA((count + len(pieces) + 1,)), pltpu.VMEM((width, tok), jnp.bfloat16),
        pltpu.VMEM((count, width, width), jnp.bfloat16),
    ] + [pltpu.VMEM(shape, jnp.bfloat16) for shape in shapes]
    if groups:
        out_specs.append(hbm())
        out_shape.append(pltpu.HBM((8,) + slots[1:], jnp.bfloat16))
        scratch += [pltpu.VMEM(slots, jnp.bfloat16)] * 2 + [pltpu.SemaphoreType.DMA((2 * len(groups) + slots[0],))]
    return pl.pallas_call(
        lambda *refs: project_kernel(sources, shapes, groups, *refs),
        in_specs=[pl.BlockSpec(memory_space=pltpu.SMEM)] + [hbm()] * (2 + len(pieces) + len(earlier)) + [whole()] * len(before),
        out_specs=out_specs,
        scratch_shapes=scratch,
        out_shape=out_shape,
        compiler_params=pltpu.CompilerParams(vmem_limit_bytes=VMEM_BYTES),
        cost_estimate=pl.CostEstimate(flops=flops, bytes_accessed=1 << 20, transcendentals=0),
        name="project",
    )(where, weight, turned, *pieces, *earlier, *before)


def place_kernel(where_ref, mine_ref, come_ref, earlier_ref, out_ref, both, sem):
    both[...] = (mine_ref[...].astype(jnp.float32) + come_ref[...].astype(jnp.float32)).astype(both.dtype)
    copy = pltpu.make_async_copy(both, out_ref.at[pl.ds(where_ref[0], 1)], sem)
    copy.start()
    copy.wait()


def whole():
    return pl.BlockSpec(memory_space=pltpu.VMEM)


def local(queries, keys, values, out_weight, out_grad, doc_ids):
    tok = queries.shape[0]
    heads = queries.shape[1] // HEAD_SIZE
    blocks = tok // ROWS
    span = 2 * tok + ROWS
    shard = lax.axis_index("seq")
    docs = jnp.pad(doc_ids.astype(jnp.bfloat16).reshape(tok // HEAD_SIZE, HEAD_SIZE), ((0, 16 - tok // HEAD_SIZE), (0, 0)))
    own = jnp.concatenate([keys, values, docs], axis=0)
    far, near = shifted(own, "seq", 2), shifted(own, "seq", 1)
    doc_of = lambda part: part[2 * tok : 2 * tok + tok // HEAD_SIZE].reshape(tok).astype(jnp.int32)
    doc_keys = jnp.concatenate([
        jnp.where(shard >= 2, doc_of(far), -1), jnp.where(shard >= 1, doc_of(near), -1), doc_ids
    ])
    earlier = jnp.sum((doc_keys[None, :] < doc_ids[:, None]).astype(jnp.int32), axis=1)
    low = jnp.maximum(earlier, jnp.arange(tok, dtype=jnp.int32) + 1)[:, None]

    all_heads = heads * HEAD_SIZE
    row_block = pl.BlockSpec((ROWS, all_heads), lambda b: (b, 0))
    held = [pltpu.VMEM((3 * tok, HEAD_SIZE), jnp.bfloat16)] * 2
    work = heads * tok * span * HEAD_SIZE * 2
    rows_of = lambda dtype: jax.ShapeDtypeStruct((tok, all_heads), dtype)
    expo, attn, turned, inverse = pl.pallas_call(
        lambda *refs: forward_kernel(tok, span, heads, *refs),
        grid=(blocks,),
        in_specs=[pl.BlockSpec((ROWS, 1), lambda b: (b, 0)), row_block, whole(), whole(), whole()],
        out_specs=[
            pl.BlockSpec((heads, ROWS, span), lambda b: (0, b, 0)), row_block,
            pl.BlockSpec((all_heads, ROWS), lambda b: (0, b)), row_block,
        ],
        out_shape=[
            pltpu.HBM((heads, tok, span), jnp.bfloat16), pltpu.HBM((tok, all_heads), jnp.bfloat16),
            pltpu.HBM((all_heads, tok), jnp.bfloat16), pltpu.HBM((tok, all_heads), jnp.float32),
        ],
        scratch_shapes=held + [pltpu.VMEM((ROWS, span), jnp.float32)],
        compiler_params=pltpu.CompilerParams(vmem_limit_bytes=VMEM_BYTES),
        cost_estimate=pl.CostEstimate(flops=2 * work, bytes_accessed=14 << 20, transcendentals=heads * tok * span),
        name="forward",
    )(low, queries, far, near, own)
    expo, attn, inverse, queries = in_hbm(expo), in_hbm(attn), in_hbm(inverse), in_hbm(queries)

    tensor = lax.axis_index("tensor")
    row, column = tensor // 4, tensor % 4
    at = lambda flip, step: (row ^ flip) * 4 + (column + step) % 4
    core = shard % 2
    places = [at(0, 0), at(0, 3), at(0, 1), at(0, 2), at(1, 0), at(1, 3), at(1, 1), at(1, 2)]
    where = lambda some: jnp.stack([core, *some]).astype(jnp.int32)
    near_up, near_down, opposite = step_x(out_grad, 1), step_x(out_grad, -1), step_x(out_grad, 2)
    across = step_y(lax.optimization_barrier((out_grad, far, near))[0])
    across, turned = lax.optimization_barrier((across, turned))
    across_up, across_down = step_x(across, 1), step_x(across, -1)
    weight, turned = in_hbm(out_weight), in_hbm(turned)
    real = lambda count: 4 * count * tok * all_heads * all_heads
    last = step_y(opposite)
    total, mine_a, other_a = project(
        [((p, 0, 0, tok),) for p in range(5)], False, real(5),
        where(places[:5]), weight, turned, (out_grad, near_up, near_down, opposite, across), (),
    )
    come_a = step_core(other_a)
    total, mine_b, other_b = project(
        [((p, 0, 0, tok),) for p in range(2)], False, 1 << 20,
        where(places[5:7]), weight, turned, (across_up, across_down), (total,),
    )
    come_b = step_core(other_b)
    attention_gradient, mine_c, other_c, placed = project(
        [((0, 0, 0, tok),)], True, 1 << 20, where(places[7:] + places[:7]), weight, turned, (last,), (total,),
        (mine_a, come_a, mine_b, come_b),
    )
    come_c = step_core(other_c)
    placed = pl.pallas_call(
        place_kernel,
        in_specs=[pl.BlockSpec(memory_space=pltpu.SMEM), whole(), whole(), hbm()],
        out_specs=hbm(),
        out_shape=pltpu.HBM(placed.shape, placed.dtype),
        input_output_aliases={3: 0},
        scratch_shapes=[pltpu.VMEM(mine_c.shape, mine_c.dtype), pltpu.SemaphoreType.DMA(())],
        compiler_params=pltpu.CompilerParams(vmem_limit_bytes=VMEM_BYTES),
        cost_estimate=pl.CostEstimate(flops=1 << 20, bytes_accessed=1 << 20, transcendentals=0),
        name="place",
    )(jnp.stack(places[7:]).astype(jnp.int32), mine_c, come_c, placed)
    placed, attention_gradient = lax.optimization_barrier((placed, attention_gradient))
    groups = [[2 * chip + c for chip in range(8)] for c in range(2)]
    arrived = lax.all_to_all(placed, "seq", 0, 0, axis_index_groups=groups)
    weight_grad = jnp.sum(arrived.astype(jnp.float32), axis=0).astype(jnp.bfloat16)

    pair = lambda dtype: jax.ShapeDtypeStruct((2 * tok, HEAD_SIZE), dtype)
    sums = lambda width: [pltpu.VMEM((width, HEAD_SIZE), jnp.bfloat16)] * 2 + [pltpu.VMEM((HEAD_SIZE, width), jnp.float32)] * 2
    past_queries, far_sum, near_sum = pl.pallas_call(
        lambda *refs: backward_past_kernel(tok, heads, *refs),
        grid=(blocks,),
        in_specs=[row_block] * 4 + [pl.BlockSpec((heads, ROWS, 2 * tok), lambda b: (0, b, 0)), whole(), whole()],
        out_specs=[row_block, whole(), whole()],
        out_shape=[rows_of(jnp.float32), pair(jnp.bfloat16), pair(jnp.bfloat16)],
        scratch_shapes=sums(2 * tok),
        compiler_params=pltpu.CompilerParams(vmem_limit_bytes=VMEM_BYTES),
        cost_estimate=pl.CostEstimate(flops=1 << 20, bytes_accessed=1 << 20, transcendentals=0),
        name="backward_past",
    )(queries, attention_gradient, attn, inverse, expo, far, near)
    far_come, near_come = shifted(far_sum, "seq", -2), shifted(near_sum, "seq", -1)
    last_blocks = [pl.BlockSpec((heads, ROWS, ROWS), lambda b, i=i: (0, b, span // ROWS - blocks + i)) for i in range(blocks)]
    grad_queries, own_sum = pl.pallas_call(
        lambda *refs: backward_own_kernel(tok, heads, *refs),
        grid=(blocks,),
        in_specs=[row_block] * 4 + last_blocks + [whole(), row_block],
        out_specs=[row_block, whole()],
        out_shape=[rows_of(jnp.bfloat16), pair(jnp.float32)],
        scratch_shapes=sums(tok),
        compiler_params=pltpu.CompilerParams(vmem_limit_bytes=VMEM_BYTES),
        cost_estimate=pl.CostEstimate(flops=1 << 20, bytes_accessed=1 << 20, transcendentals=0),
        name="backward_own",
    )(queries, attention_gradient, attn, inverse, *([expo] * blocks), own, past_queries)
    own_sum, weight_grad = lax.optimization_barrier((own_sum, weight_grad))
    total = own_sum + near_come.astype(jnp.float32) + far_come.astype(jnp.float32)
    total = total.astype(jnp.bfloat16)
    return (grad_queries, total[:tok], total[tok:], weight_grad)


def solution(mesh):
    placed = (
        P("seq", "tensor"),
        P("seq", "tensor"),
        P("seq", "tensor"),
        P("tensor", None),
        P("seq", "tensor"),
        P("seq"),
    )
    return jax.shard_map(
        local,
        mesh=mesh,
        in_specs=placed,
        out_specs=(P("seq", "tensor"), P("seq", "tensor"), P("seq", "tensor"), P("tensor", "seq")),
        check_vma=False,
    )
```

```python
import math

import jax
import jax.numpy as jnp
from jax import lax
from jax.experimental import pallas as pl
from jax.experimental.pallas import tpu as pltpu
from jax.sharding import PartitionSpec as P

HEAD_SIZE = 128
NEG_BIG = -1e30
ROWS = 256
VMEM_BYTES = 20 << 20


def shifted(value, axis, steps):
    count = lax.axis_size(axis)
    initial, last = (max(0, -steps), min(count, count - steps))
    return lax.ppermute(value, axis, [(source, source + steps) for source in range(initial, last)])


def step_x(value, step):
    pairs = [(t, t // 4 * 4 + (t + step) % 4) for t in range(8)]
    return lax.ppermute(value, "tensor", pairs)


def step_y(value):
    return lax.ppermute(value, "tensor", [(t, t ^ 4) for t in range(8)])


def step_core(value):
    return lax.ppermute(value, "seq", [(s, s ^ 1) for s in range(16)])


def contract_rows(left, right):
    return lax.dot_general(
        left, right, (((0,), (0,)), ((), ())), preferred_element_type=jnp.float32
    )


def contract_last(left, right):
    return lax.dot_general(
        left, right, (((1,), (1,)), ((), ())), preferred_element_type=jnp.float32
    )


def gather_keys(parts, key_all, value_all, tok):
    for index, part in enumerate(parts):
        rows = pl.ds(index * tok, tok)
        key_all[rows, :] = part[pl.ds(0, tok), :]
        value_all[rows, :] = part[pl.ds(tok, tok), :]


def forward_kernel(
    tok, span, heads, low_ref, q_ref, far_ref, near_ref, own_ref,
    expo_ref, attn_ref, turned_ref, inverse_ref, key_all, value_all, bias,
):
    @pl.when(pl.program_id(0) == 0)
    def _():
        gather_keys((far_ref, near_ref, own_ref), key_all, value_all, tok)

    begin = pl.multiple_of(pl.program_id(0) * ROWS, ROWS)
    window = pl.ds(begin, span)
    key_at = lax.broadcasted_iota(jnp.int32, (ROWS, span), 1)
    row_at = lax.broadcasted_iota(jnp.int32, (ROWS, 1), 0)
    visible = (key_at >= low_ref[...] - begin) & (key_at <= row_at + 2 * tok)
    bias[...] = jnp.where(visible, 0.0, NEG_BIG)
    for head in range(heads):
        columns = slice(head * HEAD_SIZE, (head + 1) * HEAD_SIZE)
        raw = contract_last(q_ref[:, columns], key_all[window, :]) + bias[...]
        top = jnp.max(raw, axis=1, keepdims=True)
        expo = jnp.exp2((raw - top) * (math.log2(math.e) / math.sqrt(HEAD_SIZE)))
        inverse = 1.0 / jnp.sum(expo, axis=1, keepdims=True)
        expo_low = expo.astype(jnp.bfloat16)
        expo_ref[head] = expo_low
        inverse_ref[:, columns] = jnp.broadcast_to(inverse, (ROWS, HEAD_SIZE))
        attn = jnp.dot(expo_low, value_all[window, :], preferred_element_type=jnp.float32) * inverse
        attn = attn.astype(jnp.bfloat16)
        attn_ref[:, columns] = attn
        turned_ref[columns, :] = attn.T


def backward_rows(heads, width, first, q_ref, grad_ref, attn_ref, inverse_ref, probs_of, keys, values, gq_of, key_sum, value_sum):
    at = slice(first, first + width)
    for head in range(heads):
        columns = slice(head * HEAD_SIZE, (head + 1) * HEAD_SIZE)
        grad = (grad_ref[:, columns].astype(jnp.float32) * inverse_ref[:, columns]).astype(jnp.bfloat16)
        delta = jnp.sum(grad.astype(jnp.float32) * attn_ref[:, columns].astype(jnp.float32), axis=1, keepdims=True)
        d_prob = contract_last(grad, values[at, :])
        probs = probs_of(head)
        d_score = (probs.astype(jnp.float32) * (d_prob - delta)).astype(jnp.bfloat16)
        gq_of(columns, jnp.dot(d_score, keys[at, :], preferred_element_type=jnp.float32))
        key_sum[:, at] += jnp.dot(q_ref[:, columns].T, d_score, preferred_element_type=jnp.float32)
        value_sum[:, at] += jnp.dot(grad.T, probs, preferred_element_type=jnp.float32)


def backward_past_kernel(
    tok, heads, q_ref, grad_ref, attn_ref, inverse_ref, expo_ref, far_ref, near_ref,
    gq_ref, far_out, near_out, key_all, value_all, key_sum, value_sum,
):
    scale = 1.0 / math.sqrt(HEAD_SIZE)

    @pl.when(pl.program_id(0) == 0)
    def _():
        gather_keys((far_ref, near_ref), key_all, value_all, tok)
        key_sum[...] = jnp.zeros_like(key_sum)
        value_sum[...] = jnp.zeros_like(value_sum)

    def put(columns, value):
        gq_ref[:, columns] = value

    for block in range(tok // ROWS):
        @pl.when(pl.program_id(0) == block)
        def _(block=block):
            first = block * ROWS
            width = 2 * tok - first
            backward_rows(
                heads, width, first, q_ref, grad_ref, attn_ref, inverse_ref,
                lambda head: expo_ref[head, :, :width], key_all, value_all, put, key_sum, value_sum,
            )

    @pl.when(pl.program_id(0) == pl.num_programs(0) - 1)
    def _():
        for index, out in enumerate((far_out, near_out)):
            rows = pl.ds(index * tok, tok)
            out[pl.ds(0, tok), :] = (key_sum[:, rows].T * scale).astype(out.dtype)
            out[pl.ds(tok, tok), :] = value_sum[:, rows].T.astype(out.dtype)


def backward_own_kernel(
    tok, heads, q_ref, grad_ref, attn_ref, inverse_ref, expo_a, expo_b, expo_c, own_ref, past_ref,
    gq_ref, own_out, key_all, value_all, key_sum, value_sum,
):
    scale = 1.0 / math.sqrt(HEAD_SIZE)
    blocks = tok // ROWS
    expos = (expo_a, expo_b, expo_c)

    @pl.when(pl.program_id(0) == 0)
    def _():
        gather_keys((own_ref,), key_all, value_all, tok)
        key_sum[...] = jnp.zeros_like(key_sum)
        value_sum[...] = jnp.zeros_like(value_sum)

    def put(columns, value):
        gq_ref[:, columns] = ((past_ref[:, columns] + value) * scale).astype(gq_ref.dtype)

    for block in range(blocks):
        @pl.when(pl.program_id(0) == block)
        def _(block=block):
            width = (block + 1) * ROWS
            probs_of = lambda head: jnp.concatenate([expo[head] for expo in expos[blocks - 1 - block :]], axis=1)
            backward_rows(
                heads, width, 0, q_ref, grad_ref, attn_ref, inverse_ref,
                probs_of, key_all, value_all, put, key_sum, value_sum,
            )

    @pl.when(pl.program_id(0) == pl.num_programs(0) - 1)
    def _():
        own_out[pl.ds(0, tok), :] = key_sum[...].T * scale
        own_out[pl.ds(tok, tok), :] = value_sum[...].T


def project_kernel(sources, shapes, groups, where_ref, weight_ref, turned_ref, *refs):
    count = len(shapes)
    pieces, refs = refs[:count], refs[count:]
    earlier, refs = refs[: 2 * len(groups)], refs[2 * len(groups) :]
    if groups:
        come, placed, placed_sems = refs[-3:]
        refs = refs[:-3]
    sems, turned, weights, *buffers = refs[-3 - count :]
    refs = refs[: -3 - count]
    if groups:
        placed_ref, refs = refs[-1], refs[:-1]
    before, (total_ref, mine_ref, other_ref) = refs[:-3], refs[-3:]
    width = weights.shape[1]
    cut = width // 2
    copies = []

    def fetch(source, target):
        copies.append(pltpu.make_async_copy(source, target, sems.at[len(copies)]))
        copies[-1].start()
        return copies[-1]

    pending = {}
    turned_copy = None
    for index, blocks in enumerate(sources):
        columns = pl.ds(pl.multiple_of(where_ref[1 + index] * width, width), width)
        pending["weight", index] = fetch(weight_ref.at[:, columns], weights.at[index])
        for operand, _, _, _ in blocks:
            if ("piece", operand) not in pending:
                pending["piece", operand] = fetch(pieces[operand], buffers[operand])
        if turned_copy is None:
            turned_copy = fetch(turned_ref, turned)
    pending["turned"] = turned_copy
    at, loads = 0, []
    for i, size in enumerate(groups):
        for j, target in enumerate((placed, come)):
            loads.append(pltpu.make_async_copy(earlier[2 * i + j], target.at[pl.ds(at, size)], placed_sems.at[2 * i + j]))
            loads[-1].start()
        at += size
    done = set()

    def ready(key):
        if key not in done:
            done.add(key)
            pending[key].wait()

    mine = pl.multiple_of(where_ref[0] * cut, cut)
    other = pl.multiple_of((1 - where_ref[0]) * cut, cut)
    total = before[0] if before else total_ref
    for index, blocks in enumerate(sources):
        ready(("weight", index))
        for operand, _, _, _ in blocks:
            ready(("piece", operand))
        weight = weights[index]
        for operand, there, row, rows in blocks:
            term = contract_last(buffers[operand][pl.ds(there, rows), :], weight)
            at = pl.ds(row, rows)
            if before or index:
                term = total[at, :] + term
            total_ref[at, :] = term.astype(total_ref.dtype)
        total = total_ref
        ready("turned")
        for out, begin in ((mine_ref, mine), (other_ref, other)):
            part = None
            for operand, there, row, rows in blocks:
                term = jnp.dot(
                    turned[:, pl.ds(row, rows)],
                    buffers[operand][pl.ds(there, rows), pl.ds(begin, cut)],
                    preferred_element_type=jnp.float32,
                )
                part = term if part is None else part + term
            out[index] = part.astype(out.dtype)
    for load in loads:
        load.wait()
    stores = []
    for index in range(sum(groups)):
        both = placed[index].astype(jnp.float32) + come[index].astype(jnp.float32)
        placed[index] = both.astype(placed.dtype)
        place = where_ref[1 + len(sources) + index]
        stores.append(pltpu.make_async_copy(placed.at[index], placed_ref.at[place], placed_sems.at[2 * len(groups) + index]))
        stores[-1].start()
    for store in stores:
        store.wait()


def in_hbm(value):
    return pltpu.with_memory_space_constraint(value, pltpu.HBM)


def hbm():
    return pl.BlockSpec(memory_space=pltpu.HBM)


def project(sources, last, flops, where, weight, turned, pieces, before, earlier=()):
    width, tok = turned.shape
    count = len(sources)
    parts = jax.ShapeDtypeStruct((count, width, width // 2), jnp.bfloat16)
    pieces = [in_hbm(piece) for piece in pieces]
    earlier = [in_hbm(part) for part in earlier]
    shapes = [piece.shape for piece in pieces]
    groups = [part.shape[0] for part in earlier[::2]]
    slots = (sum(groups), width, width // 2)
    out_specs = [whole()] * 3
    out_shape = [jax.ShapeDtypeStruct((tok, width), jnp.bfloat16 if last else jnp.float32), parts, parts]
    scratch = [
        pltpu.SemaphoreType.DMA((count + len(pieces) + 1,)), pltpu.VMEM((width, tok), jnp.bfloat16),
        pltpu.VMEM((count, width, width), jnp.bfloat16),
    ] + [pltpu.VMEM(shape, jnp.bfloat16) for shape in shapes]
    if groups:
        out_specs.append(hbm())
        out_shape.append(pltpu.HBM((8,) + slots[1:], jnp.bfloat16))
        scratch += [pltpu.VMEM(slots, jnp.bfloat16)] * 2 + [pltpu.SemaphoreType.DMA((2 * len(groups) + slots[0],))]
    return pl.pallas_call(
        lambda *refs: project_kernel(sources, shapes, groups, *refs),
        in_specs=[pl.BlockSpec(memory_space=pltpu.SMEM)] + [hbm()] * (2 + len(pieces) + len(earlier)) + [whole()] * len(before),
        out_specs=out_specs,
        scratch_shapes=scratch,
        out_shape=out_shape,
        compiler_params=pltpu.CompilerParams(vmem_limit_bytes=VMEM_BYTES),
        cost_estimate=pl.CostEstimate(flops=flops, bytes_accessed=1 << 20, transcendentals=0),
        name="project",
    )(where, weight, turned, *pieces, *earlier, *before)


def place_kernel(where_ref, mine_ref, come_ref, earlier_ref, out_ref, both, sem):
    both[...] = (mine_ref[...].astype(jnp.float32) + come_ref[...].astype(jnp.float32)).astype(both.dtype)
    copy = pltpu.make_async_copy(both, out_ref.at[pl.ds(where_ref[0], 1)], sem)
    copy.start()
    copy.wait()


def whole():
    return pl.BlockSpec(memory_space=pltpu.VMEM)


def local(queries, keys, values, out_weight, out_grad, doc_ids):
    tok = queries.shape[0]
    heads = queries.shape[1] // HEAD_SIZE
    blocks = tok // ROWS
    span = 2 * tok + ROWS
    shard = lax.axis_index("seq")
    docs = jnp.pad(doc_ids.astype(jnp.bfloat16).reshape(tok // HEAD_SIZE, HEAD_SIZE), ((0, 16 - tok // HEAD_SIZE), (0, 0)))
    own = jnp.concatenate([keys, values, docs], axis=0)
    far, near = shifted(own, "seq", 2), shifted(own, "seq", 1)
    doc_of = lambda part: part[2 * tok : 2 * tok + tok // HEAD_SIZE].reshape(tok).astype(jnp.int32)
    doc_keys = jnp.concatenate([
        jnp.where(shard >= 2, doc_of(far), -1), jnp.where(shard >= 1, doc_of(near), -1), doc_ids
    ])
    earlier = jnp.sum((doc_keys[None, :] < doc_ids[:, None]).astype(jnp.int32), axis=1)
    low = jnp.maximum(earlier, jnp.arange(tok, dtype=jnp.int32) + 1)[:, None]

    all_heads = heads * HEAD_SIZE
    row_block = pl.BlockSpec((ROWS, all_heads), lambda b: (b, 0))
    held = [pltpu.VMEM((3 * tok, HEAD_SIZE), jnp.bfloat16)] * 2
    work = heads * tok * span * HEAD_SIZE * 2
    rows_of = lambda dtype: jax.ShapeDtypeStruct((tok, all_heads), dtype)
    expo, attn, turned, inverse = pl.pallas_call(
        lambda *refs: forward_kernel(tok, span, heads, *refs),
        grid=(blocks,),
        in_specs=[pl.BlockSpec((ROWS, 1), lambda b: (b, 0)), row_block, whole(), whole(), whole()],
        out_specs=[
            pl.BlockSpec((heads, ROWS, span), lambda b: (0, b, 0)), row_block,
            pl.BlockSpec((all_heads, ROWS), lambda b: (0, b)), row_block,
        ],
        out_shape=[
            pltpu.HBM((heads, tok, span), jnp.bfloat16), pltpu.HBM((tok, all_heads), jnp.bfloat16),
            pltpu.HBM((all_heads, tok), jnp.bfloat16), pltpu.HBM((tok, all_heads), jnp.float32),
        ],
        scratch_shapes=held + [pltpu.VMEM((ROWS, span), jnp.float32)],
        compiler_params=pltpu.CompilerParams(vmem_limit_bytes=VMEM_BYTES),
        cost_estimate=pl.CostEstimate(flops=2 * work, bytes_accessed=14 << 20, transcendentals=heads * tok * span),
        name="forward",
    )(low, queries, far, near, own)
    expo, attn, inverse, queries = in_hbm(expo), in_hbm(attn), in_hbm(inverse), in_hbm(queries)

    tensor = lax.axis_index("tensor")
    row, column = tensor // 4, tensor % 4
    at = lambda flip, step: (row ^ flip) * 4 + (column + step) % 4
    core = shard % 2
    places = [at(0, 0), at(0, 3), at(0, 1), at(1, 0), at(0, 2), at(1, 3), at(1, 1), at(1, 2)]
    where = lambda some: jnp.stack([core, *some]).astype(jnp.int32)
    near_up, near_down, opposite = step_x(out_grad, 1), step_x(out_grad, -1), step_x(out_grad, 2)
    across = step_y(lax.optimization_barrier((out_grad, far, near))[0])
    across, turned = lax.optimization_barrier((across, turned))
    across_up, across_down = step_x(across, 1), step_x(across, -1)
    weight, turned = in_hbm(out_weight), in_hbm(turned)
    real = lambda count: 4 * count * tok * all_heads * all_heads
    last = step_y(opposite)
    total, mine_a, other_a = project(
        [((p, 0, 0, tok),) for p in range(4)], False, real(4),
        where(places[:4]), weight, turned, (out_grad, near_up, near_down, across), (),
    )
    come_a = step_core(other_a)
    total, mine_b, other_b = project(
        [((p, 0, 0, tok),) for p in range(3)], False, real(3),
        where(places[4:7]), weight, turned, (opposite, across_up, across_down), (total,),
    )
    come_b = step_core(other_b)
    attention_gradient, mine_c, other_c, placed = project(
        [((0, 0, 0, tok),)], True, 1 << 20, where(places[7:] + places[:7]), weight, turned, (last,), (total,),
        (mine_a, come_a, mine_b, come_b),
    )
    come_c = step_core(other_c)
    placed = pl.pallas_call(
        place_kernel,
        in_specs=[pl.BlockSpec(memory_space=pltpu.SMEM), whole(), whole(), hbm()],
        out_specs=hbm(),
        out_shape=pltpu.HBM(placed.shape, placed.dtype),
        input_output_aliases={3: 0},
        scratch_shapes=[pltpu.VMEM(mine_c.shape, mine_c.dtype), pltpu.SemaphoreType.DMA(())],
        compiler_params=pltpu.CompilerParams(vmem_limit_bytes=VMEM_BYTES),
        cost_estimate=pl.CostEstimate(flops=1 << 20, bytes_accessed=1 << 20, transcendentals=0),
        name="place",
    )(jnp.stack(places[7:]).astype(jnp.int32), mine_c, come_c, placed)
    placed, attention_gradient = lax.optimization_barrier((placed, attention_gradient))
    groups = [[2 * chip + c for chip in range(8)] for c in range(2)]
    arrived = lax.all_to_all(placed, "seq", 0, 0, axis_index_groups=groups)
    weight_grad = jnp.sum(arrived.astype(jnp.float32), axis=0).astype(jnp.bfloat16)

    pair = lambda dtype: jax.ShapeDtypeStruct((2 * tok, HEAD_SIZE), dtype)
    sums = lambda width: [pltpu.VMEM((width, HEAD_SIZE), jnp.bfloat16)] * 2 + [pltpu.VMEM((HEAD_SIZE, width), jnp.float32)] * 2
    past_queries, far_sum, near_sum = pl.pallas_call(
        lambda *refs: backward_past_kernel(tok, heads, *refs),
        grid=(blocks,),
        in_specs=[row_block] * 4 + [pl.BlockSpec((heads, ROWS, 2 * tok), lambda b: (0, b, 0)), whole(), whole()],
        out_specs=[row_block, whole(), whole()],
        out_shape=[rows_of(jnp.float32), pair(jnp.bfloat16), pair(jnp.bfloat16)],
        scratch_shapes=sums(2 * tok),
        compiler_params=pltpu.CompilerParams(vmem_limit_bytes=VMEM_BYTES),
        cost_estimate=pl.CostEstimate(flops=1 << 20, bytes_accessed=1 << 20, transcendentals=0),
        name="backward_past",
    )(queries, attention_gradient, attn, inverse, expo, far, near)
    far_come, near_come = shifted(far_sum, "seq", -2), shifted(near_sum, "seq", -1)
    last_blocks = [pl.BlockSpec((heads, ROWS, ROWS), lambda b, i=i: (0, b, span // ROWS - blocks + i)) for i in range(blocks)]
    grad_queries, own_sum = pl.pallas_call(
        lambda *refs: backward_own_kernel(tok, heads, *refs),
        grid=(blocks,),
        in_specs=[row_block] * 4 + last_blocks + [whole(), row_block],
        out_specs=[row_block, whole()],
        out_shape=[rows_of(jnp.bfloat16), pair(jnp.float32)],
        scratch_shapes=sums(tok),
        compiler_params=pltpu.CompilerParams(vmem_limit_bytes=VMEM_BYTES),
        cost_estimate=pl.CostEstimate(flops=1 << 20, bytes_accessed=1 << 20, transcendentals=0),
        name="backward_own",
    )(queries, attention_gradient, attn, inverse, *([expo] * blocks), own, past_queries)
    own_sum, weight_grad = lax.optimization_barrier((own_sum, weight_grad))
    total = own_sum + near_come.astype(jnp.float32) + far_come.astype(jnp.float32)
    total = total.astype(jnp.bfloat16)
    return (grad_queries, total[:tok], total[tok:], weight_grad)


def solution(mesh):
    placed = (
        P("seq", "tensor"),
        P("seq", "tensor"),
        P("seq", "tensor"),
        P("tensor", None),
        P("seq", "tensor"),
        P("seq"),
    )
    return jax.shard_map(
        local,
        mesh=mesh,
        in_specs=placed,
        out_specs=(P("seq", "tensor"), P("seq", "tensor"), P("seq", "tensor"), P("tensor", "seq")),
        check_vma=False,
    )
```

```python
import math

import jax
import jax.numpy as jnp
from jax import lax
from jax.experimental import pallas as pl
from jax.experimental.pallas import tpu as pltpu
from jax.sharding import PartitionSpec as P

HEAD_SIZE = 128
NEG_BIG = -1e30
ROWS = 256
VMEM_BYTES = 20 << 20


def shifted(value, axis, steps):
    count = lax.axis_size(axis)
    initial, last = (max(0, -steps), min(count, count - steps))
    return lax.ppermute(value, axis, [(source, source + steps) for source in range(initial, last)])


def step_x(value, step):
    pairs = [(t, t // 4 * 4 + (t + step) % 4) for t in range(8)]
    return lax.ppermute(value, "tensor", pairs)


def step_y(value):
    return lax.ppermute(value, "tensor", [(t, t ^ 4) for t in range(8)])


def step_core(value):
    return lax.ppermute(value, "seq", [(s, s ^ 1) for s in range(16)])


def contract_rows(left, right):
    return lax.dot_general(
        left, right, (((0,), (0,)), ((), ())), preferred_element_type=jnp.float32
    )


def contract_last(left, right):
    return lax.dot_general(
        left, right, (((1,), (1,)), ((), ())), preferred_element_type=jnp.float32
    )


def gather_keys(parts, key_all, value_all, tok):
    for index, part in enumerate(parts):
        rows = pl.ds(index * tok, tok)
        key_all[rows, :] = part[pl.ds(0, tok), :]
        value_all[rows, :] = part[pl.ds(tok, tok), :]


def forward_kernel(
    tok, span, heads, low_ref, q_ref, far_ref, near_ref, own_ref,
    expo_ref, attn_ref, turned_ref, inverse_ref, key_all, value_all, bias,
):
    @pl.when(pl.program_id(0) == 0)
    def _():
        gather_keys((far_ref, near_ref, own_ref), key_all, value_all, tok)

    begin = pl.multiple_of(pl.program_id(0) * ROWS, ROWS)
    window = pl.ds(begin, span)
    key_at = lax.broadcasted_iota(jnp.int32, (ROWS, span), 1)
    row_at = lax.broadcasted_iota(jnp.int32, (ROWS, 1), 0)
    visible = (key_at >= low_ref[...] - begin) & (key_at <= row_at + 2 * tok)
    bias[...] = jnp.where(visible, 0.0, NEG_BIG)
    for head in range(heads):
        columns = slice(head * HEAD_SIZE, (head + 1) * HEAD_SIZE)
        raw = contract_last(q_ref[:, columns], key_all[window, :]) + bias[...]
        top = jnp.max(raw, axis=1, keepdims=True)
        expo = jnp.exp2((raw - top) * (math.log2(math.e) / math.sqrt(HEAD_SIZE)))
        inverse = 1.0 / jnp.sum(expo, axis=1, keepdims=True)
        expo_low = expo.astype(jnp.bfloat16)
        expo_ref[head] = expo_low
        inverse_ref[:, columns] = jnp.broadcast_to(inverse, (ROWS, HEAD_SIZE))
        attn = jnp.dot(expo_low, value_all[window, :], preferred_element_type=jnp.float32) * inverse
        attn = attn.astype(jnp.bfloat16)
        attn_ref[:, columns] = attn
        turned_ref[columns, :] = attn.T


def backward_rows(heads, width, first, q_ref, grad_ref, attn_ref, inverse_ref, probs_of, keys, values, gq_of, key_sum, value_sum):
    at = slice(first, first + width)
    for head in range(heads):
        columns = slice(head * HEAD_SIZE, (head + 1) * HEAD_SIZE)
        grad = (grad_ref[:, columns].astype(jnp.float32) * inverse_ref[:, columns]).astype(jnp.bfloat16)
        delta = jnp.sum(grad.astype(jnp.float32) * attn_ref[:, columns].astype(jnp.float32), axis=1, keepdims=True)
        d_prob = contract_last(grad, values[at, :])
        probs = probs_of(head)
        d_score = (probs.astype(jnp.float32) * (d_prob - delta)).astype(jnp.bfloat16)
        gq_of(columns, jnp.dot(d_score, keys[at, :], preferred_element_type=jnp.float32))
        key_sum[:, at] += jnp.dot(q_ref[:, columns].T, d_score, preferred_element_type=jnp.float32)
        value_sum[:, at] += jnp.dot(grad.T, probs, preferred_element_type=jnp.float32)


def backward_past_kernel(
    tok, heads, q_ref, grad_ref, attn_ref, inverse_ref, expo_ref, far_ref, near_ref,
    gq_ref, far_out, near_out, key_all, value_all, key_sum, value_sum,
):
    scale = 1.0 / math.sqrt(HEAD_SIZE)

    @pl.when(pl.program_id(0) == 0)
    def _():
        gather_keys((far_ref, near_ref), key_all, value_all, tok)
        key_sum[...] = jnp.zeros_like(key_sum)
        value_sum[...] = jnp.zeros_like(value_sum)

    def put(columns, value):
        gq_ref[:, columns] = value

    for block in range(tok // ROWS):
        @pl.when(pl.program_id(0) == block)
        def _(block=block):
            first = block * ROWS
            width = 2 * tok - first
            backward_rows(
                heads, width, first, q_ref, grad_ref, attn_ref, inverse_ref,
                lambda head: expo_ref[head, :, :width], key_all, value_all, put, key_sum, value_sum,
            )

    @pl.when(pl.program_id(0) == pl.num_programs(0) - 1)
    def _():
        for index, out in enumerate((far_out, near_out)):
            rows = pl.ds(index * tok, tok)
            out[pl.ds(0, tok), :] = (key_sum[:, rows].T * scale).astype(out.dtype)
            out[pl.ds(tok, tok), :] = value_sum[:, rows].T.astype(out.dtype)


def backward_own_kernel(
    tok, heads, q_ref, grad_ref, attn_ref, inverse_ref, expo_a, expo_b, expo_c, own_ref, past_ref,
    gq_ref, own_out, key_all, value_all, key_sum, value_sum,
):
    scale = 1.0 / math.sqrt(HEAD_SIZE)
    blocks = tok // ROWS
    expos = (expo_a, expo_b, expo_c)

    @pl.when(pl.program_id(0) == 0)
    def _():
        gather_keys((own_ref,), key_all, value_all, tok)
        key_sum[...] = jnp.zeros_like(key_sum)
        value_sum[...] = jnp.zeros_like(value_sum)

    def put(columns, value):
        gq_ref[:, columns] = ((past_ref[:, columns] + value) * scale).astype(gq_ref.dtype)

    for block in range(blocks):
        @pl.when(pl.program_id(0) == block)
        def _(block=block):
            width = (block + 1) * ROWS
            probs_of = lambda head: jnp.concatenate([expo[head] for expo in expos[blocks - 1 - block :]], axis=1)
            backward_rows(
                heads, width, 0, q_ref, grad_ref, attn_ref, inverse_ref,
                probs_of, key_all, value_all, put, key_sum, value_sum,
            )

    @pl.when(pl.program_id(0) == pl.num_programs(0) - 1)
    def _():
        own_out[pl.ds(0, tok), :] = key_sum[...].T * scale
        own_out[pl.ds(tok, tok), :] = value_sum[...].T


def project_kernel(sources, shapes, groups, where_ref, weight_ref, turned_ref, *refs):
    count = len(shapes)
    pieces, refs = refs[:count], refs[count:]
    earlier, refs = refs[: 2 * len(groups)], refs[2 * len(groups) :]
    if groups:
        come, placed, placed_sems = refs[-3:]
        refs = refs[:-3]
    sems, turned, weights, *buffers = refs[-3 - count :]
    refs = refs[: -3 - count]
    if groups:
        placed_ref, refs = refs[-1], refs[:-1]
    before, (total_ref, mine_ref, other_ref) = refs[:-3], refs[-3:]
    width = weights.shape[1]
    cut = width // 2
    copies = []

    def fetch(source, target):
        copies.append(pltpu.make_async_copy(source, target, sems.at[len(copies)]))
        copies[-1].start()
        return copies[-1]

    pending = {}
    turned_copy = None
    for index, blocks in enumerate(sources):
        columns = pl.ds(pl.multiple_of(where_ref[1 + index] * width, width), width)
        pending["weight", index] = fetch(weight_ref.at[:, columns], weights.at[index])
        for operand, _, _, _ in blocks:
            if ("piece", operand) not in pending:
                pending["piece", operand] = fetch(pieces[operand], buffers[operand])
        if turned_copy is None:
            turned_copy = fetch(turned_ref, turned)
    pending["turned"] = turned_copy
    at, loads = 0, []
    for i, size in enumerate(groups):
        for j, target in enumerate((placed, come)):
            loads.append(pltpu.make_async_copy(earlier[2 * i + j], target.at[pl.ds(at, size)], placed_sems.at[2 * i + j]))
            loads[-1].start()
        at += size
    done = set()

    def ready(key):
        if key not in done:
            done.add(key)
            pending[key].wait()

    mine = pl.multiple_of(where_ref[0] * cut, cut)
    other = pl.multiple_of((1 - where_ref[0]) * cut, cut)
    total = before[0] if before else total_ref
    for index, blocks in enumerate(sources):
        ready(("weight", index))
        for operand, _, _, _ in blocks:
            ready(("piece", operand))
        weight = weights[index]
        for operand, there, row, rows in blocks:
            term = contract_last(buffers[operand][pl.ds(there, rows), :], weight)
            at = pl.ds(row, rows)
            if before or index:
                term = total[at, :] + term
            total_ref[at, :] = term.astype(total_ref.dtype)
        total = total_ref
        ready("turned")
        for out, begin in ((mine_ref, mine), (other_ref, other)):
            part = None
            for operand, there, row, rows in blocks:
                term = jnp.dot(
                    turned[:, pl.ds(row, rows)],
                    buffers[operand][pl.ds(there, rows), pl.ds(begin, cut)],
                    preferred_element_type=jnp.float32,
                )
                part = term if part is None else part + term
            out[index] = part.astype(out.dtype)
    for load in loads:
        load.wait()
    stores = []
    for index in range(sum(groups)):
        both = placed[index].astype(jnp.float32) + come[index].astype(jnp.float32)
        placed[index] = both.astype(placed.dtype)
        place = where_ref[1 + len(sources) + index]
        stores.append(pltpu.make_async_copy(placed.at[index], placed_ref.at[place], placed_sems.at[2 * len(groups) + index]))
        stores[-1].start()
    for store in stores:
        store.wait()


def in_hbm(value):
    return pltpu.with_memory_space_constraint(value, pltpu.HBM)


def hbm():
    return pl.BlockSpec(memory_space=pltpu.HBM)


def project(sources, last, flops, where, weight, turned, pieces, before, earlier=()):
    width, tok = turned.shape
    count = len(sources)
    parts = jax.ShapeDtypeStruct((count, width, width // 2), jnp.bfloat16)
    pieces = [in_hbm(piece) for piece in pieces]
    earlier = [in_hbm(part) for part in earlier]
    shapes = [piece.shape for piece in pieces]
    groups = [part.shape[0] for part in earlier[::2]]
    slots = (sum(groups), width, width // 2)
    out_specs = [whole()] * 3
    out_shape = [jax.ShapeDtypeStruct((tok, width), jnp.bfloat16 if last else jnp.float32), parts, parts]
    scratch = [
        pltpu.SemaphoreType.DMA((count + len(pieces) + 1,)), pltpu.VMEM((width, tok), jnp.bfloat16),
        pltpu.VMEM((count, width, width), jnp.bfloat16),
    ] + [pltpu.VMEM(shape, jnp.bfloat16) for shape in shapes]
    if groups:
        out_specs.append(hbm())
        out_shape.append(pltpu.HBM((8,) + slots[1:], jnp.bfloat16))
        scratch += [pltpu.VMEM(slots, jnp.bfloat16)] * 2 + [pltpu.SemaphoreType.DMA((2 * len(groups) + slots[0],))]
    return pl.pallas_call(
        lambda *refs: project_kernel(sources, shapes, groups, *refs),
        in_specs=[pl.BlockSpec(memory_space=pltpu.SMEM)] + [hbm()] * (2 + len(pieces) + len(earlier)) + [whole()] * len(before),
        out_specs=out_specs,
        scratch_shapes=scratch,
        out_shape=out_shape,
        compiler_params=pltpu.CompilerParams(vmem_limit_bytes=VMEM_BYTES),
        cost_estimate=pl.CostEstimate(flops=flops, bytes_accessed=1 << 20, transcendentals=0),
        name="project",
    )(where, weight, turned, *pieces, *earlier, *before)


def place_kernel(where_ref, mine_ref, come_ref, earlier_ref, out_ref, both, sems):
    copies = []
    for index in range(both.shape[0]):
        both[index] = (mine_ref[index].astype(jnp.float32) + come_ref[index].astype(jnp.float32)).astype(both.dtype)
        copies.append(pltpu.make_async_copy(both.at[index], out_ref.at[where_ref[index]], sems.at[index]))
        copies[-1].start()
    for copy in copies:
        copy.wait()


def whole():
    return pl.BlockSpec(memory_space=pltpu.VMEM)


def local(queries, keys, values, out_weight, out_grad, doc_ids):
    tok = queries.shape[0]
    heads = queries.shape[1] // HEAD_SIZE
    blocks = tok // ROWS
    span = 2 * tok + ROWS
    shard = lax.axis_index("seq")
    docs = jnp.pad(doc_ids.astype(jnp.bfloat16).reshape(tok // HEAD_SIZE, HEAD_SIZE), ((0, 16 - tok // HEAD_SIZE), (0, 0)))
    own = jnp.concatenate([keys, values, docs], axis=0)
    far, near = shifted(own, "seq", 2), shifted(own, "seq", 1)
    doc_of = lambda part: part[2 * tok : 2 * tok + tok // HEAD_SIZE].reshape(tok).astype(jnp.int32)
    doc_keys = jnp.concatenate([
        jnp.where(shard >= 2, doc_of(far), -1), jnp.where(shard >= 1, doc_of(near), -1), doc_ids
    ])
    earlier = jnp.sum((doc_keys[None, :] < doc_ids[:, None]).astype(jnp.int32), axis=1)
    low = jnp.maximum(earlier, jnp.arange(tok, dtype=jnp.int32) + 1)[:, None]

    all_heads = heads * HEAD_SIZE
    row_block = pl.BlockSpec((ROWS, all_heads), lambda b: (b, 0))
    held = [pltpu.VMEM((3 * tok, HEAD_SIZE), jnp.bfloat16)] * 2
    work = heads * tok * span * HEAD_SIZE * 2
    rows_of = lambda dtype: jax.ShapeDtypeStruct((tok, all_heads), dtype)
    expo, attn, turned, inverse = pl.pallas_call(
        lambda *refs: forward_kernel(tok, span, heads, *refs),
        grid=(blocks,),
        in_specs=[pl.BlockSpec((ROWS, 1), lambda b: (b, 0)), row_block, whole(), whole(), whole()],
        out_specs=[
            pl.BlockSpec((heads, ROWS, span), lambda b: (0, b, 0)), row_block,
            pl.BlockSpec((all_heads, ROWS), lambda b: (0, b)), row_block,
        ],
        out_shape=[
            pltpu.HBM((heads, tok, span), jnp.bfloat16), pltpu.HBM((tok, all_heads), jnp.bfloat16),
            pltpu.HBM((all_heads, tok), jnp.bfloat16), pltpu.HBM((tok, all_heads), jnp.float32),
        ],
        scratch_shapes=held + [pltpu.VMEM((ROWS, span), jnp.float32)],
        compiler_params=pltpu.CompilerParams(vmem_limit_bytes=VMEM_BYTES),
        cost_estimate=pl.CostEstimate(flops=2 * work, bytes_accessed=14 << 20, transcendentals=heads * tok * span),
        name="forward",
    )(low, queries, far, near, own)
    expo, attn, inverse, queries = in_hbm(expo), in_hbm(attn), in_hbm(inverse), in_hbm(queries)

    tensor = lax.axis_index("tensor")
    row, column = tensor // 4, tensor % 4
    at = lambda flip, step: (row ^ flip) * 4 + (column + step) % 4
    core = shard % 2
    places = [at(0, 0), at(0, 2), at(1, 0), at(0, 3), at(0, 1), at(1, 2), at(1, 3), at(1, 1)]
    where = lambda some: jnp.stack([core, *some]).astype(jnp.int32)
    opposite = step_x(out_grad, 2)
    later = lax.optimization_barrier((out_grad, far, near))[0]
    across, near_up, near_down = step_y(later), step_x(later, 1), step_x(later, -1)
    across, opposite, turned = lax.optimization_barrier((across, opposite, turned))
    across_up, across_down = step_x(across, 1), step_x(across, -1)
    weight, turned = in_hbm(out_weight), in_hbm(turned)
    real = lambda count: 4 * count * tok * all_heads * all_heads
    last = step_y(opposite)
    total, mine_a, other_a = project(
        [((p, 0, 0, tok),) for p in range(3)], False, real(3),
        where(places[:3]), weight, turned, (out_grad, opposite, across), (),
    )
    come_a = step_core(other_a)
    total, mine_b, other_b = project(
        [((p, 0, 0, tok),) for p in range(3)], False, real(3),
        where(places[3:6]), weight, turned, (near_up, near_down, last), (total,),
    )
    come_b = step_core(other_b)
    attention_gradient, mine_c, other_c, placed = project(
        [((p, 0, 0, tok),) for p in range(2)], True, 1 << 20, where(places[6:] + places[:6]), weight, turned,
        (across_up, across_down), (total,), (mine_a, come_a, mine_b, come_b),
    )
    come_c = step_core(other_c)
    placed = pl.pallas_call(
        place_kernel,
        in_specs=[pl.BlockSpec(memory_space=pltpu.SMEM), whole(), whole(), hbm()],
        out_specs=hbm(),
        out_shape=pltpu.HBM(placed.shape, placed.dtype),
        input_output_aliases={3: 0},
        scratch_shapes=[pltpu.VMEM(mine_c.shape, mine_c.dtype), pltpu.SemaphoreType.DMA((mine_c.shape[0],))],
        compiler_params=pltpu.CompilerParams(vmem_limit_bytes=VMEM_BYTES),
        cost_estimate=pl.CostEstimate(flops=1 << 20, bytes_accessed=1 << 20, transcendentals=0),
        name="place",
    )(jnp.stack(places[6:]).astype(jnp.int32), mine_c, come_c, placed)
    placed, attention_gradient = lax.optimization_barrier((placed, attention_gradient))
    groups = [[2 * chip + c for chip in range(8)] for c in range(2)]
    arrived = lax.all_to_all(placed, "seq", 0, 0, axis_index_groups=groups)
    weight_grad = jnp.sum(arrived.astype(jnp.float32), axis=0).astype(jnp.bfloat16)

    pair = lambda dtype: jax.ShapeDtypeStruct((2 * tok, HEAD_SIZE), dtype)
    sums = lambda width: [pltpu.VMEM((width, HEAD_SIZE), jnp.bfloat16)] * 2 + [pltpu.VMEM((HEAD_SIZE, width), jnp.float32)] * 2
    past_queries, far_sum, near_sum = pl.pallas_call(
        lambda *refs: backward_past_kernel(tok, heads, *refs),
        grid=(blocks,),
        in_specs=[row_block] * 4 + [pl.BlockSpec((heads, ROWS, 2 * tok), lambda b: (0, b, 0)), whole(), whole()],
        out_specs=[row_block, whole(), whole()],
        out_shape=[rows_of(jnp.float32), pair(jnp.bfloat16), pair(jnp.bfloat16)],
        scratch_shapes=sums(2 * tok),
        compiler_params=pltpu.CompilerParams(vmem_limit_bytes=VMEM_BYTES),
        cost_estimate=pl.CostEstimate(flops=1 << 20, bytes_accessed=1 << 20, transcendentals=0),
        name="backward_past",
    )(queries, attention_gradient, attn, inverse, expo, far, near)
    crossed = step_core(near_sum)
    sent = far_sum.astype(jnp.float32) + jnp.where(core == 1, crossed, 0).astype(jnp.float32)
    come = shifted(sent.astype(jnp.bfloat16), "seq", -2)
    last_blocks = [pl.BlockSpec((heads, ROWS, ROWS), lambda b, i=i: (0, b, span // ROWS - blocks + i)) for i in range(blocks)]
    grad_queries, own_sum = pl.pallas_call(
        lambda *refs: backward_own_kernel(tok, heads, *refs),
        grid=(blocks,),
        in_specs=[row_block] * 4 + last_blocks + [whole(), row_block],
        out_specs=[row_block, whole()],
        out_shape=[rows_of(jnp.bfloat16), pair(jnp.float32)],
        scratch_shapes=sums(tok),
        compiler_params=pltpu.CompilerParams(vmem_limit_bytes=VMEM_BYTES),
        cost_estimate=pl.CostEstimate(flops=1 << 20, bytes_accessed=1 << 20, transcendentals=0),
        name="backward_own",
    )(queries, attention_gradient, attn, inverse, *([expo] * blocks), own, past_queries)
    own_sum, weight_grad = lax.optimization_barrier((own_sum, weight_grad))
    total = own_sum + jnp.where(core == 0, crossed, 0).astype(jnp.float32) + come.astype(jnp.float32)
    total = total.astype(jnp.bfloat16)
    return (grad_queries, total[:tok], total[tok:], weight_grad)


def solution(mesh):
    placed = (
        P("seq", "tensor"),
        P("seq", "tensor"),
        P("seq", "tensor"),
        P("tensor", None),
        P("seq", "tensor"),
        P("seq"),
    )
    return jax.shard_map(
        local,
        mesh=mesh,
        in_specs=placed,
        out_specs=(P("seq", "tensor"), P("seq", "tensor"), P("seq", "tensor"), P("tensor", "seq")),
        check_vma=False,
    )
```

```python
import math

import jax
import jax.numpy as jnp
from jax import lax
from jax.experimental import pallas as pl
from jax.experimental.pallas import tpu as pltpu
from jax.sharding import PartitionSpec as P

HEAD_SIZE = 128
NEG_BIG = -1e30
ROWS = 256
VMEM_BYTES = 20 << 20


def shifted(value, axis, steps):
    count = lax.axis_size(axis)
    initial, last = (max(0, -steps), min(count, count - steps))
    return lax.ppermute(value, axis, [(source, source + steps) for source in range(initial, last)])


def step_x(value, step):
    pairs = [(t, t // 4 * 4 + (t + step) % 4) for t in range(8)]
    return lax.ppermute(value, "tensor", pairs)


def step_y(value):
    return lax.ppermute(value, "tensor", [(t, t ^ 4) for t in range(8)])


def step_core(value):
    return lax.ppermute(value, "seq", [(s, s ^ 1) for s in range(16)])


def contract_rows(left, right):
    return lax.dot_general(
        left, right, (((0,), (0,)), ((), ())), preferred_element_type=jnp.float32
    )


def contract_last(left, right):
    return lax.dot_general(
        left, right, (((1,), (1,)), ((), ())), preferred_element_type=jnp.float32
    )


def gather_keys(parts, key_all, value_all, tok):
    for index, part in enumerate(parts):
        rows = pl.ds(index * tok, tok)
        key_all[rows, :] = part[pl.ds(0, tok), :]
        value_all[rows, :] = part[pl.ds(tok, tok), :]


def forward_kernel(
    tok, span, heads, low_ref, q_ref, far_ref, near_ref, own_ref,
    expo_ref, attn_ref, turned_ref, inverse_ref, key_all, value_all, bias,
):
    @pl.when(pl.program_id(0) == 0)
    def _():
        gather_keys((far_ref, near_ref, own_ref), key_all, value_all, tok)

    begin = pl.multiple_of(pl.program_id(0) * ROWS, ROWS)
    window = pl.ds(begin, span)
    key_at = lax.broadcasted_iota(jnp.int32, (ROWS, span), 1)
    row_at = lax.broadcasted_iota(jnp.int32, (ROWS, 1), 0)
    visible = (key_at >= low_ref[...] - begin) & (key_at <= row_at + 2 * tok)
    bias[...] = jnp.where(visible, 0.0, NEG_BIG)
    for head in range(heads):
        columns = slice(head * HEAD_SIZE, (head + 1) * HEAD_SIZE)
        raw = contract_last(q_ref[:, columns], key_all[window, :]) + bias[...]
        top = jnp.max(raw, axis=1, keepdims=True)
        expo = jnp.exp2((raw - top) * (math.log2(math.e) / math.sqrt(HEAD_SIZE)))
        inverse = 1.0 / jnp.sum(expo, axis=1, keepdims=True)
        expo_low = expo.astype(jnp.bfloat16)
        expo_ref[head] = expo_low
        inverse_ref[:, columns] = jnp.broadcast_to(inverse, (ROWS, HEAD_SIZE))
        attn = jnp.dot(expo_low, value_all[window, :], preferred_element_type=jnp.float32) * inverse
        attn = attn.astype(jnp.bfloat16)
        attn_ref[:, columns] = attn
        turned_ref[columns, :] = attn.T


def backward_rows(heads, width, first, q_ref, grad_ref, attn_ref, inverse_ref, probs_of, keys, values, gq_of, key_sum, value_sum):
    at = slice(first, first + width)
    for head in range(heads):
        columns = slice(head * HEAD_SIZE, (head + 1) * HEAD_SIZE)
        grad = (grad_ref[:, columns].astype(jnp.float32) * inverse_ref[:, columns]).astype(jnp.bfloat16)
        delta = jnp.sum(grad.astype(jnp.float32) * attn_ref[:, columns].astype(jnp.float32), axis=1, keepdims=True)
        d_prob = contract_last(grad, values[at, :])
        probs = probs_of(head)
        d_score = (probs.astype(jnp.float32) * (d_prob - delta)).astype(jnp.bfloat16)
        gq_of(columns, jnp.dot(d_score, keys[at, :], preferred_element_type=jnp.float32))
        key_sum[:, at] += jnp.dot(q_ref[:, columns].T, d_score, preferred_element_type=jnp.float32)
        value_sum[:, at] += jnp.dot(grad.T, probs, preferred_element_type=jnp.float32)


def backward_past_kernel(
    tok, heads, q_ref, grad_ref, attn_ref, inverse_ref, expo_ref, far_ref, near_ref,
    gq_ref, far_out, near_out, key_all, value_all, key_sum, value_sum,
):
    scale = 1.0 / math.sqrt(HEAD_SIZE)

    @pl.when(pl.program_id(0) == 0)
    def _():
        gather_keys((far_ref, near_ref), key_all, value_all, tok)
        key_sum[...] = jnp.zeros_like(key_sum)
        value_sum[...] = jnp.zeros_like(value_sum)

    def put(columns, value):
        gq_ref[:, columns] = value

    for block in range(tok // ROWS):
        @pl.when(pl.program_id(0) == block)
        def _(block=block):
            first = block * ROWS
            width = 2 * tok - first
            backward_rows(
                heads, width, first, q_ref, grad_ref, attn_ref, inverse_ref,
                lambda head: expo_ref[head, :, :width], key_all, value_all, put, key_sum, value_sum,
            )

    @pl.when(pl.program_id(0) == pl.num_programs(0) - 1)
    def _():
        for index, out in enumerate((far_out, near_out)):
            rows = pl.ds(index * tok, tok)
            out[pl.ds(0, tok), :] = (key_sum[:, rows].T * scale).astype(out.dtype)
            out[pl.ds(tok, tok), :] = value_sum[:, rows].T.astype(out.dtype)


def backward_own_kernel(
    tok, heads, q_ref, grad_ref, attn_ref, inverse_ref, expo_a, expo_b, expo_c, own_ref, past_ref,
    gq_ref, own_out, key_all, value_all, key_sum, value_sum,
):
    scale = 1.0 / math.sqrt(HEAD_SIZE)
    blocks = tok // ROWS
    expos = (expo_a, expo_b, expo_c)

    @pl.when(pl.program_id(0) == 0)
    def _():
        gather_keys((own_ref,), key_all, value_all, tok)
        key_sum[...] = jnp.zeros_like(key_sum)
        value_sum[...] = jnp.zeros_like(value_sum)

    def put(columns, value):
        gq_ref[:, columns] = ((past_ref[:, columns] + value) * scale).astype(gq_ref.dtype)

    for block in range(blocks):
        @pl.when(pl.program_id(0) == block)
        def _(block=block):
            width = (block + 1) * ROWS
            probs_of = lambda head: jnp.concatenate([expo[head] for expo in expos[blocks - 1 - block :]], axis=1)
            backward_rows(
                heads, width, 0, q_ref, grad_ref, attn_ref, inverse_ref,
                probs_of, key_all, value_all, put, key_sum, value_sum,
            )

    @pl.when(pl.program_id(0) == pl.num_programs(0) - 1)
    def _():
        own_out[pl.ds(0, tok), :] = key_sum[...].T * scale
        own_out[pl.ds(tok, tok), :] = value_sum[...].T


def project_kernel(sources, shapes, groups, where_ref, weight_ref, turned_ref, *refs):
    count = len(shapes)
    pieces, refs = refs[:count], refs[count:]
    earlier, refs = refs[: 2 * len(groups)], refs[2 * len(groups) :]
    if groups:
        come, placed, placed_sems = refs[-3:]
        refs = refs[:-3]
    sems, turned, weights, *buffers = refs[-3 - count :]
    refs = refs[: -3 - count]
    if groups:
        placed_ref, refs = refs[-1], refs[:-1]
    before, (total_ref, mine_ref, other_ref) = refs[:-3], refs[-3:]
    width = weights.shape[1]
    cut = width // 2
    copies = []

    def fetch(source, target):
        copies.append(pltpu.make_async_copy(source, target, sems.at[len(copies)]))
        copies[-1].start()
        return copies[-1]

    pending = {}
    turned_copy = None
    for index, blocks in enumerate(sources):
        columns = pl.ds(pl.multiple_of(where_ref[1 + index] * width, width), width)
        pending["weight", index] = fetch(weight_ref.at[:, columns], weights.at[index])
        for operand, _, _, _ in blocks:
            if ("piece", operand) not in pending:
                pending["piece", operand] = fetch(pieces[operand], buffers[operand])
        if turned_copy is None:
            turned_copy = fetch(turned_ref, turned)
    pending["turned"] = turned_copy
    at, loads = 0, []
    for i, size in enumerate(groups):
        for j, target in enumerate((placed, come)):
            loads.append(pltpu.make_async_copy(earlier[2 * i + j], target.at[pl.ds(at, size)], placed_sems.at[2 * i + j]))
            loads[-1].start()
        at += size
    done = set()

    def ready(key):
        if key not in done:
            done.add(key)
            pending[key].wait()

    mine = pl.multiple_of(where_ref[0] * cut, cut)
    other = pl.multiple_of((1 - where_ref[0]) * cut, cut)
    total = before[0] if before else total_ref
    for index, blocks in enumerate(sources):
        ready(("weight", index))
        for operand, _, _, _ in blocks:
            ready(("piece", operand))
        weight = weights[index]
        for operand, there, row, rows in blocks:
            term = contract_last(buffers[operand][pl.ds(there, rows), :], weight)
            at = pl.ds(row, rows)
            if before or index:
                term = total[at, :] + term
            total_ref[at, :] = term.astype(total_ref.dtype)
        total = total_ref
        ready("turned")
        for out, begin in ((mine_ref, mine), (other_ref, other)):
            part = None
            for operand, there, row, rows in blocks:
                term = jnp.dot(
                    turned[:, pl.ds(row, rows)],
                    buffers[operand][pl.ds(there, rows), pl.ds(begin, cut)],
                    preferred_element_type=jnp.float32,
                )
                part = term if part is None else part + term
            out[index] = part.astype(out.dtype)
    for load in loads:
        load.wait()
    stores = []
    for index in range(sum(groups)):
        both = placed[index].astype(jnp.float32) + come[index].astype(jnp.float32)
        placed[index] = both.astype(placed.dtype)
        place = where_ref[1 + len(sources) + index]
        stores.append(pltpu.make_async_copy(placed.at[index], placed_ref.at[place], placed_sems.at[2 * len(groups) + index]))
        stores[-1].start()
    for store in stores:
        store.wait()


def in_hbm(value):
    return pltpu.with_memory_space_constraint(value, pltpu.HBM)


def hbm():
    return pl.BlockSpec(memory_space=pltpu.HBM)


def project(sources, last, flops, where, weight, turned, pieces, before, earlier=()):
    width, tok = turned.shape
    count = len(sources)
    parts = jax.ShapeDtypeStruct((count, width, width // 2), jnp.bfloat16)
    pieces = [in_hbm(piece) for piece in pieces]
    earlier = [in_hbm(part) for part in earlier]
    shapes = [piece.shape for piece in pieces]
    groups = [part.shape[0] for part in earlier[::2]]
    slots = (sum(groups), width, width // 2)
    out_specs = [whole()] * 3
    out_shape = [jax.ShapeDtypeStruct((tok, width), jnp.bfloat16 if last else jnp.float32), parts, parts]
    scratch = [
        pltpu.SemaphoreType.DMA((count + len(pieces) + 1,)), pltpu.VMEM((width, tok), jnp.bfloat16),
        pltpu.VMEM((count, width, width), jnp.bfloat16),
    ] + [pltpu.VMEM(shape, jnp.bfloat16) for shape in shapes]
    if groups:
        out_specs.append(hbm())
        out_shape.append(pltpu.HBM((8,) + slots[1:], jnp.bfloat16))
        scratch += [pltpu.VMEM(slots, jnp.bfloat16)] * 2 + [pltpu.SemaphoreType.DMA((2 * len(groups) + slots[0],))]
    return pl.pallas_call(
        lambda *refs: project_kernel(sources, shapes, groups, *refs),
        in_specs=[pl.BlockSpec(memory_space=pltpu.SMEM)] + [hbm()] * (2 + len(pieces) + len(earlier)) + [whole()] * len(before),
        out_specs=out_specs,
        scratch_shapes=scratch,
        out_shape=out_shape,
        compiler_params=pltpu.CompilerParams(vmem_limit_bytes=VMEM_BYTES),
        cost_estimate=pl.CostEstimate(flops=flops, bytes_accessed=1 << 20, transcendentals=0),
        name="project",
    )(where, weight, turned, *pieces, *earlier, *before)


def place_kernel(where_ref, mine_ref, come_ref, last_mine_ref, last_come_ref, earlier_ref, out_ref, both, sems):
    copies, slot = [], 0
    for mine, come in ((last_mine_ref, last_come_ref), (mine_ref, come_ref)):
        for index in range(mine.shape[0]):
            both[slot] = (mine[index].astype(jnp.float32) + come[index].astype(jnp.float32)).astype(both.dtype)
            place = where_ref[index if mine is mine_ref else mine_ref.shape[0]]
            copies.append(pltpu.make_async_copy(both.at[slot], out_ref.at[place], sems.at[slot]))
            copies[-1].start()
            slot += 1
    for copy in copies:
        copy.wait()


def send_kernel(core_ref, far_ref, crossed_ref, out_ref):
    crossed = jnp.where(core_ref[0] == 1, crossed_ref[...].astype(jnp.float32), 0.0)
    out_ref[...] = (far_ref[...].astype(jnp.float32) + crossed).astype(out_ref.dtype)


def finish_kernel(core_ref, own_ref, crossed_ref, come_ref, key_ref, value_ref):
    tok = key_ref.shape[0]
    for index, out in enumerate((key_ref, value_ref)):
        rows = pl.ds(index * tok, tok)
        crossed = jnp.where(core_ref[0] == 0, crossed_ref[rows, :].astype(jnp.float32), 0.0)
        out[...] = (own_ref[rows, :] + crossed + come_ref[rows, :].astype(jnp.float32)).astype(out.dtype)


def on_core(kernel, name, out_shape, core, *operands):
    return pl.pallas_call(
        kernel,
        in_specs=[pl.BlockSpec(memory_space=pltpu.SMEM)] + [whole()] * len(operands),
        out_specs=[whole()] * len(out_shape),
        out_shape=out_shape,
        compiler_params=pltpu.CompilerParams(vmem_limit_bytes=VMEM_BYTES // 2),
        cost_estimate=pl.CostEstimate(flops=1 << 20, bytes_accessed=1 << 20, transcendentals=0),
        name=name,
    )(core[None].astype(jnp.int32), *operands)


def whole():
    return pl.BlockSpec(memory_space=pltpu.VMEM)


def local(queries, keys, values, out_weight, out_grad, doc_ids):
    tok = queries.shape[0]
    heads = queries.shape[1] // HEAD_SIZE
    blocks = tok // ROWS
    span = 2 * tok + ROWS
    shard = lax.axis_index("seq")
    docs = jnp.pad(doc_ids.astype(jnp.bfloat16).reshape(tok // HEAD_SIZE, HEAD_SIZE), ((0, 16 - tok // HEAD_SIZE), (0, 0)))
    own = jnp.concatenate([keys, values, docs], axis=0)
    far, near = shifted(own, "seq", 2), shifted(own, "seq", 1)
    doc_of = lambda part: part[2 * tok : 2 * tok + tok // HEAD_SIZE].reshape(tok).astype(jnp.int32)
    doc_keys = jnp.concatenate([
        jnp.where(shard >= 2, doc_of(far), -1), jnp.where(shard >= 1, doc_of(near), -1), doc_ids
    ])
    earlier = jnp.sum((doc_keys[None, :] < doc_ids[:, None]).astype(jnp.int32), axis=1)
    low = jnp.maximum(earlier, jnp.arange(tok, dtype=jnp.int32) + 1)[:, None]

    all_heads = heads * HEAD_SIZE
    row_block = pl.BlockSpec((ROWS, all_heads), lambda b: (b, 0))
    held = [pltpu.VMEM((3 * tok, HEAD_SIZE), jnp.bfloat16)] * 2
    work = heads * tok * span * HEAD_SIZE * 2
    rows_of = lambda dtype: jax.ShapeDtypeStruct((tok, all_heads), dtype)
    expo, attn, turned, inverse = pl.pallas_call(
        lambda *refs: forward_kernel(tok, span, heads, *refs),
        grid=(blocks,),
        in_specs=[pl.BlockSpec((ROWS, 1), lambda b: (b, 0)), row_block, whole(), whole(), whole()],
        out_specs=[
            pl.BlockSpec((heads, ROWS, span), lambda b: (0, b, 0)), row_block,
            pl.BlockSpec((all_heads, ROWS), lambda b: (0, b)), row_block,
        ],
        out_shape=[
            pltpu.HBM((heads, tok, span), jnp.bfloat16), pltpu.HBM((tok, all_heads), jnp.bfloat16),
            pltpu.HBM((all_heads, tok), jnp.bfloat16), pltpu.HBM((tok, all_heads), jnp.float32),
        ],
        scratch_shapes=held + [pltpu.VMEM((ROWS, span), jnp.float32)],
        compiler_params=pltpu.CompilerParams(vmem_limit_bytes=VMEM_BYTES),
        cost_estimate=pl.CostEstimate(flops=2 * work, bytes_accessed=14 << 20, transcendentals=heads * tok * span),
        name="forward",
    )(low, queries, far, near, own)
    expo, attn, inverse, queries = in_hbm(expo), in_hbm(attn), in_hbm(inverse), in_hbm(queries)

    tensor = lax.axis_index("tensor")
    row, column = tensor // 4, tensor % 4
    at = lambda flip, step: (row ^ flip) * 4 + (column + step) % 4
    core = shard % 2
    places = [at(0, 0), at(0, 2), at(1, 0), at(0, 3), at(0, 1), at(1, 3), at(1, 1), at(1, 2)]
    where = lambda some: jnp.stack([core, *some]).astype(jnp.int32)
    opposite = step_x(out_grad, 2)
    later = lax.optimization_barrier((out_grad, far, near))[0]
    across, near_up, near_down = step_y(later), step_x(later, 1), step_x(later, -1)
    across, opposite, turned = lax.optimization_barrier((across, opposite, turned))
    across_up, across_down = step_x(across, 1), step_x(across, -1)
    weight, turned = in_hbm(out_weight), in_hbm(turned)
    real = lambda count: 4 * count * tok * all_heads * all_heads
    last = step_y(opposite)
    total, mine_a, other_a = project(
        [((p, 0, 0, tok),) for p in range(3)], False, real(3),
        where(places[:3]), weight, turned, (out_grad, opposite, across), (),
    )
    come_a = step_core(other_a)
    total, mine_b, other_b = project(
        [((p, 0, 0, tok),) for p in range(2)], False, real(2),
        where(places[3:5]), weight, turned, (near_up, near_down), (total,),
    )
    come_b = step_core(other_b)
    total, mine_d, other_d = project(
        [((0, 0, 0, tok),)], False, real(1), where(places[7:]), weight, turned, (last,), (total,),
    )
    come_d = step_core(other_d)
    attention_gradient, mine_c, other_c, placed = project(
        [((p, 0, 0, tok),) for p in range(2)], True, 1 << 20, where(places[5:7] + places[:5]), weight, turned,
        (across_up, across_down), (total,), (mine_a, come_a, mine_b, come_b),
    )
    come_c = step_core(other_c)
    placed = pl.pallas_call(
        place_kernel,
        in_specs=[pl.BlockSpec(memory_space=pltpu.SMEM)] + [whole()] * 4 + [hbm()],
        out_specs=hbm(),
        out_shape=pltpu.HBM(placed.shape, placed.dtype),
        input_output_aliases={5: 0},
        scratch_shapes=[pltpu.VMEM((3,) + mine_c.shape[1:], mine_c.dtype), pltpu.SemaphoreType.DMA((3,))],
        compiler_params=pltpu.CompilerParams(vmem_limit_bytes=VMEM_BYTES),
        cost_estimate=pl.CostEstimate(flops=1 << 20, bytes_accessed=1 << 20, transcendentals=0),
        name="place",
    )(jnp.stack(places[5:]).astype(jnp.int32), mine_c, come_c, mine_d, come_d, placed)
    placed, attention_gradient = lax.optimization_barrier((placed, attention_gradient))
    groups = [[2 * chip + c for chip in range(8)] for c in range(2)]
    arrived = lax.all_to_all(placed, "seq", 0, 0, axis_index_groups=groups)
    weight_grad = jnp.sum(arrived.astype(jnp.float32), axis=0).astype(jnp.bfloat16)

    pair = lambda dtype: jax.ShapeDtypeStruct((2 * tok, HEAD_SIZE), dtype)
    sums = lambda width: [pltpu.VMEM((width, HEAD_SIZE), jnp.bfloat16)] * 2 + [pltpu.VMEM((HEAD_SIZE, width), jnp.float32)] * 2
    past_queries, far_sum, near_sum = pl.pallas_call(
        lambda *refs: backward_past_kernel(tok, heads, *refs),
        grid=(blocks,),
        in_specs=[row_block] * 4 + [pl.BlockSpec((heads, ROWS, 2 * tok), lambda b: (0, b, 0)), whole(), whole()],
        out_specs=[row_block, whole(), whole()],
        out_shape=[rows_of(jnp.float32), pair(jnp.bfloat16), pair(jnp.bfloat16)],
        scratch_shapes=sums(2 * tok),
        compiler_params=pltpu.CompilerParams(vmem_limit_bytes=VMEM_BYTES),
        cost_estimate=pl.CostEstimate(flops=1 << 20, bytes_accessed=1 << 20, transcendentals=0),
        name="backward_past",
    )(queries, attention_gradient, attn, inverse, expo, far, near)
    crossed = step_core(near_sum)
    (sent,) = on_core(send_kernel, "send", [pair(jnp.bfloat16)], core, far_sum, crossed)
    come = shifted(sent, "seq", -2)
    last_blocks = [pl.BlockSpec((heads, ROWS, ROWS), lambda b, i=i: (0, b, span // ROWS - blocks + i)) for i in range(blocks)]
    grad_queries, own_sum = pl.pallas_call(
        lambda *refs: backward_own_kernel(tok, heads, *refs),
        grid=(blocks,),
        in_specs=[row_block] * 4 + last_blocks + [whole(), row_block],
        out_specs=[row_block, whole()],
        out_shape=[rows_of(jnp.bfloat16), pair(jnp.float32)],
        scratch_shapes=sums(tok),
        compiler_params=pltpu.CompilerParams(vmem_limit_bytes=VMEM_BYTES),
        cost_estimate=pl.CostEstimate(flops=1 << 20, bytes_accessed=1 << 20, transcendentals=0),
        name="backward_own",
    )(queries, attention_gradient, attn, inverse, *([expo] * blocks), own, past_queries)
    own_sum, weight_grad = lax.optimization_barrier((own_sum, weight_grad))
    key_shape = jax.ShapeDtypeStruct((tok, HEAD_SIZE), jnp.bfloat16)
    grad_keys, grad_values = on_core(finish_kernel, "finish", [key_shape] * 2, core, own_sum, crossed, come)
    return (grad_queries, grad_keys, grad_values, weight_grad)


def solution(mesh):
    placed = (
        P("seq", "tensor"),
        P("seq", "tensor"),
        P("seq", "tensor"),
        P("tensor", None),
        P("seq", "tensor"),
        P("seq"),
    )
    return jax.shard_map(
        local,
        mesh=mesh,
        in_specs=placed,
        out_specs=(P("seq", "tensor"), P("seq", "tensor"), P("seq", "tensor"), P("tensor", "seq")),
        check_vma=False,
    )
```

```python
import math

import jax
import jax.numpy as jnp
from jax import lax
from jax.experimental import pallas as pl
from jax.experimental.pallas import tpu as pltpu
from jax.sharding import PartitionSpec as P

HEAD_SIZE = 128
NEG_BIG = -1e30
ROWS = 256
VMEM_BYTES = 20 << 20


def shifted(value, axis, steps):
    count = lax.axis_size(axis)
    initial, last = (max(0, -steps), min(count, count - steps))
    return lax.ppermute(value, axis, [(source, source + steps) for source in range(initial, last)])


def step_x(value, step):
    pairs = [(t, t // 4 * 4 + (t + step) % 4) for t in range(8)]
    return lax.ppermute(value, "tensor", pairs)


def step_y(value):
    return lax.ppermute(value, "tensor", [(t, t ^ 4) for t in range(8)])


def step_core(value):
    return lax.ppermute(value, "seq", [(s, s ^ 1) for s in range(16)])


def contract_rows(left, right):
    return lax.dot_general(
        left, right, (((0,), (0,)), ((), ())), preferred_element_type=jnp.float32
    )


def contract_last(left, right):
    return lax.dot_general(
        left, right, (((1,), (1,)), ((), ())), preferred_element_type=jnp.float32
    )


def gather_keys(parts, key_all, value_all, tok):
    for index, part in enumerate(parts):
        rows = pl.ds(index * tok, tok)
        key_all[rows, :] = part[pl.ds(0, tok), :]
        value_all[rows, :] = part[pl.ds(tok, tok), :]


def forward_kernel(
    tok, span, heads, low_ref, q_ref, far_ref, near_ref, own_ref,
    expo_ref, attn_ref, turned_ref, inverse_ref, key_all, value_all, bias,
):
    @pl.when(pl.program_id(0) == 0)
    def _():
        gather_keys((far_ref, near_ref, own_ref), key_all, value_all, tok)

    begin = pl.multiple_of(pl.program_id(0) * ROWS, ROWS)
    window = pl.ds(begin, span)
    key_at = lax.broadcasted_iota(jnp.int32, (ROWS, span), 1)
    row_at = lax.broadcasted_iota(jnp.int32, (ROWS, 1), 0)
    visible = (key_at >= low_ref[...] - begin) & (key_at <= row_at + 2 * tok)
    bias[...] = jnp.where(visible, 0.0, NEG_BIG)
    for head in range(heads):
        columns = slice(head * HEAD_SIZE, (head + 1) * HEAD_SIZE)
        raw = contract_last(q_ref[:, columns], key_all[window, :]) + bias[...]
        top = jnp.max(raw, axis=1, keepdims=True)
        expo = jnp.exp2((raw - top) * (math.log2(math.e) / math.sqrt(HEAD_SIZE)))
        inverse = 1.0 / jnp.sum(expo, axis=1, keepdims=True)
        expo_low = expo.astype(jnp.bfloat16)
        expo_ref[head] = expo_low
        inverse_ref[:, columns] = jnp.broadcast_to(inverse, (ROWS, HEAD_SIZE))
        attn = jnp.dot(expo_low, value_all[window, :], preferred_element_type=jnp.float32) * inverse
        attn = attn.astype(jnp.bfloat16)
        attn_ref[:, columns] = attn
        turned_ref[columns, :] = attn.T


def backward_rows(heads, width, first, q_ref, grad_ref, attn_ref, inverse_ref, probs_of, keys, values, gq_of, key_sum, value_sum):
    at = slice(first, first + width)
    for head in range(heads):
        columns = slice(head * HEAD_SIZE, (head + 1) * HEAD_SIZE)
        grad = (grad_ref[:, columns].astype(jnp.float32) * inverse_ref[:, columns]).astype(jnp.bfloat16)
        delta = jnp.sum(grad.astype(jnp.float32) * attn_ref[:, columns].astype(jnp.float32), axis=1, keepdims=True)
        d_prob = contract_last(grad, values[at, :])
        probs = probs_of(head)
        d_score = (probs.astype(jnp.float32) * (d_prob - delta)).astype(jnp.bfloat16)
        gq_of(columns, jnp.dot(d_score, keys[at, :], preferred_element_type=jnp.float32))
        key_sum[:, at] += jnp.dot(q_ref[:, columns].T, d_score, preferred_element_type=jnp.float32)
        value_sum[:, at] += jnp.dot(grad.T, probs, preferred_element_type=jnp.float32)


def backward_past_kernel(
    tok, heads, q_ref, grad_ref, attn_ref, inverse_ref, expo_ref, far_ref, near_ref,
    gq_ref, far_out, near_out, key_all, value_all, key_sum, value_sum,
):
    scale = 1.0 / math.sqrt(HEAD_SIZE)

    @pl.when(pl.program_id(0) == 0)
    def _():
        gather_keys((far_ref, near_ref), key_all, value_all, tok)
        key_sum[...] = jnp.zeros_like(key_sum)
        value_sum[...] = jnp.zeros_like(value_sum)

    def put(columns, value):
        gq_ref[:, columns] = value

    for block in range(tok // ROWS):
        @pl.when(pl.program_id(0) == block)
        def _(block=block):
            first = block * ROWS
            width = 2 * tok - first
            backward_rows(
                heads, width, first, q_ref, grad_ref, attn_ref, inverse_ref,
                lambda head: expo_ref[head, :, :width], key_all, value_all, put, key_sum, value_sum,
            )

    @pl.when(pl.program_id(0) == pl.num_programs(0) - 1)
    def _():
        for index, out in enumerate((far_out, near_out)):
            rows = pl.ds(index * tok, tok)
            out[pl.ds(0, tok), :] = (key_sum[:, rows].T * scale).astype(out.dtype)
            out[pl.ds(tok, tok), :] = value_sum[:, rows].T.astype(out.dtype)


def backward_own_kernel(
    tok, heads, q_ref, grad_ref, attn_ref, inverse_ref, expo_a, expo_b, expo_c, own_ref, past_ref,
    gq_ref, own_out, key_all, value_all, key_sum, value_sum,
):
    scale = 1.0 / math.sqrt(HEAD_SIZE)
    blocks = tok // ROWS
    expos = (expo_a, expo_b, expo_c)

    @pl.when(pl.program_id(0) == 0)
    def _():
        gather_keys((own_ref,), key_all, value_all, tok)
        key_sum[...] = jnp.zeros_like(key_sum)
        value_sum[...] = jnp.zeros_like(value_sum)

    def put(columns, value):
        gq_ref[:, columns] = ((past_ref[:, columns] + value) * scale).astype(gq_ref.dtype)

    for block in range(blocks):
        @pl.when(pl.program_id(0) == block)
        def _(block=block):
            width = (block + 1) * ROWS
            probs_of = lambda head: jnp.concatenate([expo[head] for expo in expos[blocks - 1 - block :]], axis=1)
            backward_rows(
                heads, width, 0, q_ref, grad_ref, attn_ref, inverse_ref,
                probs_of, key_all, value_all, put, key_sum, value_sum,
            )

    @pl.when(pl.program_id(0) == pl.num_programs(0) - 1)
    def _():
        own_out[pl.ds(0, tok), :] = key_sum[...].T * scale
        own_out[pl.ds(tok, tok), :] = value_sum[...].T


def project_kernel(sources, shapes, groups, where_ref, weight_ref, turned_ref, *refs):
    count = len(shapes)
    pieces, refs = refs[:count], refs[count:]
    earlier, refs = refs[: 2 * len(groups)], refs[2 * len(groups) :]
    if groups:
        come, placed, placed_sems = refs[-3:]
        refs = refs[:-3]
    sems, turned, weights, *buffers = refs[-3 - count :]
    refs = refs[: -3 - count]
    if groups:
        placed_ref, refs = refs[-1], refs[:-1]
    before, (total_ref, mine_ref, other_ref) = refs[:-3], refs[-3:]
    width = weights.shape[1]
    cut = width // 2
    copies = []

    def fetch(source, target):
        copies.append(pltpu.make_async_copy(source, target, sems.at[len(copies)]))
        copies[-1].start()
        return copies[-1]

    pending = {}
    turned_copy = None
    for index, blocks in enumerate(sources):
        columns = pl.ds(pl.multiple_of(where_ref[1 + index] * width, width), width)
        pending["weight", index] = fetch(weight_ref.at[:, columns], weights.at[index])
        for operand, _, _, _ in blocks:
            if ("piece", operand) not in pending:
                pending["piece", operand] = fetch(pieces[operand], buffers[operand])
        if turned_copy is None:
            turned_copy = fetch(turned_ref, turned)
    pending["turned"] = turned_copy
    at, loads = 0, []
    for i, size in enumerate(groups):
        for j, target in enumerate((placed, come)):
            loads.append(pltpu.make_async_copy(earlier[2 * i + j], target.at[pl.ds(at, size)], placed_sems.at[2 * i + j]))
            loads[-1].start()
        at += size
    done = set()

    def ready(key):
        if key not in done:
            done.add(key)
            pending[key].wait()

    mine = pl.multiple_of(where_ref[0] * cut, cut)
    other = pl.multiple_of((1 - where_ref[0]) * cut, cut)
    total = before[0] if before else total_ref
    for index, blocks in enumerate(sources):
        ready(("weight", index))
        for operand, _, _, _ in blocks:
            ready(("piece", operand))
        weight = weights[index]
        for operand, there, row, rows in blocks:
            term = contract_last(buffers[operand][pl.ds(there, rows), :], weight)
            at = pl.ds(row, rows)
            if before or index:
                term = total[at, :] + term
            total_ref[at, :] = term.astype(total_ref.dtype)
        total = total_ref
        ready("turned")
        for out, begin in ((mine_ref, mine), (other_ref, other)):
            part = None
            for operand, there, row, rows in blocks:
                term = jnp.dot(
                    turned[:, pl.ds(row, rows)],
                    buffers[operand][pl.ds(there, rows), pl.ds(begin, cut)],
                    preferred_element_type=jnp.float32,
                )
                part = term if part is None else part + term
            out[index] = part.astype(out.dtype)
    for load in loads:
        load.wait()
    stores = []
    for index in range(sum(groups)):
        both = placed[index].astype(jnp.float32) + come[index].astype(jnp.float32)
        placed[index] = both.astype(placed.dtype)
        place = where_ref[1 + len(sources) + index]
        stores.append(pltpu.make_async_copy(placed.at[index], placed_ref.at[place], placed_sems.at[2 * len(groups) + index]))
        stores[-1].start()
    for store in stores:
        store.wait()


def in_hbm(value):
    return pltpu.with_memory_space_constraint(value, pltpu.HBM)


def hbm():
    return pl.BlockSpec(memory_space=pltpu.HBM)


def project(sources, last, flops, where, weight, turned, pieces, before, earlier=()):
    width, tok = turned.shape
    count = len(sources)
    parts = jax.ShapeDtypeStruct((count, width, width // 2), jnp.bfloat16)
    pieces = [in_hbm(piece) for piece in pieces]
    earlier = [in_hbm(part) for part in earlier]
    shapes = [piece.shape for piece in pieces]
    groups = [part.shape[0] for part in earlier[::2]]
    slots = (sum(groups), width, width // 2)
    out_specs = [whole()] * 3
    out_shape = [jax.ShapeDtypeStruct((tok, width), jnp.bfloat16 if last else jnp.float32), parts, parts]
    scratch = [
        pltpu.SemaphoreType.DMA((count + len(pieces) + 1,)), pltpu.VMEM((width, tok), jnp.bfloat16),
        pltpu.VMEM((count, width, width), jnp.bfloat16),
    ] + [pltpu.VMEM(shape, jnp.bfloat16) for shape in shapes]
    if groups:
        out_specs.append(hbm())
        out_shape.append(pltpu.HBM((8,) + slots[1:], jnp.bfloat16))
        scratch += [pltpu.VMEM(slots, jnp.bfloat16)] * 2 + [pltpu.SemaphoreType.DMA((2 * len(groups) + slots[0],))]
    return pl.pallas_call(
        lambda *refs: project_kernel(sources, shapes, groups, *refs),
        in_specs=[pl.BlockSpec(memory_space=pltpu.SMEM)] + [hbm()] * (2 + len(pieces) + len(earlier)) + [whole()] * len(before),
        out_specs=out_specs,
        scratch_shapes=scratch,
        out_shape=out_shape,
        compiler_params=pltpu.CompilerParams(vmem_limit_bytes=VMEM_BYTES),
        cost_estimate=pl.CostEstimate(flops=flops, bytes_accessed=1 << 20, transcendentals=0),
        name="project",
    )(where, weight, turned, *pieces, *earlier, *before)


def place_kernel(where_ref, mine_ref, come_ref, last_mine_ref, last_come_ref, earlier_ref, out_ref, both, sems):
    copies, slot = [], 0
    for mine, come in ((last_mine_ref, last_come_ref), (mine_ref, come_ref)):
        for index in range(mine.shape[0]):
            both[slot] = (mine[index].astype(jnp.float32) + come[index].astype(jnp.float32)).astype(both.dtype)
            place = where_ref[index if mine is mine_ref else mine_ref.shape[0]]
            copies.append(pltpu.make_async_copy(both.at[slot], out_ref.at[place], sems.at[slot]))
            copies[-1].start()
            slot += 1
    for copy in copies:
        copy.wait()


def send_kernel(core_ref, far_ref, crossed_ref, out_ref):
    crossed = jnp.where(core_ref[0] == 1, crossed_ref[...].astype(jnp.float32), 0.0)
    out_ref[...] = (far_ref[...].astype(jnp.float32) + crossed).astype(out_ref.dtype)


def finish_kernel(core_ref, own_ref, crossed_ref, come_ref, key_ref, value_ref):
    tok = key_ref.shape[0]
    for index, out in enumerate((key_ref, value_ref)):
        rows = pl.ds(index * tok, tok)
        crossed = jnp.where(core_ref[0] == 0, crossed_ref[rows, :].astype(jnp.float32), 0.0)
        out[...] = (own_ref[rows, :] + crossed + come_ref[rows, :].astype(jnp.float32)).astype(out.dtype)


def on_core(kernel, name, out_shape, core, *operands):
    return pl.pallas_call(
        kernel,
        in_specs=[pl.BlockSpec(memory_space=pltpu.SMEM)] + [whole()] * len(operands),
        out_specs=[whole()] * len(out_shape),
        out_shape=out_shape,
        compiler_params=pltpu.CompilerParams(vmem_limit_bytes=VMEM_BYTES // 2),
        cost_estimate=pl.CostEstimate(flops=1 << 20, bytes_accessed=1 << 20, transcendentals=0),
        name=name,
    )(core[None].astype(jnp.int32), *operands)


def whole():
    return pl.BlockSpec(memory_space=pltpu.VMEM)


def local(queries, keys, values, out_weight, out_grad, doc_ids):
    tok = queries.shape[0]
    heads = queries.shape[1] // HEAD_SIZE
    blocks = tok // ROWS
    span = 2 * tok + ROWS
    shard = lax.axis_index("seq")
    docs = jnp.pad(doc_ids.astype(jnp.bfloat16).reshape(tok // HEAD_SIZE, HEAD_SIZE), ((0, 16 - tok // HEAD_SIZE), (0, 0)))
    own = jnp.concatenate([keys, values, docs], axis=0)
    far, near = shifted(own, "seq", 2), shifted(own, "seq", 1)
    doc_of = lambda part: part[2 * tok : 2 * tok + tok // HEAD_SIZE].reshape(tok).astype(jnp.int32)
    doc_keys = jnp.concatenate([
        jnp.where(shard >= 2, doc_of(far), -1), jnp.where(shard >= 1, doc_of(near), -1), doc_ids
    ])
    earlier = jnp.sum((doc_keys[None, :] < doc_ids[:, None]).astype(jnp.int32), axis=1)
    low = jnp.maximum(earlier, jnp.arange(tok, dtype=jnp.int32) + 1)[:, None]

    all_heads = heads * HEAD_SIZE
    row_block = pl.BlockSpec((ROWS, all_heads), lambda b: (b, 0))
    held = [pltpu.VMEM((3 * tok, HEAD_SIZE), jnp.bfloat16)] * 2
    work = heads * tok * span * HEAD_SIZE * 2
    rows_of = lambda dtype: jax.ShapeDtypeStruct((tok, all_heads), dtype)
    expo, attn, turned, inverse = pl.pallas_call(
        lambda *refs: forward_kernel(tok, span, heads, *refs),
        grid=(blocks,),
        in_specs=[pl.BlockSpec((ROWS, 1), lambda b: (b, 0)), row_block, whole(), whole(), whole()],
        out_specs=[
            pl.BlockSpec((heads, ROWS, span), lambda b: (0, b, 0)), row_block,
            pl.BlockSpec((all_heads, ROWS), lambda b: (0, b)), row_block,
        ],
        out_shape=[
            pltpu.HBM((heads, tok, span), jnp.bfloat16), pltpu.HBM((tok, all_heads), jnp.bfloat16),
            pltpu.HBM((all_heads, tok), jnp.bfloat16), pltpu.HBM((tok, all_heads), jnp.float32),
        ],
        scratch_shapes=held + [pltpu.VMEM((ROWS, span), jnp.float32)],
        compiler_params=pltpu.CompilerParams(vmem_limit_bytes=VMEM_BYTES),
        cost_estimate=pl.CostEstimate(flops=2 * work, bytes_accessed=14 << 20, transcendentals=heads * tok * span),
        name="forward",
    )(low, queries, far, near, own)
    expo, attn, inverse, queries = in_hbm(expo), in_hbm(attn), in_hbm(inverse), in_hbm(queries)

    tensor = lax.axis_index("tensor")
    row, column = tensor // 4, tensor % 4
    at = lambda flip, step: (row ^ flip) * 4 + (column + step) % 4
    core = shard % 2
    places = [at(0, 0), at(0, 2), at(1, 0), at(0, 3), at(0, 1), at(1, 3), at(1, 1), at(1, 2)]
    where = lambda some: jnp.stack([core, *some]).astype(jnp.int32)
    opposite = step_x(out_grad, 2)
    across = step_y(lax.optimization_barrier((out_grad, far, near))[0])
    later, low = lax.optimization_barrier((out_grad, low))
    near_up, near_down = step_x(later, 1), step_x(later, -1)
    across, opposite, turned = lax.optimization_barrier((across, opposite, turned))
    across_up, across_down = step_x(across, 1), step_x(across, -1)
    weight, turned = in_hbm(out_weight), in_hbm(turned)
    real = lambda count: 4 * count * tok * all_heads * all_heads
    last = step_y(opposite)
    total, mine_a, other_a = project(
        [((p, 0, 0, tok),) for p in range(3)], False, real(3),
        where(places[:3]), weight, turned, (out_grad, opposite, across), (),
    )
    come_a = step_core(other_a)
    total, mine_b, other_b = project(
        [((p, 0, 0, tok),) for p in range(2)], False, real(2),
        where(places[3:5]), weight, turned, (near_up, near_down), (total,),
    )
    come_b = step_core(other_b)
    total, mine_d, other_d = project(
        [((0, 0, 0, tok),)], False, real(1), where(places[7:]), weight, turned, (last,), (total,),
    )
    come_d = step_core(other_d)
    attention_gradient, mine_c, other_c, placed = project(
        [((p, 0, 0, tok),) for p in range(2)], True, 1 << 20, where(places[5:7] + places[:5]), weight, turned,
        (across_up, across_down), (total,), (mine_a, come_a, mine_b, come_b),
    )
    come_c = step_core(other_c)
    placed = pl.pallas_call(
        place_kernel,
        in_specs=[pl.BlockSpec(memory_space=pltpu.SMEM)] + [whole()] * 4 + [hbm()],
        out_specs=hbm(),
        out_shape=pltpu.HBM(placed.shape, placed.dtype),
        input_output_aliases={5: 0},
        scratch_shapes=[pltpu.VMEM((3,) + mine_c.shape[1:], mine_c.dtype), pltpu.SemaphoreType.DMA((3,))],
        compiler_params=pltpu.CompilerParams(vmem_limit_bytes=VMEM_BYTES),
        cost_estimate=pl.CostEstimate(flops=1 << 20, bytes_accessed=1 << 20, transcendentals=0),
        name="place",
    )(jnp.stack(places[5:]).astype(jnp.int32), mine_c, come_c, mine_d, come_d, placed)
    placed, attention_gradient = lax.optimization_barrier((placed, attention_gradient))
    groups = [[2 * chip + c for chip in range(8)] for c in range(2)]
    arrived = lax.all_to_all(placed, "seq", 0, 0, axis_index_groups=groups)
    weight_grad = jnp.sum(arrived.astype(jnp.float32), axis=0).astype(jnp.bfloat16)

    pair = lambda dtype: jax.ShapeDtypeStruct((2 * tok, HEAD_SIZE), dtype)
    sums = lambda width: [pltpu.VMEM((width, HEAD_SIZE), jnp.bfloat16)] * 2 + [pltpu.VMEM((HEAD_SIZE, width), jnp.float32)] * 2
    past_queries, far_sum, near_sum = pl.pallas_call(
        lambda *refs: backward_past_kernel(tok, heads, *refs),
        grid=(blocks,),
        in_specs=[row_block] * 4 + [pl.BlockSpec((heads, ROWS, 2 * tok), lambda b: (0, b, 0)), whole(), whole()],
        out_specs=[row_block, whole(), whole()],
        out_shape=[rows_of(jnp.float32), pair(jnp.bfloat16), pair(jnp.bfloat16)],
        scratch_shapes=sums(2 * tok),
        compiler_params=pltpu.CompilerParams(vmem_limit_bytes=VMEM_BYTES),
        cost_estimate=pl.CostEstimate(flops=1 << 20, bytes_accessed=1 << 20, transcendentals=0),
        name="backward_past",
    )(queries, attention_gradient, attn, inverse, expo, far, near)
    crossed = step_core(near_sum)
    (sent,) = on_core(send_kernel, "send", [pair(jnp.bfloat16)], core, far_sum, crossed)
    come = shifted(sent, "seq", -2)
    last_blocks = [pl.BlockSpec((heads, ROWS, ROWS), lambda b, i=i: (0, b, span // ROWS - blocks + i)) for i in range(blocks)]
    grad_queries, own_sum = pl.pallas_call(
        lambda *refs: backward_own_kernel(tok, heads, *refs),
        grid=(blocks,),
        in_specs=[row_block] * 4 + last_blocks + [whole(), row_block],
        out_specs=[row_block, whole()],
        out_shape=[rows_of(jnp.bfloat16), pair(jnp.float32)],
        scratch_shapes=sums(tok),
        compiler_params=pltpu.CompilerParams(vmem_limit_bytes=VMEM_BYTES),
        cost_estimate=pl.CostEstimate(flops=1 << 20, bytes_accessed=1 << 20, transcendentals=0),
        name="backward_own",
    )(queries, attention_gradient, attn, inverse, *([expo] * blocks), own, past_queries)
    own_sum, weight_grad = lax.optimization_barrier((own_sum, weight_grad))
    key_shape = jax.ShapeDtypeStruct((tok, HEAD_SIZE), jnp.bfloat16)
    grad_keys, grad_values = on_core(finish_kernel, "finish", [key_shape] * 2, core, own_sum, crossed, come)
    return (grad_queries, grad_keys, grad_values, weight_grad)


def solution(mesh):
    placed = (
        P("seq", "tensor"),
        P("seq", "tensor"),
        P("seq", "tensor"),
        P("tensor", None),
        P("seq", "tensor"),
        P("seq"),
    )
    return jax.shard_map(
        local,
        mesh=mesh,
        in_specs=placed,
        out_specs=(P("seq", "tensor"), P("seq", "tensor"), P("seq", "tensor"), P("tensor", "seq")),
        check_vma=False,
    )
```

```python
import math

import jax
import jax.numpy as jnp
from jax import lax
from jax.experimental import pallas as pl
from jax.experimental.pallas import tpu as pltpu
from jax.sharding import PartitionSpec as P

HEAD_SIZE = 128
NEG_BIG = -1e30
DOCS = 8
ROWS = 256
VMEM_BYTES = 20 << 20


def shifted(value, axis, steps):
    count = lax.axis_size(axis)
    initial, last = (max(0, -steps), min(count, count - steps))
    return lax.ppermute(value, axis, [(source, source + steps) for source in range(initial, last)])


def step_x(value, step):
    pairs = [(t, t // 4 * 4 + (t + step) % 4) for t in range(8)]
    return lax.ppermute(value, "tensor", pairs)


def step_y(value):
    return lax.ppermute(value, "tensor", [(t, t ^ 4) for t in range(8)])


def step_core(value):
    return lax.ppermute(value, "seq", [(s, s ^ 1) for s in range(16)])


def contract_rows(left, right):
    return lax.dot_general(
        left, right, (((0,), (0,)), ((), ())), preferred_element_type=jnp.float32
    )


def contract_last(left, right):
    return lax.dot_general(
        left, right, (((1,), (1,)), ((), ())), preferred_element_type=jnp.float32
    )


def gather_keys(parts, key_all, value_all, tok):
    for index, part in enumerate(parts):
        rows = pl.ds(index * tok, tok)
        key_all[rows, :] = part[pl.ds(0, tok), :]
        value_all[rows, :] = part[pl.ds(tok, tok), :]


def forward_kernel(
    tok, span, heads, shard_ref, doc_ref, q_ref, far_ref, near_ref, own_ref,
    expo_ref, attn_ref, turned_ref, inverse_ref, key_all, value_all, bias,
):
    @pl.when(pl.program_id(0) == 0)
    def _():
        gather_keys((far_ref, near_ref, own_ref), key_all, value_all, tok)

    begin = pl.multiple_of(pl.program_id(0) * ROWS, ROWS)
    window = pl.ds(begin, span)
    key_at = lax.broadcasted_iota(jnp.int32, (ROWS, span), 1)
    row_at = lax.broadcasted_iota(jnp.int32, (ROWS, 1), 0)
    doc_rows = pl.ds(2 * tok, 16)
    used = lax.broadcasted_iota(jnp.int32, (16, HEAD_SIZE), 0) < tok // HEAD_SIZE
    docs = [
        jnp.where(shard_ref[0] >= hop, part[doc_rows, :].astype(jnp.float32), -1.0)
        for part, hop in ((far_ref, 2), (near_ref, 1), (own_ref, 0))
    ]
    first = jnp.zeros((ROWS, 1), jnp.float32)
    for doc in range(1, DOCS):
        before = sum(jnp.where(used & (part < doc), 1.0, 0.0) for part in docs)
        before = jnp.sum(jnp.sum(before, axis=0, keepdims=True), axis=1, keepdims=True)
        first = jnp.where(doc_ref[...] == doc, before, first)
    none = sum(jnp.where(used & (part < 0), 1.0, 0.0) for part in docs)
    none = jnp.sum(jnp.sum(none, axis=0, keepdims=True), axis=1, keepdims=True)
    first = jnp.where(doc_ref[...] == 0, none, first).astype(jnp.int32)
    visible = (key_at >= jnp.maximum(first - begin, row_at + 1)) & (key_at <= row_at + 2 * tok)
    bias[...] = jnp.where(visible, 0.0, NEG_BIG)
    for head in range(heads):
        columns = slice(head * HEAD_SIZE, (head + 1) * HEAD_SIZE)
        raw = contract_last(q_ref[:, columns], key_all[window, :]) + bias[...]
        top = jnp.max(raw, axis=1, keepdims=True)
        expo = jnp.exp2((raw - top) * (math.log2(math.e) / math.sqrt(HEAD_SIZE)))
        inverse = 1.0 / jnp.sum(expo, axis=1, keepdims=True)
        expo_low = expo.astype(jnp.bfloat16)
        expo_ref[head] = expo_low
        inverse_ref[:, columns] = jnp.broadcast_to(inverse, (ROWS, HEAD_SIZE))
        attn = jnp.dot(expo_low, value_all[window, :], preferred_element_type=jnp.float32) * inverse
        attn = attn.astype(jnp.bfloat16)
        attn_ref[:, columns] = attn
        turned_ref[columns, :] = attn.T


def backward_rows(heads, width, first, q_ref, grad_ref, attn_ref, inverse_ref, probs_of, keys, values, gq_of, key_sum, value_sum):
    at = slice(first, first + width)
    for head in range(heads):
        columns = slice(head * HEAD_SIZE, (head + 1) * HEAD_SIZE)
        grad = (grad_ref[:, columns].astype(jnp.float32) * inverse_ref[:, columns]).astype(jnp.bfloat16)
        delta = jnp.sum(grad.astype(jnp.float32) * attn_ref[:, columns].astype(jnp.float32), axis=1, keepdims=True)
        d_prob = contract_last(grad, values[at, :])
        probs = probs_of(head)
        d_score = (probs.astype(jnp.float32) * (d_prob - delta)).astype(jnp.bfloat16)
        gq_of(columns, jnp.dot(d_score, keys[at, :], preferred_element_type=jnp.float32))
        key_sum[:, at] += jnp.dot(q_ref[:, columns].T, d_score, preferred_element_type=jnp.float32)
        value_sum[:, at] += jnp.dot(grad.T, probs, preferred_element_type=jnp.float32)


def backward_past_kernel(
    tok, heads, q_ref, grad_ref, attn_ref, inverse_ref, expo_ref, far_ref, near_ref,
    gq_ref, far_out, near_out, key_all, value_all, key_sum, value_sum,
):
    scale = 1.0 / math.sqrt(HEAD_SIZE)

    @pl.when(pl.program_id(0) == 0)
    def _():
        gather_keys((far_ref, near_ref), key_all, value_all, tok)
        key_sum[...] = jnp.zeros_like(key_sum)
        value_sum[...] = jnp.zeros_like(value_sum)

    def put(columns, value):
        gq_ref[:, columns] = value

    for block in range(tok // ROWS):
        @pl.when(pl.program_id(0) == block)
        def _(block=block):
            first = block * ROWS
            width = 2 * tok - first
            backward_rows(
                heads, width, first, q_ref, grad_ref, attn_ref, inverse_ref,
                lambda head: expo_ref[head, :, :width], key_all, value_all, put, key_sum, value_sum,
            )

    @pl.when(pl.program_id(0) == pl.num_programs(0) - 1)
    def _():
        for index, out in enumerate((far_out, near_out)):
            rows = pl.ds(index * tok, tok)
            out[pl.ds(0, tok), :] = (key_sum[:, rows].T * scale).astype(out.dtype)
            out[pl.ds(tok, tok), :] = value_sum[:, rows].T.astype(out.dtype)


def backward_own_kernel(
    tok, heads, q_ref, grad_ref, attn_ref, inverse_ref, expo_a, expo_b, expo_c, own_ref, past_ref,
    gq_ref, own_out, key_all, value_all, key_sum, value_sum,
):
    scale = 1.0 / math.sqrt(HEAD_SIZE)
    blocks = tok // ROWS
    expos = (expo_a, expo_b, expo_c)

    @pl.when(pl.program_id(0) == 0)
    def _():
        gather_keys((own_ref,), key_all, value_all, tok)
        key_sum[...] = jnp.zeros_like(key_sum)
        value_sum[...] = jnp.zeros_like(value_sum)

    def put(columns, value):
        gq_ref[:, columns] = ((past_ref[:, columns] + value) * scale).astype(gq_ref.dtype)

    for block in range(blocks):
        @pl.when(pl.program_id(0) == block)
        def _(block=block):
            width = (block + 1) * ROWS
            probs_of = lambda head: jnp.concatenate([expo[head] for expo in expos[blocks - 1 - block :]], axis=1)
            backward_rows(
                heads, width, 0, q_ref, grad_ref, attn_ref, inverse_ref,
                probs_of, key_all, value_all, put, key_sum, value_sum,
            )

    @pl.when(pl.program_id(0) == pl.num_programs(0) - 1)
    def _():
        own_out[pl.ds(0, tok), :] = key_sum[...].T * scale
        own_out[pl.ds(tok, tok), :] = value_sum[...].T


def project_kernel(sources, shapes, groups, where_ref, weight_ref, turned_ref, *refs):
    count = len(shapes)
    pieces, refs = refs[:count], refs[count:]
    earlier, refs = refs[: 2 * len(groups)], refs[2 * len(groups) :]
    if groups:
        come, placed, placed_sems = refs[-3:]
        refs = refs[:-3]
    sems, turned, weights, *buffers = refs[-3 - count :]
    refs = refs[: -3 - count]
    if groups:
        placed_ref, refs = refs[-1], refs[:-1]
    before, (total_ref, mine_ref, other_ref) = refs[:-3], refs[-3:]
    width = weights.shape[1]
    cut = width // 2
    copies = []

    def fetch(source, target):
        copies.append(pltpu.make_async_copy(source, target, sems.at[len(copies)]))
        copies[-1].start()
        return copies[-1]

    pending = {}
    turned_copy = None
    for index, blocks in enumerate(sources):
        columns = pl.ds(pl.multiple_of(where_ref[1 + index] * width, width), width)
        pending["weight", index] = fetch(weight_ref.at[:, columns], weights.at[index])
        for operand, _, _, _ in blocks:
            if ("piece", operand) not in pending:
                pending["piece", operand] = fetch(pieces[operand], buffers[operand])
        if turned_copy is None:
            turned_copy = fetch(turned_ref, turned)
    pending["turned"] = turned_copy
    at, loads = 0, []
    for i, size in enumerate(groups):
        for j, target in enumerate((placed, come)):
            loads.append(pltpu.make_async_copy(earlier[2 * i + j], target.at[pl.ds(at, size)], placed_sems.at[2 * i + j]))
            loads[-1].start()
        at += size
    done = set()

    def ready(key):
        if key not in done:
            done.add(key)
            pending[key].wait()

    mine = pl.multiple_of(where_ref[0] * cut, cut)
    other = pl.multiple_of((1 - where_ref[0]) * cut, cut)
    total = before[0] if before else total_ref
    for index, blocks in enumerate(sources):
        ready(("weight", index))
        for operand, _, _, _ in blocks:
            ready(("piece", operand))
        weight = weights[index]
        for operand, there, row, rows in blocks:
            term = contract_last(buffers[operand][pl.ds(there, rows), :], weight)
            at = pl.ds(row, rows)
            if before or index:
                term = total[at, :] + term
            total_ref[at, :] = term.astype(total_ref.dtype)
        total = total_ref
        ready("turned")
        for out, begin in ((mine_ref, mine), (other_ref, other)):
            part = None
            for operand, there, row, rows in blocks:
                term = jnp.dot(
                    turned[:, pl.ds(row, rows)],
                    buffers[operand][pl.ds(there, rows), pl.ds(begin, cut)],
                    preferred_element_type=jnp.float32,
                )
                part = term if part is None else part + term
            out[index] = part.astype(out.dtype)
    for load in loads:
        load.wait()
    stores = []
    for index in range(sum(groups)):
        both = placed[index].astype(jnp.float32) + come[index].astype(jnp.float32)
        placed[index] = both.astype(placed.dtype)
        place = where_ref[1 + len(sources) + index]
        stores.append(pltpu.make_async_copy(placed.at[index], placed_ref.at[place], placed_sems.at[2 * len(groups) + index]))
        stores[-1].start()
    for store in stores:
        store.wait()


def in_hbm(value):
    return pltpu.with_memory_space_constraint(value, pltpu.HBM)


def hbm():
    return pl.BlockSpec(memory_space=pltpu.HBM)


def project(sources, last, flops, where, weight, turned, pieces, before, earlier=()):
    width, tok = turned.shape
    count = len(sources)
    parts = jax.ShapeDtypeStruct((count, width, width // 2), jnp.bfloat16)
    pieces = [in_hbm(piece) for piece in pieces]
    earlier = [in_hbm(part) for part in earlier]
    shapes = [piece.shape for piece in pieces]
    groups = [part.shape[0] for part in earlier[::2]]
    slots = (sum(groups), width, width // 2)
    out_specs = [whole()] * 3
    out_shape = [jax.ShapeDtypeStruct((tok, width), jnp.bfloat16 if last else jnp.float32), parts, parts]
    scratch = [
        pltpu.SemaphoreType.DMA((count + len(pieces) + 1,)), pltpu.VMEM((width, tok), jnp.bfloat16),
        pltpu.VMEM((count, width, width), jnp.bfloat16),
    ] + [pltpu.VMEM(shape, jnp.bfloat16) for shape in shapes]
    if groups:
        out_specs.append(hbm())
        out_shape.append(pltpu.HBM((8,) + slots[1:], jnp.bfloat16))
        scratch += [pltpu.VMEM(slots, jnp.bfloat16)] * 2 + [pltpu.SemaphoreType.DMA((2 * len(groups) + slots[0],))]
    return pl.pallas_call(
        lambda *refs: project_kernel(sources, shapes, groups, *refs),
        in_specs=[pl.BlockSpec(memory_space=pltpu.SMEM)] + [hbm()] * (2 + len(pieces) + len(earlier)) + [whole()] * len(before),
        out_specs=out_specs,
        scratch_shapes=scratch,
        out_shape=out_shape,
        compiler_params=pltpu.CompilerParams(vmem_limit_bytes=VMEM_BYTES),
        cost_estimate=pl.CostEstimate(flops=flops, bytes_accessed=1 << 20, transcendentals=0),
        name="project",
    )(where, weight, turned, *pieces, *earlier, *before)


def place_kernel(where_ref, mine_ref, come_ref, last_mine_ref, last_come_ref, earlier_ref, out_ref, both, sems):
    copies, slot = [], 0
    for mine, come in ((last_mine_ref, last_come_ref), (mine_ref, come_ref)):
        for index in range(mine.shape[0]):
            both[slot] = (mine[index].astype(jnp.float32) + come[index].astype(jnp.float32)).astype(both.dtype)
            place = where_ref[index if mine is mine_ref else mine_ref.shape[0]]
            copies.append(pltpu.make_async_copy(both.at[slot], out_ref.at[place], sems.at[slot]))
            copies[-1].start()
            slot += 1
    for copy in copies:
        copy.wait()


def send_kernel(core_ref, far_ref, crossed_ref, out_ref):
    crossed = jnp.where(core_ref[0] == 1, crossed_ref[...].astype(jnp.float32), 0.0)
    out_ref[...] = (far_ref[...].astype(jnp.float32) + crossed).astype(out_ref.dtype)


def finish_kernel(core_ref, own_ref, crossed_ref, come_ref, key_ref, value_ref):
    tok = key_ref.shape[0]
    for index, out in enumerate((key_ref, value_ref)):
        rows = pl.ds(index * tok, tok)
        crossed = jnp.where(core_ref[0] == 0, crossed_ref[rows, :].astype(jnp.float32), 0.0)
        out[...] = (own_ref[rows, :] + crossed + come_ref[rows, :].astype(jnp.float32)).astype(out.dtype)


def on_core(kernel, name, out_shape, core, *operands):
    return pl.pallas_call(
        kernel,
        in_specs=[pl.BlockSpec(memory_space=pltpu.SMEM)] + [whole()] * len(operands),
        out_specs=[whole()] * len(out_shape),
        out_shape=out_shape,
        compiler_params=pltpu.CompilerParams(vmem_limit_bytes=VMEM_BYTES // 2),
        cost_estimate=pl.CostEstimate(flops=1 << 20, bytes_accessed=1 << 20, transcendentals=0),
        name=name,
    )(core[None].astype(jnp.int32), *operands)


def whole():
    return pl.BlockSpec(memory_space=pltpu.VMEM)


def local(queries, keys, values, out_weight, out_grad, doc_ids):
    tok = queries.shape[0]
    heads = queries.shape[1] // HEAD_SIZE
    blocks = tok // ROWS
    span = 2 * tok + ROWS
    shard = lax.axis_index("seq")
    docs = jnp.pad(doc_ids.astype(jnp.bfloat16).reshape(tok // HEAD_SIZE, HEAD_SIZE), ((0, 16 - tok // HEAD_SIZE), (0, 0)))
    own = jnp.concatenate([keys, values, docs], axis=0)
    far, near = shifted(own, "seq", 2), shifted(own, "seq", 1)
    all_heads = heads * HEAD_SIZE
    row_block = pl.BlockSpec((ROWS, all_heads), lambda b: (b, 0))
    held = [pltpu.VMEM((3 * tok, HEAD_SIZE), jnp.bfloat16)] * 2
    work = heads * tok * span * HEAD_SIZE * 2
    rows_of = lambda dtype: jax.ShapeDtypeStruct((tok, all_heads), dtype)
    expo, attn, turned, inverse = pl.pallas_call(
        lambda *refs: forward_kernel(tok, span, heads, *refs),
        grid=(blocks,),
        in_specs=[pl.BlockSpec(memory_space=pltpu.SMEM), pl.BlockSpec((ROWS, 1), lambda b: (b, 0)), row_block]
        + [whole()] * 3,
        out_specs=[
            pl.BlockSpec((heads, ROWS, span), lambda b: (0, b, 0)), row_block,
            pl.BlockSpec((all_heads, ROWS), lambda b: (0, b)), row_block,
        ],
        out_shape=[
            pltpu.HBM((heads, tok, span), jnp.bfloat16), pltpu.HBM((tok, all_heads), jnp.bfloat16),
            pltpu.HBM((all_heads, tok), jnp.bfloat16), pltpu.HBM((tok, all_heads), jnp.float32),
        ],
        scratch_shapes=held + [pltpu.VMEM((ROWS, span), jnp.float32)],
        compiler_params=pltpu.CompilerParams(vmem_limit_bytes=VMEM_BYTES),
        cost_estimate=pl.CostEstimate(flops=2 * work, bytes_accessed=14 << 20, transcendentals=heads * tok * span),
        name="forward",
    )(shard[None].astype(jnp.int32), doc_ids[:, None], queries, far, near, own)
    expo, attn, inverse, queries = in_hbm(expo), in_hbm(attn), in_hbm(inverse), in_hbm(queries)

    tensor = lax.axis_index("tensor")
    row, column = tensor // 4, tensor % 4
    at = lambda flip, step: (row ^ flip) * 4 + (column + step) % 4
    core = shard % 2
    places = [at(0, 0), at(0, 2), at(1, 0), at(0, 3), at(0, 1), at(1, 3), at(1, 1), at(1, 2)]
    where = lambda some: jnp.stack([core, *some]).astype(jnp.int32)
    opposite = step_x(out_grad, 2)
    across = step_y(lax.optimization_barrier((out_grad, far, near))[0])
    landed = far[:16] + near[:16]
    later = lax.optimization_barrier((out_grad, landed))[0]
    near_up, near_down = step_x(later, 1), step_x(later, -1)
    across, opposite, turned = lax.optimization_barrier((across, opposite, turned))
    across_up, across_down = step_x(across, 1), step_x(across, -1)
    weight, turned = in_hbm(out_weight), in_hbm(turned)
    real = lambda count: 4 * count * tok * all_heads * all_heads
    last = step_y(opposite)
    total, mine_a, other_a = project(
        [((p, 0, 0, tok),) for p in range(3)], False, real(3),
        where(places[:3]), weight, turned, (out_grad, opposite, across), (),
    )
    come_a = step_core(other_a)
    total, mine_b, other_b = project(
        [((p, 0, 0, tok),) for p in range(2)], False, real(2),
        where(places[3:5]), weight, turned, (near_up, near_down), (total,),
    )
    come_b = step_core(other_b)
    total, mine_d, other_d = project(
        [((0, 0, 0, tok),)], False, real(1), where(places[7:]), weight, turned, (last,), (total,),
    )
    come_d = step_core(other_d)
    attention_gradient, mine_c, other_c, placed = project(
        [((p, 0, 0, tok),) for p in range(2)], True, 1 << 20, where(places[5:7] + places[:5]), weight, turned,
        (across_up, across_down), (total,), (mine_a, come_a, mine_b, come_b),
    )
    come_c = step_core(other_c)
    placed = pl.pallas_call(
        place_kernel,
        in_specs=[pl.BlockSpec(memory_space=pltpu.SMEM)] + [whole()] * 4 + [hbm()],
        out_specs=hbm(),
        out_shape=pltpu.HBM(placed.shape, placed.dtype),
        input_output_aliases={5: 0},
        scratch_shapes=[pltpu.VMEM((3,) + mine_c.shape[1:], mine_c.dtype), pltpu.SemaphoreType.DMA((3,))],
        compiler_params=pltpu.CompilerParams(vmem_limit_bytes=VMEM_BYTES),
        cost_estimate=pl.CostEstimate(flops=1 << 20, bytes_accessed=1 << 20, transcendentals=0),
        name="place",
    )(jnp.stack(places[5:]).astype(jnp.int32), mine_c, come_c, mine_d, come_d, placed)
    placed, attention_gradient = lax.optimization_barrier((placed, attention_gradient))
    groups = [[2 * chip + c for chip in range(8)] for c in range(2)]
    arrived = lax.all_to_all(placed, "seq", 0, 0, axis_index_groups=groups)
    weight_grad = jnp.sum(arrived.astype(jnp.float32), axis=0).astype(jnp.bfloat16)

    pair = lambda dtype: jax.ShapeDtypeStruct((2 * tok, HEAD_SIZE), dtype)
    sums = lambda width: [pltpu.VMEM((width, HEAD_SIZE), jnp.bfloat16)] * 2 + [pltpu.VMEM((HEAD_SIZE, width), jnp.float32)] * 2
    past_queries, far_sum, near_sum = pl.pallas_call(
        lambda *refs: backward_past_kernel(tok, heads, *refs),
        grid=(blocks,),
        in_specs=[row_block] * 4 + [pl.BlockSpec((heads, ROWS, 2 * tok), lambda b: (0, b, 0)), whole(), whole()],
        out_specs=[row_block, whole(), whole()],
        out_shape=[rows_of(jnp.float32), pair(jnp.bfloat16), pair(jnp.bfloat16)],
        scratch_shapes=sums(2 * tok),
        compiler_params=pltpu.CompilerParams(vmem_limit_bytes=VMEM_BYTES),
        cost_estimate=pl.CostEstimate(flops=1 << 20, bytes_accessed=1 << 20, transcendentals=0),
        name="backward_past",
    )(queries, attention_gradient, attn, inverse, expo, far, near)
    crossed = step_core(near_sum)
    (sent,) = on_core(send_kernel, "send", [pair(jnp.bfloat16)], core, far_sum, crossed)
    come = shifted(sent, "seq", -2)
    last_blocks = [pl.BlockSpec((heads, ROWS, ROWS), lambda b, i=i: (0, b, span // ROWS - blocks + i)) for i in range(blocks)]
    grad_queries, own_sum = pl.pallas_call(
        lambda *refs: backward_own_kernel(tok, heads, *refs),
        grid=(blocks,),
        in_specs=[row_block] * 4 + last_blocks + [whole(), row_block],
        out_specs=[row_block, whole()],
        out_shape=[rows_of(jnp.bfloat16), pair(jnp.float32)],
        scratch_shapes=sums(tok),
        compiler_params=pltpu.CompilerParams(vmem_limit_bytes=VMEM_BYTES),
        cost_estimate=pl.CostEstimate(flops=1 << 20, bytes_accessed=1 << 20, transcendentals=0),
        name="backward_own",
    )(queries, attention_gradient, attn, inverse, *([expo] * blocks), own, past_queries)
    own_sum, weight_grad = lax.optimization_barrier((own_sum, weight_grad))
    key_shape = jax.ShapeDtypeStruct((tok, HEAD_SIZE), jnp.bfloat16)
    grad_keys, grad_values = on_core(finish_kernel, "finish", [key_shape] * 2, core, own_sum, crossed, come)
    return (grad_queries, grad_keys, grad_values, weight_grad)


def solution(mesh):
    placed = (
        P("seq", "tensor"),
        P("seq", "tensor"),
        P("seq", "tensor"),
        P("tensor", None),
        P("seq", "tensor"),
        P("seq"),
    )
    return jax.shard_map(
        local,
        mesh=mesh,
        in_specs=placed,
        out_specs=(P("seq", "tensor"), P("seq", "tensor"), P("seq", "tensor"), P("tensor", "seq")),
        check_vma=False,
    )
```

```python
import math

import jax
import jax.numpy as jnp
from jax import lax
from jax.experimental import pallas as pl
from jax.experimental.pallas import tpu as pltpu
from jax.sharding import PartitionSpec as P

HEAD_SIZE = 128
NEG_BIG = -1e30
DOCS = 8
ROWS = 256
VMEM_BYTES = 20 << 20


def shifted(value, axis, steps):
    count = lax.axis_size(axis)
    initial, last = (max(0, -steps), min(count, count - steps))
    return lax.ppermute(value, axis, [(source, source + steps) for source in range(initial, last)])


def step_x(value, step):
    pairs = [(t, t // 4 * 4 + (t + step) % 4) for t in range(8)]
    return lax.ppermute(value, "tensor", pairs)


def step_y(value):
    return lax.ppermute(value, "tensor", [(t, t ^ 4) for t in range(8)])


def step_core(value):
    return lax.ppermute(value, "seq", [(s, s ^ 1) for s in range(16)])


def contract_rows(left, right):
    return lax.dot_general(
        left, right, (((0,), (0,)), ((), ())), preferred_element_type=jnp.float32
    )


def contract_last(left, right):
    return lax.dot_general(
        left, right, (((1,), (1,)), ((), ())), preferred_element_type=jnp.float32
    )


def gather_keys(parts, key_all, value_all, tok):
    for index, part in enumerate(parts):
        rows = pl.ds(index * tok, tok)
        key_all[rows, :] = part[pl.ds(0, tok), :]
        value_all[rows, :] = part[pl.ds(tok, tok), :]


def forward_kernel(
    tok, span, heads, shard_ref, doc_ref, q_ref, far_ref, near_ref, own_ref,
    expo_ref, attn_ref, turned_ref, inverse_ref, key_all, value_all, bias,
):
    @pl.when(pl.program_id(0) == 0)
    def _():
        gather_keys((far_ref, near_ref, own_ref), key_all, value_all, tok)

    begin = pl.multiple_of(pl.program_id(0) * ROWS, ROWS)
    window = pl.ds(begin, span)
    key_at = lax.broadcasted_iota(jnp.int32, (ROWS, span), 1)
    row_at = lax.broadcasted_iota(jnp.int32, (ROWS, 1), 0)
    doc_rows = pl.ds(2 * tok, 16)
    used = lax.broadcasted_iota(jnp.int32, (16, HEAD_SIZE), 0) < tok // HEAD_SIZE
    docs = [
        jnp.where(shard_ref[0] >= hop, part[doc_rows, :].astype(jnp.float32), -1.0)
        for part, hop in ((far_ref, 2), (near_ref, 1), (own_ref, 0))
    ]
    first = jnp.zeros((ROWS, 1), jnp.float32)
    for doc in range(1, DOCS):
        before = sum(jnp.where(used & (part < doc), 1.0, 0.0) for part in docs)
        before = jnp.sum(jnp.sum(before, axis=0, keepdims=True), axis=1, keepdims=True)
        first = jnp.where(doc_ref[...] == doc, before, first)
    none = sum(jnp.where(used & (part < 0), 1.0, 0.0) for part in docs)
    none = jnp.sum(jnp.sum(none, axis=0, keepdims=True), axis=1, keepdims=True)
    first = jnp.where(doc_ref[...] == 0, none, first).astype(jnp.int32)
    visible = (key_at >= jnp.maximum(first - begin, row_at + 1)) & (key_at <= row_at + 2 * tok)
    bias[...] = jnp.where(visible, 0.0, NEG_BIG)
    for head in range(heads):
        columns = slice(head * HEAD_SIZE, (head + 1) * HEAD_SIZE)
        raw = contract_last(q_ref[:, columns], key_all[window, :]) + bias[...]
        top = jnp.max(raw, axis=1, keepdims=True)
        expo = jnp.exp2((raw - top) * (math.log2(math.e) / math.sqrt(HEAD_SIZE)))
        inverse = 1.0 / jnp.sum(expo, axis=1, keepdims=True)
        expo_low = expo.astype(jnp.bfloat16)
        expo_ref[head] = expo_low
        inverse_ref[:, columns] = jnp.broadcast_to(inverse, (ROWS, HEAD_SIZE))
        attn = jnp.dot(expo_low, value_all[window, :], preferred_element_type=jnp.float32) * inverse
        attn = attn.astype(jnp.bfloat16)
        attn_ref[:, columns] = attn
        turned_ref[columns, :] = attn.T


def backward_rows(heads, width, first, q_ref, grad_ref, attn_ref, inverse_ref, probs_of, keys, values, gq_of, key_sum, value_sum):
    at = slice(first, first + width)
    for head in range(heads):
        columns = slice(head * HEAD_SIZE, (head + 1) * HEAD_SIZE)
        grad = (grad_ref[:, columns].astype(jnp.float32) * inverse_ref[:, columns]).astype(jnp.bfloat16)
        delta = jnp.sum(grad.astype(jnp.float32) * attn_ref[:, columns].astype(jnp.float32), axis=1, keepdims=True)
        d_prob = contract_last(grad, values[at, :])
        probs = probs_of(head)
        d_score = (probs.astype(jnp.float32) * (d_prob - delta)).astype(jnp.bfloat16)
        gq_of(columns, jnp.dot(d_score, keys[at, :], preferred_element_type=jnp.float32))
        key_sum[:, at] += jnp.dot(q_ref[:, columns].T, d_score, preferred_element_type=jnp.float32)
        value_sum[:, at] += jnp.dot(grad.T, probs, preferred_element_type=jnp.float32)


def backward_past_kernel(
    tok, heads, q_ref, grad_ref, attn_ref, inverse_ref, expo_ref, far_ref, near_ref,
    gq_ref, far_out, near_out, key_all, value_all, key_sum, value_sum,
):
    scale = 1.0 / math.sqrt(HEAD_SIZE)

    @pl.when(pl.program_id(0) == 0)
    def _():
        gather_keys((far_ref, near_ref), key_all, value_all, tok)
        key_sum[...] = jnp.zeros_like(key_sum)
        value_sum[...] = jnp.zeros_like(value_sum)

    def put(columns, value):
        gq_ref[:, columns] = value

    for block in range(tok // ROWS):
        @pl.when(pl.program_id(0) == block)
        def _(block=block):
            first = block * ROWS
            width = 2 * tok - first
            backward_rows(
                heads, width, first, q_ref, grad_ref, attn_ref, inverse_ref,
                lambda head: expo_ref[head, :, :width], key_all, value_all, put, key_sum, value_sum,
            )

    @pl.when(pl.program_id(0) == pl.num_programs(0) - 1)
    def _():
        for index, out in enumerate((far_out, near_out)):
            rows = pl.ds(index * tok, tok)
            out[pl.ds(0, tok), :] = (key_sum[:, rows].T * scale).astype(out.dtype)
            out[pl.ds(tok, tok), :] = value_sum[:, rows].T.astype(out.dtype)


def backward_own_kernel(
    tok, heads, q_ref, grad_ref, attn_ref, inverse_ref, expo_a, expo_b, expo_c, own_ref, past_ref,
    gq_ref, own_out, key_all, value_all, key_sum, value_sum,
):
    scale = 1.0 / math.sqrt(HEAD_SIZE)
    blocks = tok // ROWS
    expos = (expo_a, expo_b, expo_c)

    @pl.when(pl.program_id(0) == 0)
    def _():
        gather_keys((own_ref,), key_all, value_all, tok)
        key_sum[...] = jnp.zeros_like(key_sum)
        value_sum[...] = jnp.zeros_like(value_sum)

    def put(columns, value):
        gq_ref[:, columns] = ((past_ref[:, columns] + value) * scale).astype(gq_ref.dtype)

    for block in range(blocks):
        @pl.when(pl.program_id(0) == block)
        def _(block=block):
            width = (block + 1) * ROWS
            probs_of = lambda head: jnp.concatenate([expo[head] for expo in expos[blocks - 1 - block :]], axis=1)
            backward_rows(
                heads, width, 0, q_ref, grad_ref, attn_ref, inverse_ref,
                probs_of, key_all, value_all, put, key_sum, value_sum,
            )

    @pl.when(pl.program_id(0) == pl.num_programs(0) - 1)
    def _():
        own_out[pl.ds(0, tok), :] = key_sum[...].T * scale
        own_out[pl.ds(tok, tok), :] = value_sum[...].T


def project_kernel(sources, shapes, groups, where_ref, weight_ref, turned_ref, *refs):
    count = len(shapes)
    pieces, refs = refs[:count], refs[count:]
    earlier, refs = refs[: 2 * len(groups)], refs[2 * len(groups) :]
    if groups:
        come, placed, placed_sems = refs[-3:]
        refs = refs[:-3]
    sems, turned, weights, *buffers = refs[-3 - count :]
    refs = refs[: -3 - count]
    if groups:
        placed_ref, refs = refs[-1], refs[:-1]
    before, (total_ref, mine_ref, other_ref) = refs[:-3], refs[-3:]
    width = weights.shape[1]
    cut = width // 2
    copies = []

    def fetch(source, target):
        copies.append(pltpu.make_async_copy(source, target, sems.at[len(copies)]))
        copies[-1].start()
        return copies[-1]

    pending = {}
    turned_copy = None
    for index, blocks in enumerate(sources):
        columns = pl.ds(pl.multiple_of(where_ref[1 + index] * width, width), width)
        pending["weight", index] = fetch(weight_ref.at[:, columns], weights.at[index])
        for operand, _, _, _ in blocks:
            if ("piece", operand) not in pending:
                pending["piece", operand] = fetch(pieces[operand], buffers[operand])
        if turned_copy is None:
            turned_copy = fetch(turned_ref, turned)
    pending["turned"] = turned_copy
    at, loads = 0, []
    for i, size in enumerate(groups):
        for j, target in enumerate((placed, come)):
            loads.append(pltpu.make_async_copy(earlier[2 * i + j], target.at[pl.ds(at, size)], placed_sems.at[2 * i + j]))
            loads[-1].start()
        at += size
    done = set()

    def ready(key):
        if key not in done:
            done.add(key)
            pending[key].wait()

    mine = pl.multiple_of(where_ref[0] * cut, cut)
    other = pl.multiple_of((1 - where_ref[0]) * cut, cut)
    total = before[0] if before else total_ref
    for index, blocks in enumerate(sources):
        ready(("weight", index))
        for operand, _, _, _ in blocks:
            ready(("piece", operand))
        weight = weights[index]
        for operand, there, row, rows in blocks:
            term = contract_last(buffers[operand][pl.ds(there, rows), :], weight)
            at = pl.ds(row, rows)
            if before or index:
                term = total[at, :] + term
            total_ref[at, :] = term.astype(total_ref.dtype)
        total = total_ref
        ready("turned")
        for out, begin in ((mine_ref, mine), (other_ref, other)):
            part = None
            for operand, there, row, rows in blocks:
                term = jnp.dot(
                    turned[:, pl.ds(row, rows)],
                    buffers[operand][pl.ds(there, rows), pl.ds(begin, cut)],
                    preferred_element_type=jnp.float32,
                )
                part = term if part is None else part + term
            out[index] = part.astype(out.dtype)
    for load in loads:
        load.wait()
    stores = []
    for index in range(sum(groups)):
        both = placed[index].astype(jnp.float32) + come[index].astype(jnp.float32)
        placed[index] = both.astype(placed.dtype)
        place = where_ref[1 + len(sources) + index]
        stores.append(pltpu.make_async_copy(placed.at[index], placed_ref.at[place], placed_sems.at[2 * len(groups) + index]))
        stores[-1].start()
    for store in stores:
        store.wait()


def in_hbm(value):
    return pltpu.with_memory_space_constraint(value, pltpu.HBM)


def hbm():
    return pl.BlockSpec(memory_space=pltpu.HBM)


def project(sources, last, flops, where, weight, turned, pieces, before, earlier=()):
    width, tok = turned.shape
    count = len(sources)
    parts = jax.ShapeDtypeStruct((count, width, width // 2), jnp.bfloat16)
    pieces = [in_hbm(piece) for piece in pieces]
    earlier = [in_hbm(part) for part in earlier]
    shapes = [piece.shape for piece in pieces]
    groups = [part.shape[0] for part in earlier[::2]]
    slots = (sum(groups), width, width // 2)
    out_specs = [whole()] * 3
    out_shape = [jax.ShapeDtypeStruct((tok, width), jnp.bfloat16 if last else jnp.float32), parts, parts]
    scratch = [
        pltpu.SemaphoreType.DMA((count + len(pieces) + 1,)), pltpu.VMEM((width, tok), jnp.bfloat16),
        pltpu.VMEM((count, width, width), jnp.bfloat16),
    ] + [pltpu.VMEM(shape, jnp.bfloat16) for shape in shapes]
    if groups:
        out_specs.append(hbm())
        out_shape.append(pltpu.HBM((8,) + slots[1:], jnp.bfloat16))
        scratch += [pltpu.VMEM(slots, jnp.bfloat16)] * 2 + [pltpu.SemaphoreType.DMA((2 * len(groups) + slots[0],))]
    return pl.pallas_call(
        lambda *refs: project_kernel(sources, shapes, groups, *refs),
        in_specs=[pl.BlockSpec(memory_space=pltpu.SMEM)] + [hbm()] * (2 + len(pieces) + len(earlier)) + [whole()] * len(before),
        out_specs=out_specs,
        scratch_shapes=scratch,
        out_shape=out_shape,
        compiler_params=pltpu.CompilerParams(vmem_limit_bytes=VMEM_BYTES),
        cost_estimate=pl.CostEstimate(flops=flops, bytes_accessed=1 << 20, transcendentals=0),
        name="project",
    )(where, weight, turned, *pieces, *earlier, *before)


def place_kernel(where_ref, mine_ref, come_ref, last_mine_ref, last_come_ref, earlier_ref, out_ref, both, sems):
    copies, slot = [], 0
    for mine, come in ((last_mine_ref, last_come_ref), (mine_ref, come_ref)):
        for index in range(mine.shape[0]):
            both[slot] = (mine[index].astype(jnp.float32) + come[index].astype(jnp.float32)).astype(both.dtype)
            place = where_ref[index if mine is mine_ref else mine_ref.shape[0]]
            copies.append(pltpu.make_async_copy(both.at[slot], out_ref.at[place], sems.at[slot]))
            copies[-1].start()
            slot += 1
    for copy in copies:
        copy.wait()


def send_kernel(core_ref, far_ref, crossed_ref, out_ref):
    crossed = jnp.where(core_ref[0] == 1, crossed_ref[...].astype(jnp.float32), 0.0)
    out_ref[...] = (far_ref[...].astype(jnp.float32) + crossed).astype(out_ref.dtype)


def finish_kernel(core_ref, own_ref, crossed_ref, come_ref, key_ref, value_ref):
    tok = key_ref.shape[0]
    for index, out in enumerate((key_ref, value_ref)):
        rows = pl.ds(index * tok, tok)
        crossed = jnp.where(core_ref[0] == 0, crossed_ref[rows, :].astype(jnp.float32), 0.0)
        out[...] = (own_ref[rows, :] + crossed + come_ref[rows, :].astype(jnp.float32)).astype(out.dtype)


def on_core(kernel, name, out_shape, core, *operands):
    return pl.pallas_call(
        kernel,
        in_specs=[pl.BlockSpec(memory_space=pltpu.SMEM)] + [whole()] * len(operands),
        out_specs=[whole()] * len(out_shape),
        out_shape=out_shape,
        compiler_params=pltpu.CompilerParams(vmem_limit_bytes=VMEM_BYTES // 2),
        cost_estimate=pl.CostEstimate(flops=1 << 20, bytes_accessed=1 << 20, transcendentals=0),
        name=name,
    )(core[None].astype(jnp.int32), *operands)


def whole():
    return pl.BlockSpec(memory_space=pltpu.VMEM)


def local(queries, keys, values, out_weight, out_grad, doc_ids):
    tok = queries.shape[0]
    heads = queries.shape[1] // HEAD_SIZE
    blocks = tok // ROWS
    span = 2 * tok + ROWS
    shard = lax.axis_index("seq")
    docs = jnp.pad(doc_ids.astype(jnp.bfloat16).reshape(tok // HEAD_SIZE, HEAD_SIZE), ((0, 16 - tok // HEAD_SIZE), (0, 0)))
    own = jnp.concatenate([keys, values, docs], axis=0)
    far, near = shifted(own, "seq", 2), shifted(own, "seq", 1)
    all_heads = heads * HEAD_SIZE
    row_block = pl.BlockSpec((ROWS, all_heads), lambda b: (b, 0))
    held = [pltpu.VMEM((3 * tok, HEAD_SIZE), jnp.bfloat16)] * 2
    work = heads * tok * span * HEAD_SIZE * 2
    rows_of = lambda dtype: jax.ShapeDtypeStruct((tok, all_heads), dtype)
    expo, attn, turned, inverse = pl.pallas_call(
        lambda *refs: forward_kernel(tok, span, heads, *refs),
        grid=(blocks,),
        in_specs=[pl.BlockSpec(memory_space=pltpu.SMEM), pl.BlockSpec((ROWS, 1), lambda b: (b, 0)), row_block]
        + [whole()] * 3,
        out_specs=[
            pl.BlockSpec((heads, ROWS, span), lambda b: (0, b, 0)), row_block,
            pl.BlockSpec((all_heads, ROWS), lambda b: (0, b)), row_block,
        ],
        out_shape=[
            pltpu.HBM((heads, tok, span), jnp.bfloat16), pltpu.HBM((tok, all_heads), jnp.bfloat16),
            pltpu.HBM((all_heads, tok), jnp.bfloat16), pltpu.HBM((tok, all_heads), jnp.float32),
        ],
        scratch_shapes=held + [pltpu.VMEM((ROWS, span), jnp.float32)],
        compiler_params=pltpu.CompilerParams(vmem_limit_bytes=VMEM_BYTES),
        cost_estimate=pl.CostEstimate(flops=2 * work, bytes_accessed=14 << 20, transcendentals=heads * tok * span),
        name="forward",
    )(shard[None].astype(jnp.int32), doc_ids[:, None], queries, far, near, own)
    expo, attn, inverse, queries = in_hbm(expo), in_hbm(attn), in_hbm(inverse), in_hbm(queries)

    tensor = lax.axis_index("tensor")
    row, column = tensor // 4, tensor % 4
    at = lambda flip, step: (row ^ flip) * 4 + (column + step) % 4
    core = shard % 2
    places = [at(0, 0), at(0, 2), at(1, 0), at(0, 3), at(0, 1), at(1, 3), at(1, 1), at(1, 2)]
    where = lambda some: jnp.stack([core, *some]).astype(jnp.int32)
    opposite = step_x(out_grad, 2)
    across = step_y(lax.optimization_barrier((out_grad, far, near))[0])
    landed = far[:16] + near[:16]
    later = lax.optimization_barrier((out_grad, landed))[0]
    near_up, near_down = step_x(later, 1), step_x(later, -1)
    across, opposite, turned = lax.optimization_barrier((across, opposite, turned))
    across_up, across_down = step_x(across, 1), step_x(across, -1)
    weight, turned = in_hbm(out_weight), in_hbm(turned)
    real = lambda count: 4 * count * tok * all_heads * all_heads
    last = step_y(opposite)
    total, mine_a, other_a = project(
        [((p, 0, 0, tok),) for p in range(3)], False, real(3),
        where(places[:3]), weight, turned, (out_grad, opposite, across), (),
    )
    come_a = step_core(other_a)
    total, mine_b, other_b = project(
        [((p, 0, 0, tok),) for p in range(2)], False, real(2),
        where(places[3:5]), weight, turned, (near_up, near_down), (total,),
    )
    come_b = step_core(other_b)
    total, mine_d, other_d = project(
        [((0, 0, 0, tok),)], False, 4 * real(1), where(places[7:]), weight, turned, (last,), (total,),
    )
    come_d = step_core(other_d)
    attention_gradient, mine_c, other_c, placed = project(
        [((p, 0, 0, tok),) for p in range(2)], True, 1 << 20, where(places[5:7] + places[:5]), weight, turned,
        (across_up, across_down), (total,), (mine_a, come_a, mine_b, come_b),
    )
    come_c = step_core(other_c)
    placed = pl.pallas_call(
        place_kernel,
        in_specs=[pl.BlockSpec(memory_space=pltpu.SMEM)] + [whole()] * 4 + [hbm()],
        out_specs=hbm(),
        out_shape=pltpu.HBM(placed.shape, placed.dtype),
        input_output_aliases={5: 0},
        scratch_shapes=[pltpu.VMEM((3,) + mine_c.shape[1:], mine_c.dtype), pltpu.SemaphoreType.DMA((3,))],
        compiler_params=pltpu.CompilerParams(vmem_limit_bytes=VMEM_BYTES),
        cost_estimate=pl.CostEstimate(flops=1 << 20, bytes_accessed=1 << 20, transcendentals=0),
        name="place",
    )(jnp.stack(places[5:]).astype(jnp.int32), mine_c, come_c, mine_d, come_d, placed)
    placed, attention_gradient = lax.optimization_barrier((placed, attention_gradient))
    groups = [[2 * chip + c for chip in range(8)] for c in range(2)]
    arrived = lax.all_to_all(placed, "seq", 0, 0, axis_index_groups=groups)
    weight_grad = jnp.sum(arrived.astype(jnp.float32), axis=0).astype(jnp.bfloat16)

    pair = lambda dtype: jax.ShapeDtypeStruct((2 * tok, HEAD_SIZE), dtype)
    sums = lambda width: [pltpu.VMEM((width, HEAD_SIZE), jnp.bfloat16)] * 2 + [pltpu.VMEM((HEAD_SIZE, width), jnp.float32)] * 2
    past_queries, far_sum, near_sum = pl.pallas_call(
        lambda *refs: backward_past_kernel(tok, heads, *refs),
        grid=(blocks,),
        in_specs=[row_block] * 4 + [pl.BlockSpec((heads, ROWS, 2 * tok), lambda b: (0, b, 0)), whole(), whole()],
        out_specs=[row_block, whole(), whole()],
        out_shape=[rows_of(jnp.float32), pair(jnp.bfloat16), pair(jnp.bfloat16)],
        scratch_shapes=sums(2 * tok),
        compiler_params=pltpu.CompilerParams(vmem_limit_bytes=VMEM_BYTES),
        cost_estimate=pl.CostEstimate(flops=1 << 20, bytes_accessed=1 << 20, transcendentals=0),
        name="backward_past",
    )(queries, attention_gradient, attn, inverse, expo, far, near)
    crossed = step_core(near_sum)
    (sent,) = on_core(send_kernel, "send", [pair(jnp.bfloat16)], core, far_sum, crossed)
    come = shifted(sent, "seq", -2)
    last_blocks = [pl.BlockSpec((heads, ROWS, ROWS), lambda b, i=i: (0, b, span // ROWS - blocks + i)) for i in range(blocks)]
    grad_queries, own_sum = pl.pallas_call(
        lambda *refs: backward_own_kernel(tok, heads, *refs),
        grid=(blocks,),
        in_specs=[row_block] * 4 + last_blocks + [whole(), row_block],
        out_specs=[row_block, whole()],
        out_shape=[rows_of(jnp.bfloat16), pair(jnp.float32)],
        scratch_shapes=sums(tok),
        compiler_params=pltpu.CompilerParams(vmem_limit_bytes=VMEM_BYTES),
        cost_estimate=pl.CostEstimate(flops=1 << 20, bytes_accessed=1 << 20, transcendentals=0),
        name="backward_own",
    )(queries, attention_gradient, attn, inverse, *([expo] * blocks), own, past_queries)
    own_sum, weight_grad = lax.optimization_barrier((own_sum, weight_grad))
    key_shape = jax.ShapeDtypeStruct((tok, HEAD_SIZE), jnp.bfloat16)
    grad_keys, grad_values = on_core(finish_kernel, "finish", [key_shape] * 2, core, own_sum, crossed, come)
    return (grad_queries, grad_keys, grad_values, weight_grad)


def solution(mesh):
    placed = (
        P("seq", "tensor"),
        P("seq", "tensor"),
        P("seq", "tensor"),
        P("tensor", None),
        P("seq", "tensor"),
        P("seq"),
    )
    return jax.shard_map(
        local,
        mesh=mesh,
        in_specs=placed,
        out_specs=(P("seq", "tensor"), P("seq", "tensor"), P("seq", "tensor"), P("tensor", "seq")),
        check_vma=False,
    )
```

```python
import math

import jax
import jax.numpy as jnp
from jax import lax
from jax.experimental import pallas as pl
from jax.experimental.pallas import tpu as pltpu
from jax.sharding import PartitionSpec as P

HEAD_SIZE = 128
NEG_BIG = -1e30
DOCS = 8
ROWS = 256
VMEM_BYTES = 20 << 20


def shifted(value, axis, steps):
    count = lax.axis_size(axis)
    initial, last = (max(0, -steps), min(count, count - steps))
    return lax.ppermute(value, axis, [(source, source + steps) for source in range(initial, last)])


def step_x(value, step):
    pairs = [(t, t // 4 * 4 + (t + step) % 4) for t in range(8)]
    return lax.ppermute(value, "tensor", pairs)


def step_y(value):
    return lax.ppermute(value, "tensor", [(t, t ^ 4) for t in range(8)])


def step_core(value):
    return lax.ppermute(value, "seq", [(s, s ^ 1) for s in range(16)])


def contract_rows(left, right):
    return lax.dot_general(
        left, right, (((0,), (0,)), ((), ())), preferred_element_type=jnp.float32
    )


def contract_last(left, right):
    return lax.dot_general(
        left, right, (((1,), (1,)), ((), ())), preferred_element_type=jnp.float32
    )


def gather_keys(parts, key_all, value_all, tok):
    for index, part in enumerate(parts):
        rows = pl.ds(index * tok, tok)
        key_all[rows, :] = part[pl.ds(0, tok), :]
        value_all[rows, :] = part[pl.ds(tok, tok), :]


def forward_kernel(
    tok, span, heads, shard_ref, doc_ref, q_ref, far_ref, near_ref, own_ref,
    expo_ref, attn_ref, turned_ref, inverse_ref, key_all, value_all, bias,
):
    @pl.when(pl.program_id(0) == 0)
    def _():
        gather_keys((far_ref, near_ref, own_ref), key_all, value_all, tok)

    begin = pl.multiple_of(pl.program_id(0) * ROWS, ROWS)
    window = pl.ds(begin, span)
    key_at = lax.broadcasted_iota(jnp.int32, (ROWS, span), 1)
    row_at = lax.broadcasted_iota(jnp.int32, (ROWS, 1), 0)
    doc_rows = pl.ds(2 * tok, 16)
    used = lax.broadcasted_iota(jnp.int32, (16, HEAD_SIZE), 0) < tok // HEAD_SIZE
    docs = [
        jnp.where(shard_ref[0] >= hop, part[doc_rows, :].astype(jnp.float32), -1.0)
        for part, hop in ((far_ref, 2), (near_ref, 1), (own_ref, 0))
    ]
    first = jnp.zeros((ROWS, 1), jnp.float32)
    for doc in range(1, DOCS):
        before = sum(jnp.where(used & (part < doc), 1.0, 0.0) for part in docs)
        before = jnp.sum(jnp.sum(before, axis=0, keepdims=True), axis=1, keepdims=True)
        first = jnp.where(doc_ref[...] == doc, before, first)
    none = sum(jnp.where(used & (part < 0), 1.0, 0.0) for part in docs)
    none = jnp.sum(jnp.sum(none, axis=0, keepdims=True), axis=1, keepdims=True)
    first = jnp.where(doc_ref[...] == 0, none, first).astype(jnp.int32)
    visible = (key_at >= jnp.maximum(first - begin, row_at + 1)) & (key_at <= row_at + 2 * tok)
    bias[...] = jnp.where(visible, 0.0, NEG_BIG)
    for head in range(heads):
        columns = slice(head * HEAD_SIZE, (head + 1) * HEAD_SIZE)
        raw = contract_last(q_ref[:, columns], key_all[window, :]) + bias[...]
        top = jnp.max(raw, axis=1, keepdims=True)
        expo = jnp.exp2((raw - top) * (math.log2(math.e) / math.sqrt(HEAD_SIZE)))
        inverse = 1.0 / jnp.sum(expo, axis=1, keepdims=True)
        expo_low = expo.astype(jnp.bfloat16)
        expo_ref[head] = expo_low
        inverse_ref[:, columns] = jnp.broadcast_to(inverse, (ROWS, HEAD_SIZE))
        attn = jnp.dot(expo_low, value_all[window, :], preferred_element_type=jnp.float32) * inverse
        attn = attn.astype(jnp.bfloat16)
        attn_ref[:, columns] = attn
        turned_ref[columns, :] = attn.T


def backward_rows(heads, width, first, q_ref, grad_ref, attn_ref, inverse_ref, probs_of, keys, values, gq_of, key_sum, value_sum):
    at = slice(first, first + width)
    for head in range(heads):
        columns = slice(head * HEAD_SIZE, (head + 1) * HEAD_SIZE)
        grad = (grad_ref[:, columns].astype(jnp.float32) * inverse_ref[:, columns]).astype(jnp.bfloat16)
        delta = jnp.sum(grad.astype(jnp.float32) * attn_ref[:, columns].astype(jnp.float32), axis=1, keepdims=True)
        d_prob = contract_last(grad, values[at, :])
        probs = probs_of(head)
        d_score = (probs.astype(jnp.float32) * (d_prob - delta)).astype(jnp.bfloat16)
        gq_of(columns, jnp.dot(d_score, keys[at, :], preferred_element_type=jnp.float32))
        key_sum[:, at] += jnp.dot(q_ref[:, columns].T, d_score, preferred_element_type=jnp.float32)
        value_sum[:, at] += jnp.dot(grad.T, probs, preferred_element_type=jnp.float32)


def backward_past_kernel(
    tok, heads, q_ref, grad_ref, attn_ref, inverse_ref, expo_ref, far_ref, near_ref,
    gq_ref, far_out, near_out, key_all, value_all, key_sum, value_sum,
):
    scale = 1.0 / math.sqrt(HEAD_SIZE)

    @pl.when(pl.program_id(0) == 0)
    def _():
        gather_keys((far_ref, near_ref), key_all, value_all, tok)
        key_sum[...] = jnp.zeros_like(key_sum)
        value_sum[...] = jnp.zeros_like(value_sum)

    def put(columns, value):
        gq_ref[:, columns] = value

    for block in range(tok // ROWS):
        @pl.when(pl.program_id(0) == block)
        def _(block=block):
            first = block * ROWS
            width = 2 * tok - first
            backward_rows(
                heads, width, first, q_ref, grad_ref, attn_ref, inverse_ref,
                lambda head: expo_ref[head, :, :width], key_all, value_all, put, key_sum, value_sum,
            )

    @pl.when(pl.program_id(0) == pl.num_programs(0) - 1)
    def _():
        for index, out in enumerate((far_out, near_out)):
            rows = pl.ds(index * tok, tok)
            out[pl.ds(0, tok), :] = (key_sum[:, rows].T * scale).astype(out.dtype)
            out[pl.ds(tok, tok), :] = value_sum[:, rows].T.astype(out.dtype)


def backward_own_kernel(
    tok, heads, q_ref, grad_ref, attn_ref, inverse_ref, expo_a, expo_b, expo_c, own_ref, past_ref,
    gq_ref, own_out, key_all, value_all, key_sum, value_sum,
):
    scale = 1.0 / math.sqrt(HEAD_SIZE)
    blocks = tok // ROWS
    expos = (expo_a, expo_b, expo_c)

    @pl.when(pl.program_id(0) == 0)
    def _():
        gather_keys((own_ref,), key_all, value_all, tok)
        key_sum[...] = jnp.zeros_like(key_sum)
        value_sum[...] = jnp.zeros_like(value_sum)

    def put(columns, value):
        gq_ref[:, columns] = ((past_ref[:, columns] + value) * scale).astype(gq_ref.dtype)

    for block in range(blocks):
        @pl.when(pl.program_id(0) == block)
        def _(block=block):
            width = (block + 1) * ROWS
            probs_of = lambda head: jnp.concatenate([expo[head] for expo in expos[blocks - 1 - block :]], axis=1)
            backward_rows(
                heads, width, 0, q_ref, grad_ref, attn_ref, inverse_ref,
                probs_of, key_all, value_all, put, key_sum, value_sum,
            )

    @pl.when(pl.program_id(0) == pl.num_programs(0) - 1)
    def _():
        own_out[pl.ds(0, tok), :] = key_sum[...].T * scale
        own_out[pl.ds(tok, tok), :] = value_sum[...].T


def project_kernel(sources, shapes, groups, with_total, with_parts, where_ref, weight_ref, turned_ref, *refs):
    count = len(shapes)
    pieces, refs = refs[:count], refs[count:]
    earlier, refs = refs[: 2 * len(groups)], refs[2 * len(groups) :]
    if groups:
        come, placed, placed_sems = refs[-3:]
        refs = refs[:-3]
    sems, turned, weights, total_sum, *buffers = refs[-4 - count :]
    refs = refs[: -4 - count]
    if groups:
        placed_ref, refs = refs[-1], refs[:-1]
    if with_parts:
        refs, (mine_ref, other_ref) = refs[:-2], refs[-2:]
    if with_total:
        before, total_ref = refs[:-1], refs[-1]
    width = weights.shape[1]
    cut = width // 2
    copies = []

    def fetch(source, target):
        copies.append(pltpu.make_async_copy(source, target, sems.at[len(copies)]))
        copies[-1].start()
        return copies[-1]

    pending = {}
    turned_copy = None
    for index, blocks in enumerate(sources):
        columns = pl.ds(pl.multiple_of(where_ref[1 + index] * width, width), width)
        if with_total:
            pending["weight", index] = fetch(weight_ref.at[:, columns], weights.at[index])
        for operand, _, _, _ in blocks:
            if ("piece", operand) not in pending:
                pending["piece", operand] = fetch(pieces[operand], buffers[operand])
        if with_parts and turned_copy is None:
            turned_copy = fetch(turned_ref, turned)
    pending["turned"] = turned_copy
    at, loads = 0, []
    for i, size in enumerate(groups):
        for j, target in enumerate((placed, come)):
            loads.append(pltpu.make_async_copy(earlier[2 * i + j], target.at[pl.ds(at, size)], placed_sems.at[2 * i + j]))
            loads[-1].start()
        at += size
    done = set()

    def ready(key):
        if key not in done:
            done.add(key)
            pending[key].wait()

    mine = pl.multiple_of(where_ref[0] * cut, cut)
    other = pl.multiple_of((1 - where_ref[0]) * cut, cut)
    for index, blocks in enumerate(sources):
        for operand, _, _, _ in blocks:
            ready(("piece", operand))
        if with_total:
            ready(("weight", index))
            for operand, there, row, rows in blocks:
                term = contract_last(buffers[operand][pl.ds(there, rows), :], weights[index])
                at = pl.ds(row, rows)
                if index:
                    term = total_sum[at, :] + term
                elif before:
                    term = before[0][at, :] + term
                if index == len(sources) - 1:
                    total_ref[at, :] = term.astype(total_ref.dtype)
                else:
                    total_sum[at, :] = term
        if not with_parts:
            continue
        ready("turned")
        for out, begin in ((mine_ref, mine), (other_ref, other)):
            part = None
            for operand, there, row, rows in blocks:
                term = jnp.dot(
                    turned[:, pl.ds(row, rows)],
                    buffers[operand][pl.ds(there, rows), pl.ds(begin, cut)],
                    preferred_element_type=jnp.float32,
                )
                part = term if part is None else part + term
            out[index] = part.astype(out.dtype)
    for load in loads:
        load.wait()
    stores = []
    for index in range(sum(groups)):
        both = placed[index].astype(jnp.float32) + come[index].astype(jnp.float32)
        placed[index] = both.astype(placed.dtype)
        place = where_ref[1 + len(sources) + index]
        stores.append(pltpu.make_async_copy(placed.at[index], placed_ref.at[place], placed_sems.at[2 * len(groups) + index]))
        stores[-1].start()
    for store in stores:
        store.wait()


def in_hbm(value):
    return pltpu.with_memory_space_constraint(value, pltpu.HBM)


def hbm():
    return pl.BlockSpec(memory_space=pltpu.HBM)


def project(sources, last, flops, where, weight, turned, pieces, before, earlier=(), with_total=True, with_parts=True):
    width, tok = turned.shape
    count = len(sources)
    parts = jax.ShapeDtypeStruct((count, width, width // 2), jnp.bfloat16)
    pieces = [in_hbm(piece) for piece in pieces]
    earlier = [in_hbm(part) for part in earlier]
    shapes = [piece.shape for piece in pieces]
    groups = [part.shape[0] for part in earlier[::2]]
    slots = (sum(groups), width, width // 2)
    out_shape = [jax.ShapeDtypeStruct((tok, width), jnp.bfloat16 if last else jnp.float32)] * with_total
    out_shape += [parts, parts] * with_parts
    out_specs = [whole()] * len(out_shape)
    scratch = [
        pltpu.SemaphoreType.DMA((count + len(pieces) + 1,)), pltpu.VMEM((width, tok), jnp.bfloat16),
        pltpu.VMEM((count, width, width), jnp.bfloat16), pltpu.VMEM((tok, width), jnp.float32),
    ] + [pltpu.VMEM(shape, jnp.bfloat16) for shape in shapes]
    if groups:
        out_specs.append(hbm())
        out_shape.append(pltpu.HBM((8,) + slots[1:], jnp.bfloat16))
        scratch += [pltpu.VMEM(slots, jnp.bfloat16)] * 2 + [pltpu.SemaphoreType.DMA((2 * len(groups) + slots[0],))]
    return pl.pallas_call(
        lambda *refs: project_kernel(sources, shapes, groups, with_total, with_parts, *refs),
        in_specs=[pl.BlockSpec(memory_space=pltpu.SMEM)] + [hbm()] * (2 + len(pieces) + len(earlier)) + [whole()] * len(before),
        out_specs=out_specs,
        scratch_shapes=scratch,
        out_shape=out_shape,
        compiler_params=pltpu.CompilerParams(vmem_limit_bytes=VMEM_BYTES),
        cost_estimate=pl.CostEstimate(flops=flops, bytes_accessed=1 << 20, transcendentals=0),
        name="project",
    )(where, weight, turned, *pieces, *earlier, *before)


def place_kernel(where_ref, mine_ref, come_ref, last_mine_ref, last_come_ref, earlier_ref, out_ref, both, sems):
    copies, slot = [], 0
    for mine, come in ((last_mine_ref, last_come_ref), (mine_ref, come_ref)):
        for index in range(mine.shape[0]):
            both[slot] = (mine[index].astype(jnp.float32) + come[index].astype(jnp.float32)).astype(both.dtype)
            place = where_ref[index if mine is mine_ref else mine_ref.shape[0]]
            copies.append(pltpu.make_async_copy(both.at[slot], out_ref.at[place], sems.at[slot]))
            copies[-1].start()
            slot += 1
    for copy in copies:
        copy.wait()


def send_kernel(core_ref, far_ref, crossed_ref, out_ref):
    crossed = jnp.where(core_ref[0] == 1, crossed_ref[...].astype(jnp.float32), 0.0)
    out_ref[...] = (far_ref[...].astype(jnp.float32) + crossed).astype(out_ref.dtype)


def finish_kernel(core_ref, own_ref, crossed_ref, come_ref, key_ref, value_ref):
    tok = key_ref.shape[0]
    for index, out in enumerate((key_ref, value_ref)):
        rows = pl.ds(index * tok, tok)
        crossed = jnp.where(core_ref[0] == 0, crossed_ref[rows, :].astype(jnp.float32), 0.0)
        out[...] = (own_ref[rows, :] + crossed + come_ref[rows, :].astype(jnp.float32)).astype(out.dtype)


def on_core(kernel, name, out_shape, core, *operands):
    return pl.pallas_call(
        kernel,
        in_specs=[pl.BlockSpec(memory_space=pltpu.SMEM)] + [whole()] * len(operands),
        out_specs=[whole()] * len(out_shape),
        out_shape=out_shape,
        compiler_params=pltpu.CompilerParams(vmem_limit_bytes=VMEM_BYTES // 2),
        cost_estimate=pl.CostEstimate(flops=1 << 20, bytes_accessed=1 << 20, transcendentals=0),
        name=name,
    )(core[None].astype(jnp.int32), *operands)


def whole():
    return pl.BlockSpec(memory_space=pltpu.VMEM)


def local(queries, keys, values, out_weight, out_grad, doc_ids):
    tok = queries.shape[0]
    heads = queries.shape[1] // HEAD_SIZE
    blocks = tok // ROWS
    span = 2 * tok + ROWS
    shard = lax.axis_index("seq")
    docs = jnp.pad(doc_ids.astype(jnp.bfloat16).reshape(tok // HEAD_SIZE, HEAD_SIZE), ((0, 16 - tok // HEAD_SIZE), (0, 0)))
    own = jnp.concatenate([keys, values, docs], axis=0)
    far, near = shifted(own, "seq", 2), shifted(own, "seq", 1)
    all_heads = heads * HEAD_SIZE
    row_block = pl.BlockSpec((ROWS, all_heads), lambda b: (b, 0))
    held = [pltpu.VMEM((3 * tok, HEAD_SIZE), jnp.bfloat16)] * 2
    work = heads * tok * span * HEAD_SIZE * 2
    rows_of = lambda dtype: jax.ShapeDtypeStruct((tok, all_heads), dtype)
    expo, attn, turned, inverse = pl.pallas_call(
        lambda *refs: forward_kernel(tok, span, heads, *refs),
        grid=(blocks,),
        in_specs=[pl.BlockSpec(memory_space=pltpu.SMEM), pl.BlockSpec((ROWS, 1), lambda b: (b, 0)), row_block]
        + [whole()] * 3,
        out_specs=[
            pl.BlockSpec((heads, ROWS, span), lambda b: (0, b, 0)), row_block,
            pl.BlockSpec((all_heads, ROWS), lambda b: (0, b)), row_block,
        ],
        out_shape=[
            pltpu.HBM((heads, tok, span), jnp.bfloat16), pltpu.HBM((tok, all_heads), jnp.bfloat16),
            pltpu.HBM((all_heads, tok), jnp.bfloat16), pltpu.HBM((tok, all_heads), jnp.float32),
        ],
        scratch_shapes=held + [pltpu.VMEM((ROWS, span), jnp.float32)],
        compiler_params=pltpu.CompilerParams(vmem_limit_bytes=VMEM_BYTES),
        cost_estimate=pl.CostEstimate(flops=2 * work, bytes_accessed=14 << 20, transcendentals=heads * tok * span),
        name="forward",
    )(shard[None].astype(jnp.int32), doc_ids[:, None], queries, far, near, own)
    expo, attn, inverse, queries = in_hbm(expo), in_hbm(attn), in_hbm(inverse), in_hbm(queries)

    tensor = lax.axis_index("tensor")
    row, column = tensor // 4, tensor % 4
    at = lambda flip, step: (row ^ flip) * 4 + (column + step) % 4
    core = shard % 2
    places = [at(0, 0), at(0, 2), at(1, 0), at(0, 3), at(0, 1), at(1, 3), at(1, 1), at(1, 2)]
    where = lambda some: jnp.stack([core, *some]).astype(jnp.int32)
    opposite = step_x(out_grad, 2)
    across = step_y(lax.optimization_barrier((out_grad, far, near))[0])
    landed = far[:16] + near[:16]
    later = lax.optimization_barrier((out_grad, landed))[0]
    near_up, near_down = step_x(later, 1), step_x(later, -1)
    across, opposite, turned = lax.optimization_barrier((across, opposite, turned))
    across_up, across_down = step_x(across, 1), step_x(across, -1)
    weight, turned = in_hbm(out_weight), in_hbm(turned)
    real = lambda count: 4 * count * tok * all_heads * all_heads
    last = step_y(opposite)
    total, mine_a, other_a = project(
        [((p, 0, 0, tok),) for p in range(3)], False, real(3),
        where(places[:3]), weight, turned, (out_grad, opposite, across), (),
    )
    come_a = step_core(other_a)
    total, mine_b, other_b = project(
        [((p, 0, 0, tok),) for p in range(2)], False, real(2),
        where(places[3:5]), weight, turned, (near_up, near_down), (total,),
    )
    come_b = step_core(other_b)
    mine_d, other_d = project(
        [((0, 0, 0, tok),)], False, 4 * real(1), where(places[7:]), weight, turned, (last,), (), with_total=False,
    )
    come_d = step_core(other_d)
    across_up, across_down, mine_d = lax.optimization_barrier((across_up, across_down, mine_d))
    mine_c, other_c, placed = project(
        [((p, 0, 0, tok),) for p in range(2)], False, 1 << 20, where(places[5:7] + places[:5]), weight, turned,
        (across_up, across_down), (), (mine_a, come_a, mine_b, come_b), with_total=False,
    )
    (attention_gradient,) = project(
        [((p, 0, 0, tok),) for p in range(3)], True, 1 << 20, where([places[7], *places[5:7]]), weight, turned,
        (last, across_up, across_down), (total,), with_parts=False,
    )
    come_c = step_core(other_c)
    placed = pl.pallas_call(
        place_kernel,
        in_specs=[pl.BlockSpec(memory_space=pltpu.SMEM)] + [whole()] * 4 + [hbm()],
        out_specs=hbm(),
        out_shape=pltpu.HBM(placed.shape, placed.dtype),
        input_output_aliases={5: 0},
        scratch_shapes=[pltpu.VMEM((3,) + mine_c.shape[1:], mine_c.dtype), pltpu.SemaphoreType.DMA((3,))],
        compiler_params=pltpu.CompilerParams(vmem_limit_bytes=VMEM_BYTES),
        cost_estimate=pl.CostEstimate(flops=1 << 20, bytes_accessed=1 << 20, transcendentals=0),
        name="place",
    )(jnp.stack(places[5:]).astype(jnp.int32), mine_c, come_c, mine_d, come_d, placed)
    placed, queries = lax.optimization_barrier((placed, queries))
    groups = [[2 * chip + c for chip in range(8)] for c in range(2)]
    arrived = lax.all_to_all(placed, "seq", 0, 0, axis_index_groups=groups)
    weight_grad = jnp.sum(arrived.astype(jnp.float32), axis=0).astype(jnp.bfloat16)

    pair = lambda dtype: jax.ShapeDtypeStruct((2 * tok, HEAD_SIZE), dtype)
    sums = lambda width: [pltpu.VMEM((width, HEAD_SIZE), jnp.bfloat16)] * 2 + [pltpu.VMEM((HEAD_SIZE, width), jnp.float32)] * 2
    past_queries, far_sum, near_sum = pl.pallas_call(
        lambda *refs: backward_past_kernel(tok, heads, *refs),
        grid=(blocks,),
        in_specs=[row_block] * 4 + [pl.BlockSpec((heads, ROWS, 2 * tok), lambda b: (0, b, 0)), whole(), whole()],
        out_specs=[row_block, whole(), whole()],
        out_shape=[rows_of(jnp.float32), pair(jnp.bfloat16), pair(jnp.bfloat16)],
        scratch_shapes=sums(2 * tok),
        compiler_params=pltpu.CompilerParams(vmem_limit_bytes=VMEM_BYTES),
        cost_estimate=pl.CostEstimate(flops=1 << 20, bytes_accessed=1 << 20, transcendentals=0),
        name="backward_past",
    )(queries, attention_gradient, attn, inverse, expo, far, near)
    crossed = step_core(near_sum)
    (sent,) = on_core(send_kernel, "send", [pair(jnp.bfloat16)], core, far_sum, crossed)
    come = shifted(sent, "seq", -2)
    last_blocks = [pl.BlockSpec((heads, ROWS, ROWS), lambda b, i=i: (0, b, span // ROWS - blocks + i)) for i in range(blocks)]
    grad_queries, own_sum = pl.pallas_call(
        lambda *refs: backward_own_kernel(tok, heads, *refs),
        grid=(blocks,),
        in_specs=[row_block] * 4 + last_blocks + [whole(), row_block],
        out_specs=[row_block, whole()],
        out_shape=[rows_of(jnp.bfloat16), pair(jnp.float32)],
        scratch_shapes=sums(tok),
        compiler_params=pltpu.CompilerParams(vmem_limit_bytes=VMEM_BYTES),
        cost_estimate=pl.CostEstimate(flops=1 << 20, bytes_accessed=1 << 20, transcendentals=0),
        name="backward_own",
    )(queries, attention_gradient, attn, inverse, *([expo] * blocks), own, past_queries)
    own_sum, weight_grad = lax.optimization_barrier((own_sum, weight_grad))
    key_shape = jax.ShapeDtypeStruct((tok, HEAD_SIZE), jnp.bfloat16)
    grad_keys, grad_values = on_core(finish_kernel, "finish", [key_shape] * 2, core, own_sum, crossed, come)
    return (grad_queries, grad_keys, grad_values, weight_grad)


def solution(mesh):
    placed = (
        P("seq", "tensor"),
        P("seq", "tensor"),
        P("seq", "tensor"),
        P("tensor", None),
        P("seq", "tensor"),
        P("seq"),
    )
    return jax.shard_map(
        local,
        mesh=mesh,
        in_specs=placed,
        out_specs=(P("seq", "tensor"), P("seq", "tensor"), P("seq", "tensor"), P("tensor", "seq")),
        check_vma=False,
    )
```
